32 devices in a mesh: dir: 2 (over x), pos: 16 (over z, y, core).
Axes of the slice: x: 2, y: 2, z: 4, core: 2. Of those that a mesh axis runs over, the one named last changes fastest.
Arguments:
- coherence: bfloat16 [2, 64, 64, 64, 128], P(None, 'dir', 'pos'), may hold values from -6 to 6
- shift_first: int32 [64], replicated, may hold values from -4 to 3, as said below
- fraction_first: float32 [64], replicated, may hold values from 0.1 to 0.9
- shift_second: int32 [64], replicated, may hold values from -16 to 15, as said below
- fraction_second: float32 [64], replicated, may hold values from 0.1 to 0.9
- scatter_kernel: float32 [17, 64], replicated, may hold values from -0.1875 to 0.1875
Outputs:
- wigner_next: float32 [64, 64, 64, 128], P('dir', None, 'pos')
The draws below stay inside these ranges and needn't reach their ends.
Inputs may be any that keep to these rules, and one draw needn't show every extreme that they name: `shift_first`: each value of the range is taken by exactly 8 directions. `shift_second`: each value of the range is taken by exactly 2 directions.
All inputs are finite; a program needn't handle non-finite values.
Results may differ from the reference program's by a relative error of at most 0.0003.
Values may be sent and summed in bfloat16 or wider, within the bound.
No kernel may reach another device: no remote copies, remote signals or barrier semaphores. Data moves between devices by JAX's collectives and lax.ppermute only.
A program may use at most 256 MiB of HBM per device.

```python
import math
import jax
import jax.numpy as jnp
from jax import lax

K1 = 64
K2 = 64
R = 8
H = 4
H2 = 16
X2 = 128
X1 = 64


def draw_shift_first(key, part):
    shuffled = jax.random.permutation(jax.random.fold_in(key, 101), K1)
    return (shuffled % (2 * H) - H).astype(jnp.int32)


def draw_shift_second(key, part):
    shuffled = jax.random.permutation(jax.random.fold_in(key, 202), K2)
    return (shuffled % (2 * H2) - H2).astype(jnp.int32)


def block_scale(rng, shape, shards, low, top_value):
    def one(dim, parts):
        draws = jax.random.uniform(jax.random.fold_in(jax.random.fold_in(rng, 6), dim), (parts,), jnp.float32, low / len(shards), top_value / len(shards))
        return jnp.repeat(jnp.exp(draws), shape[dim] // parts).reshape((-1,) + (1,) * (len(shape) - dim - 1))

    level = one(*shards[0])
    for cut in shards[1:]:
        level = level * one(*cut)
    return level


def bell_draw(own_key, extent, deviation, most, shards=(), held_as=jnp.bfloat16):
    result = deviation * jax.random.normal(own_key, extent, jnp.float32)
    if shards:
        result = result * block_scale(own_key, extent, shards, -0.22, 0.18)
    return jnp.clip(result, -most, most).astype(held_as)


def setup_inputs(seed: int = 0) -> dict:
    seeds = jax.random.split(jax.random.key(seed), 7)
    return {
        "coherence": bell_draw(seeds[0], (2, K1, K2, X1, X2), 1.0, 6.0, ((1, 2), (2, 16))),
        "shift_first": draw_shift_first(jax.random.fold_in(seeds[6], 71), 0),
        "fraction_first": jnp.clip(jax.random.uniform(seeds[2], (K1,), jnp.float32, 0.1, 0.9), 0.1, 0.9),
        "shift_second": draw_shift_second(jax.random.fold_in(seeds[6], 71), 0),
        "fraction_second": jnp.clip(jax.random.uniform(seeds[4], (K2,), jnp.float32, 0.1, 0.9), 0.1, 0.9),
        "scatter_kernel": bell_draw(seeds[5], (2 * R + 1, K2), ((2 * R + 1) * K2) ** -0.5, 0.1875, (), jnp.float32),
    }


def phase_tables(length):
    counter = jnp.arange(length, dtype=jnp.int32)
    product = counter[:, None] * counter[None, :] % length
    angles = product.astype(jnp.float32) * (2.0 * math.pi / length)
    factor = 1.0 / math.sqrt(length)
    return (jnp.cos(angles) * factor, jnp.sin(angles) * factor)

def contract(pattern, operand_a, operand_b):
    return jnp.einsum(pattern, operand_a, operand_b, precision=lax.Precision.HIGHEST, preferred_element_type=jnp.float32)

def reference(coherence, shift_first, fraction_first, shift_second, fraction_second, scatter_kernel):
    cos_one, sin_one = phase_tables(K1)
    cos_two, sin_two = phase_tables(K2)
    block_rows = 16

    def transform(block_index):
        start = (block_index * block_rows).astype(jnp.int32)
        block = lax.dynamic_slice_in_dim(coherence, start, block_rows, axis=3).astype(jnp.float32)
        real_mid = contract('ts,ksax->ktax', cos_two, block[0]) + contract('ts,ksax->ktax', sin_two, block[1])
        imag_mid = contract('ts,ksax->ktax', cos_two, block[1]) - contract('ts,ksax->ktax', sin_two, block[0])
        return contract('ts,sbax->tbax', cos_one, real_mid) + contract('ts,sbax->tbax', sin_one, imag_mid)
    blocks = lax.map(transform, jnp.arange(X1 // block_rows, dtype=jnp.int32))
    wigner = jnp.transpose(blocks, (1, 2, 0, 3, 4)).reshape(K1, K2, X1, X2)
    padded_one = jnp.pad(wigner, ((0, 0), (0, 0), (H, H), (0, 0)))

    def shear_first(slab, shift, weight):
        start = (H - shift).astype(jnp.int32)
        near_rows = lax.dynamic_slice_in_dim(slab, start, X1, axis=1)
        far_rows = lax.dynamic_slice_in_dim(slab, start - 1, X1, axis=1)
        return (1.0 - weight) * near_rows + weight * far_rows
    moved_one = jax.vmap(shear_first)(padded_one, shift_first, fraction_first)
    padded_two = jnp.pad(moved_one, ((0, 0), (0, 0), (0, 0), (H2, H2)))

    def shear_second(slab, shift, weight):
        start = (H2 - shift).astype(jnp.int32)
        near_rows = lax.dynamic_slice_in_dim(slab, start, X2, axis=2)
        far_rows = lax.dynamic_slice_in_dim(slab, start - 1, X2, axis=2)
        return (1.0 - weight) * near_rows + weight * far_rows
    moved_two = jax.vmap(shear_second, in_axes=(1, 0, 0), out_axes=1)(padded_two, shift_second, fraction_second)
    positions = jnp.arange(K2, dtype=jnp.int32)
    lag_index = (positions[:, None] - positions[None, :]) % K2
    circulant = scatter_kernel[:, lag_index]
    summed = moved_two
    for offset in range(2 * R + 1):
        rolled = jnp.roll(moved_two, -(offset - R), axis=0)
        summed = summed + contract('ij,kjax->kiax', circulant[offset], rolled)
    return summed
```

```python
import functools
import math

import jax
import jax.numpy as jnp
import numpy as np
from jax import lax
from jax.experimental import pallas as pl
from jax.experimental.pallas import tpu as pltpu
from jax.sharding import PartitionSpec as P

R = 8
H = 4
H2 = 16

UP_NEAR = ((4, 1), (5, 0), (5, 1), (6, 0), (6, 1), (7, 0))
UP_FAR = ((6, 1), (7, 0), (7, 1))
DOWN_NEAR = ((3, 0), (2, 0), (2, 1), (1, 0), (1, 1), (0, 1))
DOWN_FAR = ((1, 0), (0, 0), (0, 1))
HALOS = (UP_NEAR, UP_FAR, DOWN_NEAR, DOWN_FAR)
PER_SHIFT = 8
VMEM = pltpu.VMEM
SMEM = pltpu.SMEM


def split_np(table):
    high = table.astype(jnp.bfloat16)
    low = (table - high.astype(np.float32)).astype(jnp.bfloat16)
    return high, low


def split(value):
    high = value.astype(jnp.bfloat16)
    low = (value - high.astype(jnp.float32)).astype(jnp.bfloat16)
    return high, low


def natural_tables(length):
    counter = np.arange(length)
    angles = (counter[:, None] * counter[None, :] % length) * (2.0 * math.pi / length)
    factor = 1.0 / math.sqrt(length)
    return np.cos(angles) * factor, np.sin(angles) * factor


def first_tables(length, cuts):
    cos, sin = natural_tables(length)
    width = length // cuts
    real, imag = [], []
    for cut in range(cuts):
        cols = slice(cut * width, (cut + 1) * width)
        real += [cos[:, cols], sin[:, cols]]
        imag += [-sin[:, cols], cos[:, cols]]
    table = np.concatenate(real + imag, axis=1).astype(np.float32)
    return np.concatenate(split_np(table), axis=1)


def second_tables(length):
    cos, sin = natural_tables(length)
    table = np.concatenate([cos, sin], axis=1).astype(np.float32)
    return np.concatenate(split_np(table), axis=1)


def slot_onehot(shift_row, low, stride_shift, stride_repeat):
    count = shift_row.shape[1]
    across = jnp.broadcast_to(shift_row, (count, count))
    down = across.astype(jnp.float32).T.astype(jnp.int32)
    first = lax.broadcasted_iota(jnp.int32, (count, count), 0)
    second = lax.broadcasted_iota(jnp.int32, (count, count), 1)
    same = jnp.where((across == down) & (first < second), 1, 0)
    repeat = jnp.sum(same, axis=0, keepdims=True)
    slot = (shift_row - low) * stride_shift + repeat * stride_repeat
    return first == slot


def dot(lhs, rhs):
    return jnp.dot(lhs, rhs, preferred_element_type=jnp.float32)


def transform_kernel(
    pairs, shift_one, shift_two, fraction_two, table_one, table_two, received,
    out, up_near, up_far, down_near, down_far, left_one, left_two, weight_near, weight_far, middle,
):
    count = 64
    lanes = out.shape[-1]
    sources, local = received.shape[0], received.shape[1]
    groups = sources // pairs
    onehot_one = jnp.where(slot_onehot(shift_one[...], -H, PER_SHIFT, 1), 1.0, 0.0)
    picked = dot(onehot_one.astype(jnp.bfloat16), table_one[...]).astype(jnp.bfloat16)
    for part in range(4):
        left_one[part * count : (part + 1) * count, :] = picked[:, part * 128 : (part + 1) * 128]
    hot_two = slot_onehot(shift_two[...], -H2, 1, 2 * H2)
    onehot_two = jnp.where(hot_two, 1.0, 0.0)
    picked = dot(onehot_two.astype(jnp.bfloat16), table_two[...]).astype(jnp.bfloat16)
    left_two[:count, :128] = picked[:, :128]
    left_two[:count, 128:] = picked[:, :128]
    left_two[count:, :128] = picked[:, 128:]
    left_two[count:, 128:] = jnp.zeros((count, 128), jnp.bfloat16)
    part_two = jnp.sum(
        jnp.where(hot_two, jnp.broadcast_to(fraction_two[...], hot_two.shape), 0.0),
        axis=1, keepdims=True,
    )
    rows = lax.broadcasted_iota(jnp.int32, (count, lanes), 0)
    origin = lax.broadcasted_iota(jnp.int32, (count, lanes), 1) - (lax.rem(rows, 2 * H2) - H2)
    weight_near[...] = jnp.where((origin >= 0) & (origin < lanes), 1.0 - part_two, 0.0)
    weight_far[...] = jnp.where((origin >= 1) & (origin <= lanes), part_two, 0.0)

    def first(group, carry):
        for own in range(local):
            columns = []
            for row in range(2):
                blocks = [
                    received[pair * groups + group, own, part, row]
                    for pair in range(pairs)
                    for part in range(2)
                ]
                columns.append(jnp.concatenate(blocks, axis=0))
            both = dot(left_one[...], jnp.concatenate(columns, axis=1))
            both = both[: 2 * count] + both[2 * count :]
            start = pl.multiple_of((group * local + own) * 2 * count, 2 * count)
            for row in range(2):
                middle[row, pl.ds(start, 2 * count), :] = both[:, row * lanes : (row + 1) * lanes]
        return carry

    lax.fori_loop(0, groups, first, 0)

    targets = (up_near, up_far, down_near, down_far)
    for value in range(2 * H):

        def second(item, carry):
            slot = value * PER_SHIFT + item
            columns = []
            for row in range(2):
                parts = [
                    middle[row, pl.ds(part * count + slot, count, stride=2 * count), :]
                    for part in range(2)
                ]
                columns.append(jnp.concatenate(parts, axis=0))
            both = dot(
                left_two[...],
                jnp.concatenate(split(jnp.concatenate(columns, axis=1)), axis=0),
            )
            both = both[:count] + both[count:]
            for row in range(2):
                pieces = []
                for block in range(count // 8):
                    piece = both[block * 8 : block * 8 + 8, row * lanes : (row + 1) * lanes]
                    base = (lanes - H2 + 8 * (block % (2 * H2 // 8))) % lanes
                    near = pltpu.roll(piece, base, 1, stride=1, stride_axis=0)
                    far = pltpu.roll(near, 1, 1)
                    span = slice(block * 8, block * 8 + 8)
                    pieces.append(near * weight_near[span, :] + far * weight_far[span, :])
                moved = jnp.concatenate(pieces, axis=0)
                out[slot, row] = moved
                for target, wanted in zip(targets, HALOS):
                    if (value, row) in wanted:
                        target[wanted.index((value, row)) * PER_SHIFT + item] = moved
            return carry

        lax.fori_loop(0, PER_SHIFT, second, 0, unroll=2)


def scatter_table_kernel(shift_two, kernel, table, rows):
    count = kernel.shape[1]
    reach = kernel.shape[0]
    offsets = lax.broadcasted_iota(jnp.int32, kernel.shape, 0)
    lags = lax.broadcasted_iota(jnp.int32, kernel.shape, 1)
    full = kernel[...] + jnp.where((offsets == R) & (lags == 0), 1.0, 0.0)
    high, low = split(full)
    lag = lax.broadcasted_iota(jnp.int32, (count, 2 * count), 0)
    lane = lax.broadcasted_iota(jnp.int32, (count, 2 * count), 1)
    mirror = jnp.where(lax.rem(lag + lane, count) == 0, 1.0, 0.0).astype(jnp.bfloat16)
    rows[...] = jnp.zeros(rows.shape, jnp.float32)
    rows[0, 3 : 3 + reach, :] = dot(high, mirror)
    rows[1, 3 : 3 + reach, :] = dot(low, mirror)
    onehot = jnp.where(slot_onehot(shift_two[...], -H2, 1, 2 * H2), 1.0, 0.0).T
    blank = jnp.zeros((count, count), jnp.float32)
    choose = jnp.concatenate(
        [jnp.concatenate([onehot, blank], axis=1), jnp.concatenate([blank, onehot], axis=1)], axis=0
    ).astype(jnp.bfloat16)
    left = lane < count

    def circulant(part, index):
        row = jnp.broadcast_to(rows[part, index : index + 1, :], (8, 2 * count))
        return jnp.concatenate(
            [pltpu.roll(row, 8 * block, 1, stride=1, stride_axis=0) for block in range(count // 8)],
            axis=0,
        )

    for part in range(2):
        here = circulant(part, 0)
        for index in range(reach + 5):
            there = circulant(part, index + 1)
            pair = dot(jnp.where(left, here, there).astype(jnp.bfloat16), choose)
            pair = pair.astype(jnp.bfloat16)
            here = there
            for band in range(4):
                if (index - 3 + band) % 2 == 0 and 0 <= (index - 3 + band) // 2 < 10:
                    column = (index - 3 + band) // 2 * 128
                    start = part * 256 + band * count
                    table[start : start + count, column : column + 128] = pair


def scatter_groups(first_group, groups, table, high, low, out):
    def step(index, carry):
        start = pl.multiple_of((first_group + index) * 256, 256)
        both = dot(table[...], high[pl.ds(start, 1280), :])
        rest = dot(table[:256, :], low[pl.ds(start, 1280), :])
        total = both[:256] + both[256:] + rest
        target = pl.multiple_of(index * 256, 256)
        for row in range(2):
            out[row, pl.ds(target, 256), :] = total[:, row * 128 : (row + 1) * 128]
        return carry

    lax.fori_loop(0, groups, step, 0)


def shear_kernel(
    shift_one, fraction_one, table, moved, up_near, up_far, down_near, down_far,
    high, low, out, order, seen,
):
    count = moved.shape[0]
    for value in range(2 * H):
        seen[value] = 0

    def place(band, carry):
        value = shift_one[band] + H
        repeat = seen[value]
        order[value * PER_SHIFT + repeat] = band
        seen[value] = repeat + 1
        return carry

    lax.fori_loop(0, count, place, 0)
    sources = (up_near, up_far, down_near, down_far)

    def fetch(value, item, row):
        if row in (0, 1):
            return moved[value * PER_SHIFT + item, row]
        if row < 0:
            kind, key = (0, (value, row + 2)) if row >= -2 else (1, (value, row + 4))
        else:
            kind, key = (2, (value, row - 2)) if row <= 3 else (3, (value, row - 4))
        return sources[kind][HALOS[kind].index(key) * PER_SHIFT + item]

    for value in range(2 * H):
        shift = value - H

        def shear(item, carry):
            band = order[value * PER_SHIFT + item]
            weight = fraction_one[band]
            need = {
                row: fetch(value, item, row)
                for row in (-shift - 1, -shift, 1 - shift)
            }
            full = jnp.concatenate(
                [
                    (1.0 - weight) * need[row - shift] + weight * need[row - shift - 1]
                    for row in range(2)
                ],
                axis=1,
            )
            top, bottom = split(full)

            def put(index):
                start = pl.multiple_of(index * count, count)
                high[pl.ds(start, count), :] = top
                low[pl.ds(start, count), :] = bottom

            put(band + R)

            @pl.when(band < R)
            def _():
                put(band + R + count)

            @pl.when(band >= count - R)
            def _():
                put(band + R - count)

            return carry

        lax.fori_loop(0, PER_SHIFT, shear, 0)
    half = count // 8
    scatter_groups((1 - lax.axis_index("dir")) * half, half, table, high, low, out)


def scatter_kernel_own(table, high, low, out):
    half = out.shape[1] // 256
    scatter_groups(lax.axis_index("dir") * half, half, table, high, low, out)


def merge_kernel(own, other, out):
    size = own.shape[1]
    for d in range(2):

        @pl.when(lax.axis_index("dir") == d)
        def _():
            for row in range(2):
                out[pl.ds(2 * d + row, size, stride=4), :] = own[row]
                out[pl.ds(2 * (1 - d) + row, size, stride=4), :] = other[row]


def vmem(number):
    return [pl.BlockSpec(memory_space=VMEM)] * number


def smem(number):
    return [pl.BlockSpec(memory_space=SMEM)] * number


def fast_body(coherence, shift_first, fraction_first, shift_second, fraction_second, scatter_kernel):
    f32, bf16 = jnp.float32, jnp.bfloat16
    shape = jax.ShapeDtypeStruct
    pairs, places = lax.axis_size("dir"), lax.axis_size("pos")
    parts, own_first, own_second, cells, lanes = coherence.shape
    bands = own_first * pairs
    cut = coherence.reshape(parts, own_first, own_second, places, pairs, 2, lanes)
    cut = cut.transpose(4, 3, 2, 0, 5, 1, 6)
    cut = cut.reshape((pairs * places,) + cut.shape[2:])
    received = lax.all_to_all(cut, ("dir", "pos"), split_axis=0, concat_axis=0, tiled=True)

    row_one, row_two = shift_first.reshape(1, bands), shift_second.reshape(1, bands)
    halo_shapes = [shape((len(one) * PER_SHIFT, bands, lanes), f32) for one in HALOS]
    moved, *halos = pl.pallas_call(
        functools.partial(transform_kernel, pairs),
        out_shape=[shape((bands, 2, bands, lanes), f32)] + halo_shapes,
        in_specs=vmem(6),
        out_specs=vmem(5),
        scratch_shapes=[
            VMEM((4 * bands, 2 * bands), bf16),
            VMEM((2 * bands, 4 * bands), bf16),
            VMEM((bands, lanes), f32),
            VMEM((bands, lanes), f32),
            VMEM((2, 2 * bands * bands, lanes), f32),
        ],
        name="transform",
    )(
        row_one, row_two, fraction_second.reshape(1, bands),
        jnp.asarray(first_tables(bands, pairs)), jnp.asarray(second_tables(bands)), received,
    )

    def place(block):
        return block % pairs * places + block // pairs

    total = pairs * places
    arrived = []
    for halo, step in zip(halos, (1, 2, -1, -2)):
        hops = [(place(b), place(b + step)) for b in range(total) if 0 <= b + step < total]
        arrived.append(lax.ppermute(halo, ("dir", "pos"), hops))

    table = pl.pallas_call(
        scatter_table_kernel,
        out_shape=shape((512, 1280), bf16),
        in_specs=vmem(2),
        out_specs=pl.BlockSpec(memory_space=VMEM),
        scratch_shapes=[VMEM((2, 32, 2 * bands), f32)],
        name="scatter_table",
    )(row_two, scatter_kernel)

    wrapped = (bands + 2 * R) * bands
    half = bands * bands // 2
    high, low, away = pl.pallas_call(
        shear_kernel,
        out_shape=[shape((wrapped, 2 * lanes), bf16)] * 2 + [shape((2, half, lanes), f32)],
        in_specs=smem(2) + vmem(6),
        out_specs=vmem(3),
        scratch_shapes=[SMEM((bands,), jnp.int32), SMEM((2 * H,), jnp.int32)],
        name="shear",
    )(shift_first, fraction_first, table, moved, *arrived)
    other = lax.ppermute(away, "dir", [(0, 1), (1, 0)])
    own = pl.pallas_call(
        scatter_kernel_own,
        out_shape=shape((2, half, lanes), f32),
        in_specs=vmem(3),
        out_specs=pl.BlockSpec(memory_space=VMEM),
        name="scatter",
    )(table, high, low)
    steps = 8
    merged = pl.pallas_call(
        merge_kernel,
        out_shape=shape((half * 4, lanes), f32),
        grid=(steps,),
        in_specs=[pl.BlockSpec((2, half // steps, lanes), lambda i: (0, i, 0))] * 2,
        out_specs=pl.BlockSpec((half * 4 // steps, lanes), lambda i: (i, 0)),
        name="merge",
    )(own, other)
    return merged.reshape(own_first, bands, 4, lanes)


def with_halo(cells, sides, width, closed):
    for axis, dim in sides:
        count = lax.axis_size(axis)
        ends = count if closed else count - 1
        head = lax.slice_in_dim(cells, 0, width, axis=dim)
        tail = lax.slice_in_dim(cells, cells.shape[dim] - width, cells.shape[dim], axis=dim)
        cells = jnp.concatenate(
            [
                lax.ppermute(tail, axis, [(i, (i + 1) % count) for i in range(ends)]),
                cells,
                lax.ppermute(head, axis, [((i + 1) % count, i) for i in range(ends)]),
            ],
            axis=dim,
        )
    return cells


def phase_tables(length):
    counter = jnp.arange(length, dtype=jnp.int32)
    product = counter[:, None] * counter[None, :] % length
    angles = product.astype(jnp.float32) * (2.0 * math.pi / length)
    factor = 1.0 / math.sqrt(length)
    return (jnp.cos(angles) * factor, jnp.sin(angles) * factor)


def contract(pattern, operand_a, operand_b):
    return jnp.einsum(
        pattern,
        operand_a,
        operand_b,
        precision=lax.Precision.HIGHEST,
        preferred_element_type=jnp.float32,
    )


def finish_bands(received):
    cos_one, sin_one = phase_tables(received.shape[1])
    real_part = contract("ts,sbax->tbax", cos_one, received[0]) + contract(
        "ts,sbax->tbax", sin_one, received[1]
    )
    return lax.all_to_all(real_part, "dir", split_axis=0, concat_axis=1, tiled=True)


def shear_block(wigner, shift_first, fraction_first):
    band_count = wigner.shape[0]
    cell_count = wigner.shape[2]
    first_band = lax.axis_index("dir") * band_count
    shifts = lax.dynamic_slice_in_dim(shift_first, first_band, band_count)
    weights = lax.dynamic_slice_in_dim(fraction_first, first_band, band_count)
    padded = with_halo(wigner, (("pos", 2),), H, False)
    rows_out = jnp.arange(cell_count, dtype=jnp.int32)
    rows_in = jnp.arange(cell_count + 2 * H, dtype=jnp.int32)
    target = rows_out[None, :, None] + H - shifts[:, None, None]
    near_tap = (rows_in[None, None, :] == target).astype(jnp.float32)
    far_tap = (rows_in[None, None, :] == target - 1).astype(jnp.float32)
    band_matrix = (1.0 - weights)[:, None, None] * near_tap + weights[:, None, None] * far_tap
    return contract("kaj,kbjx->kbax", band_matrix, padded)


def convolve(circulant, source, out_rows):
    summed = jnp.zeros((out_rows,) + source.shape[1:], jnp.float32)
    for offset in range(circulant.shape[0]):
        summed = summed + contract(
            "ij,kjax->kiax", circulant[offset], source[offset : offset + out_rows]
        )
    return summed


def body(coherence, shift_first, fraction_first, shift_second, fraction_second, scatter_kernel):
    direction_count = coherence.shape[2] * lax.axis_size("pos")
    cos_two, sin_two = phase_tables(direction_count)
    cell_block = lax.all_to_all(coherence, "pos", split_axis=3, concat_axis=2, tiled=True)
    real_in = cell_block[0].astype(jnp.float32)
    imag_in = cell_block[1].astype(jnp.float32)
    real_mid = contract("ts,bsax->btax", cos_two, real_in) + contract(
        "ts,bsax->btax", sin_two, imag_in
    )
    imag_mid = contract("ts,bsax->btax", cos_two, imag_in) - contract(
        "ts,bsax->btax", sin_two, real_in
    )
    mixed = jnp.stack([real_mid, imag_mid])
    wigner = finish_bands(lax.all_to_all(mixed, "dir", split_axis=2, concat_axis=1, tiled=True))
    moved_one = shear_block(wigner, shift_first, fraction_first)
    band_count = moved_one.shape[0]
    column_count = moved_one.shape[3]
    positions = jnp.arange(column_count, dtype=jnp.int32)
    target_two = positions[None, :, None] - shift_second[:, None, None]
    near_two = (positions[None, None, :] == target_two).astype(jnp.float32)
    far_two = (positions[None, None, :] == target_two - 1).astype(jnp.float32)
    shear_matrix = (1.0 - fraction_second)[:, None, None] * near_two + fraction_second[
        :, None, None
    ] * far_two
    moved_two = contract("bxy,kbay->kbax", shear_matrix, moved_one)
    kernel_positions = jnp.arange(direction_count, dtype=jnp.int32)
    lag_index = (kernel_positions[:, None] - kernel_positions[None, :]) % direction_count
    circulant = scatter_kernel[:, lag_index]
    extended = with_halo(moved_two, (("dir", 0),), R, True)
    summed = moved_two + convolve(circulant, extended, band_count)
    return summed


def fits(mesh, coherence):
    pairs, places = mesh.shape["dir"], mesh.shape["pos"]
    parts, first, second, cells, lanes = coherence.shape
    return (pairs, first, second, cells, lanes) == (2, 64, 64, 4 * places, 128)


def solution(mesh):
    placed = (P(None, "dir", "pos", None, None), P(), P(), P(), P(), P())

    def run(*arrays):
        chosen = fast_body if fits(mesh, arrays[0]) else body
        return jax.shard_map(
            chosen, mesh=mesh, in_specs=placed, out_specs=P("dir", None, "pos", None), check_vma=False
        )(*arrays)

    return run
```

```python
import functools
import math

import jax
import jax.numpy as jnp
import numpy as np
from jax import lax
from jax.experimental import pallas as pl
from jax.experimental.pallas import tpu as pltpu
from jax.sharding import PartitionSpec as P

R = 8
H = 4
H2 = 16

UP_NEAR = ((4, 1), (5, 0), (5, 1), (6, 0), (6, 1), (7, 0))
UP_FAR = ((6, 1), (7, 0), (7, 1))
DOWN_NEAR = ((3, 0), (2, 0), (2, 1), (1, 0), (1, 1), (0, 1))
DOWN_FAR = ((1, 0), (0, 0), (0, 1))
HALOS = (UP_NEAR, UP_FAR, DOWN_NEAR, DOWN_FAR)
PER_SHIFT = 8
TOP = 32600.0
FINE = 8.0
LEAST = 1e-30
VMEM = pltpu.VMEM
SMEM = pltpu.SMEM


def split_np(table):
    high = table.astype(jnp.bfloat16)
    low = (table - high.astype(np.float32)).astype(jnp.bfloat16)
    return high, low


def split(value):
    high = value.astype(jnp.bfloat16)
    low = (value - high.astype(jnp.float32)).astype(jnp.bfloat16)
    return high, low


def natural_tables(length):
    counter = np.arange(length)
    angles = (counter[:, None] * counter[None, :] % length) * (2.0 * math.pi / length)
    factor = 1.0 / math.sqrt(length)
    return np.cos(angles) * factor, np.sin(angles) * factor


def first_tables(length, cuts):
    cos, sin = natural_tables(length)
    width = length // cuts
    real, imag = [], []
    for cut in range(cuts):
        cols = slice(cut * width, (cut + 1) * width)
        real += [cos[:, cols], sin[:, cols]]
        imag += [-sin[:, cols], cos[:, cols]]
    table = np.concatenate(real + imag, axis=1).astype(np.float32)
    return np.concatenate(split_np(table), axis=1)


def second_tables(length):
    cos, sin = natural_tables(length)
    table = np.concatenate([cos, sin], axis=1).astype(np.float32)
    return np.concatenate(split_np(table), axis=1)


def slot_onehot(shift_row, low, stride_shift, stride_repeat):
    count = shift_row.shape[1]
    across = jnp.broadcast_to(shift_row, (count, count))
    down = across.astype(jnp.float32).T.astype(jnp.int32)
    first = lax.broadcasted_iota(jnp.int32, (count, count), 0)
    second = lax.broadcasted_iota(jnp.int32, (count, count), 1)
    same = jnp.where((across == down) & (first < second), 1, 0)
    repeat = jnp.sum(same, axis=0, keepdims=True)
    slot = (shift_row - low) * stride_shift + repeat * stride_repeat
    return first == slot


def dot(lhs, rhs):
    return jnp.dot(lhs, rhs, preferred_element_type=jnp.float32)


def encode(columns):
    largest = jnp.maximum(jnp.max(jnp.abs(columns), axis=0, keepdims=True), LEAST)
    scale = jnp.ceil(jnp.log2(largest) * FINE)
    codes = jnp.round(columns * (jnp.exp2(scale * (-1.0 / FINE)) * TOP))
    return codes.astype(jnp.int32).astype(jnp.int16), scale


def decode(codes, scale):
    return codes.astype(jnp.int32).astype(jnp.float32) * (jnp.exp2(scale * (1.0 / FINE)) * (1.0 / TOP))


def transform_kernel(
    pairs, shift_one, shift_two, fraction_two, table_one, table_two, received,
    out, up_near, up_far, down_near, down_far, left_one, left_two, weight_near, weight_far, middle, scales,
):
    count = 64
    lanes = out.shape[-1]
    sources, local = received.shape[0], received.shape[1]
    groups = sources // pairs
    onehot_one = jnp.where(slot_onehot(shift_one[...], -H, PER_SHIFT, 1), 1.0, 0.0)
    picked = dot(onehot_one.astype(jnp.bfloat16), table_one[...]).astype(jnp.bfloat16)
    for part in range(4):
        left_one[part * count : (part + 1) * count, :] = picked[:, part * 128 : (part + 1) * 128]
    hot_two = slot_onehot(shift_two[...], -H2, 1, 2 * H2)
    onehot_two = jnp.where(hot_two, 1.0, 0.0)
    picked = dot(onehot_two.astype(jnp.bfloat16), table_two[...]).astype(jnp.bfloat16)
    left_two[:count, :128] = picked[:, :128]
    left_two[:count, 128:] = picked[:, :128]
    left_two[count:, :128] = picked[:, 128:]
    left_two[count:, 128:] = jnp.zeros((count, 128), jnp.bfloat16)
    part_two = jnp.sum(
        jnp.where(hot_two, jnp.broadcast_to(fraction_two[...], hot_two.shape), 0.0),
        axis=1, keepdims=True,
    )
    rows = lax.broadcasted_iota(jnp.int32, (count, lanes), 0)
    origin = lax.broadcasted_iota(jnp.int32, (count, lanes), 1) - (lax.rem(rows, 2 * H2) - H2)
    weight_near[...] = jnp.where((origin >= 0) & (origin < lanes), 1.0 - part_two, 0.0)
    weight_far[...] = jnp.where((origin >= 1) & (origin <= lanes), part_two, 0.0)

    def first(group, carry):
        for own in range(local):
            columns = []
            for row in range(2):
                blocks = [
                    received[pair * groups + group, own, part, row]
                    for pair in range(pairs)
                    for part in range(2)
                ]
                columns.append(jnp.concatenate(blocks, axis=0))
            both = dot(left_one[...], jnp.concatenate(columns, axis=1))
            both = both[: 2 * count] + both[2 * count :]
            start = pl.multiple_of((group * local + own) * 2 * count, 2 * count)
            for row in range(2):
                middle[row, pl.ds(start, 2 * count), :] = both[:, row * lanes : (row + 1) * lanes]
        return carry

    lax.fori_loop(0, groups, first, 0)

    targets = (up_near, up_far, down_near, down_far)
    for value in range(2 * H):

        def second(item, carry):
            slot = value * PER_SHIFT + item
            columns = []
            for row in range(2):
                parts = [
                    middle[row, pl.ds(part * count + slot, count, stride=2 * count), :]
                    for part in range(2)
                ]
                columns.append(jnp.concatenate(parts, axis=0))
            both = dot(
                left_two[...],
                jnp.concatenate(split(jnp.concatenate(columns, axis=1)), axis=0),
            )
            both = both[:count] + both[count:]
            for row in range(2):
                pieces = []
                for block in range(count // 8):
                    piece = both[block * 8 : block * 8 + 8, row * lanes : (row + 1) * lanes]
                    base = (lanes - H2 + 8 * (block % (2 * H2 // 8))) % lanes
                    near = pltpu.roll(piece, base, 1, stride=1, stride_axis=0)
                    far = pltpu.roll(near, 1, 1)
                    span = slice(block * 8, block * 8 + 8)
                    pieces.append(near * weight_near[span, :] + far * weight_far[span, :])
                moved = jnp.concatenate(pieces, axis=0)
                out[slot, row] = moved
                hits = [
                    (kind, wanted.index((value, row)))
                    for kind, wanted in enumerate(HALOS)
                    if (value, row) in wanted
                ]
                if hits:
                    codes, scale = encode(moved)
                for kind, index in hits:
                    place = index * PER_SHIFT + item
                    start = pl.multiple_of(place * count, count)
                    targets[kind][pl.ds(start, count), :] = codes
                    scales[kind, pl.ds(place, 1), :] = scale
            return carry

        lax.fori_loop(0, PER_SHIFT, second, 0, unroll=2)
    for kind, target in enumerate(targets):
        entries = target.shape[0] // (count + 1)
        target[entries * count :, :] = scales[kind, :entries, :].astype(jnp.int32).astype(jnp.int16)


def scatter_table_kernel(shift_two, kernel, table, rows):
    count = kernel.shape[1]
    reach = kernel.shape[0]
    offsets = lax.broadcasted_iota(jnp.int32, kernel.shape, 0)
    lags = lax.broadcasted_iota(jnp.int32, kernel.shape, 1)
    full = kernel[...] + jnp.where((offsets == R) & (lags == 0), 1.0, 0.0)
    high, low = split(full)
    lag = lax.broadcasted_iota(jnp.int32, (count, 2 * count), 0)
    lane = lax.broadcasted_iota(jnp.int32, (count, 2 * count), 1)
    mirror = jnp.where(lax.rem(lag + lane, count) == 0, 1.0, 0.0).astype(jnp.bfloat16)
    rows[...] = jnp.zeros(rows.shape, jnp.float32)
    rows[0, 3 : 3 + reach, :] = dot(high, mirror)
    rows[1, 3 : 3 + reach, :] = dot(low, mirror)
    onehot = jnp.where(slot_onehot(shift_two[...], -H2, 1, 2 * H2), 1.0, 0.0).T
    blank = jnp.zeros((count, count), jnp.float32)
    choose = jnp.concatenate(
        [jnp.concatenate([onehot, blank], axis=1), jnp.concatenate([blank, onehot], axis=1)], axis=0
    ).astype(jnp.bfloat16)
    left = lane < count

    def circulant(part, index):
        row = jnp.broadcast_to(rows[part, index : index + 1, :], (8, 2 * count))
        return jnp.concatenate(
            [pltpu.roll(row, 8 * block, 1, stride=1, stride_axis=0) for block in range(count // 8)],
            axis=0,
        )

    for part in range(2):
        here = circulant(part, 0)
        for index in range(reach + 5):
            there = circulant(part, index + 1)
            pair = dot(jnp.where(left, here, there).astype(jnp.bfloat16), choose)
            pair = pair.astype(jnp.bfloat16)
            here = there
            for band in range(4):
                if (index - 3 + band) % 2 == 0 and 0 <= (index - 3 + band) // 2 < 10:
                    column = (index - 3 + band) // 2 * 128
                    start = part * 256 + band * count
                    table[start : start + count, column : column + 128] = pair


def scatter_groups(first_group, groups, table, high, low, out, scales=None):
    def step(index, carry):
        start = pl.multiple_of((first_group + index) * 256, 256)
        both = dot(table[...], high[pl.ds(start, 1280), :])
        rest = dot(table[:256, :], low[pl.ds(start, 1280), :])
        total = both[:256] + both[256:] + rest
        target = pl.multiple_of(index * 256, 256)
        for row in range(2):
            part = total[:, row * 128 : (row + 1) * 128]
            if scales is None:
                out[row, pl.ds(target, 256), :] = part
                continue
            blocks = [encode(part[band * 64 : band * 64 + 64]) for band in range(4)]
            out[row, pl.ds(target, 256), :] = jnp.concatenate([codes for codes, _ in blocks], axis=0)
            for band in range(4):
                scales[row, pl.ds(index * 4 + band, 1), :] = blocks[band][1]
        return carry

    lax.fori_loop(0, groups, step, 0)


def shear_kernel(
    shift_one, fraction_one, table, moved, up_near, up_far, down_near, down_far,
    high, low, out, order, seen, arrived, sent,
):
    count = moved.shape[0]
    for value in range(2 * H):
        seen[value] = 0

    def place(band, carry):
        value = shift_one[band] + H
        repeat = seen[value]
        order[value * PER_SHIFT + repeat] = band
        seen[value] = repeat + 1
        return carry

    lax.fori_loop(0, count, place, 0)
    sources = (up_near, up_far, down_near, down_far)
    for kind, source in enumerate(sources):
        entries = source.shape[0] // (count + 1)
        codes = source[entries * count :, :].astype(jnp.int32)
        arrived[kind, :entries, :] = codes.astype(jnp.float32)

    def fetch(value, item, row):
        if row in (0, 1):
            return moved[value * PER_SHIFT + item, row]
        if row < 0:
            kind, key = (0, (value, row + 2)) if row >= -2 else (1, (value, row + 4))
        else:
            kind, key = (2, (value, row - 2)) if row <= 3 else (3, (value, row - 4))
        place = HALOS[kind].index(key) * PER_SHIFT + item
        start = pl.multiple_of(place * count, count)
        return decode(sources[kind][pl.ds(start, count), :], arrived[kind, pl.ds(place, 1), :])

    for value in range(2 * H):
        shift = value - H

        def shear(item, carry):
            band = order[value * PER_SHIFT + item]
            weight = fraction_one[band]
            need = {
                row: fetch(value, item, row)
                for row in (-shift - 1, -shift, 1 - shift)
            }
            full = jnp.concatenate(
                [
                    (1.0 - weight) * need[row - shift] + weight * need[row - shift - 1]
                    for row in range(2)
                ],
                axis=1,
            )
            top, bottom = split(full)

            def put(index):
                start = pl.multiple_of(index * count, count)
                high[pl.ds(start, count), :] = top
                low[pl.ds(start, count), :] = bottom

            put(band + R)

            @pl.when(band < R)
            def _():
                put(band + R + count)

            @pl.when(band >= count - R)
            def _():
                put(band + R - count)

            return carry

        lax.fori_loop(0, PER_SHIFT, shear, 0)
    half = count // 8
    scatter_groups((1 - lax.axis_index("dir")) * half, half, table, high, low, out, sent)
    size = 4 * half * count
    for row in range(2):
        out[row, size:, :] = sent[row].astype(jnp.int32).astype(jnp.int16)


def scatter_kernel_own(table, high, low, out):
    half = out.shape[1] // 256
    scatter_groups(lax.axis_index("dir") * half, half, table, high, low, out)


def merge_kernel(own, other, scale, out, scales):
    size = own.shape[1]
    bands = size // 64
    for row in range(2):
        scales[row] = scale[row].astype(jnp.int32).astype(jnp.float32)
    step = pl.program_id(0)
    for d in range(2):

        @pl.when(lax.axis_index("dir") == d)
        def _():
            for row in range(2):
                out[pl.ds(2 * d + row, size, stride=4), :] = own[row]
                for band in range(bands):
                    rows = other[row, band * 64 : band * 64 + 64, :]
                    value = decode(rows, scales[row, pl.ds(step * bands + band, 1), :])
                    out[pl.ds(2 * (1 - d) + row + band * 256, 64, stride=4), :] = value


def vmem(number):
    return [pl.BlockSpec(memory_space=VMEM)] * number


def smem(number):
    return [pl.BlockSpec(memory_space=SMEM)] * number


def fast_body(coherence, shift_first, fraction_first, shift_second, fraction_second, scatter_kernel):
    f32, bf16 = jnp.float32, jnp.bfloat16
    shape = jax.ShapeDtypeStruct
    pairs, places = lax.axis_size("dir"), lax.axis_size("pos")
    parts, own_first, own_second, cells, lanes = coherence.shape
    bands = own_first * pairs
    cut = coherence.reshape(parts, own_first, own_second, places, pairs, 2, lanes)
    cut = cut.transpose(4, 3, 2, 0, 5, 1, 6)
    cut = cut.reshape((pairs * places,) + cut.shape[2:])
    received = lax.all_to_all(cut, ("dir", "pos"), split_axis=0, concat_axis=0, tiled=True)

    row_one, row_two = shift_first.reshape(1, bands), shift_second.reshape(1, bands)
    halo_shapes = [shape((len(one) * PER_SHIFT * (bands + 1), lanes), jnp.int16) for one in HALOS]
    moved, *halos = pl.pallas_call(
        functools.partial(transform_kernel, pairs),
        out_shape=[shape((bands, 2, bands, lanes), f32)] + halo_shapes,
        in_specs=vmem(6),
        out_specs=vmem(5),
        scratch_shapes=[
            VMEM((4 * bands, 2 * bands), bf16),
            VMEM((2 * bands, 4 * bands), bf16),
            VMEM((bands, lanes), f32),
            VMEM((bands, lanes), f32),
            VMEM((2, 2 * bands * bands, lanes), f32),
            VMEM((4, len(UP_NEAR) * PER_SHIFT, lanes), f32),
        ],
        name="transform",
    )(
        row_one, row_two, fraction_second.reshape(1, bands),
        jnp.asarray(first_tables(bands, pairs)), jnp.asarray(second_tables(bands)), received,
    )

    def place(block):
        return block % pairs * places + block // pairs

    total = pairs * places
    arrived = []
    for halo, step in zip(halos, (1, 2, -1, -2)):
        hops = [(place(b), place(b + step)) for b in range(total) if 0 <= b + step < total]
        arrived.append(lax.ppermute(halo, ("dir", "pos"), hops))

    table = pl.pallas_call(
        scatter_table_kernel,
        out_shape=shape((512, 1280), bf16),
        in_specs=vmem(2),
        out_specs=pl.BlockSpec(memory_space=VMEM),
        scratch_shapes=[VMEM((2, 32, 2 * bands), f32)],
        name="scatter_table",
    )(row_two, scatter_kernel)

    wrapped = (bands + 2 * R) * bands
    half = bands * bands // 2
    high, low, away = pl.pallas_call(
        shear_kernel,
        out_shape=[shape((wrapped, 2 * lanes), bf16)] * 2 + [shape((2, half + bands // 2, lanes), jnp.int16)],
        in_specs=smem(2) + vmem(6),
        out_specs=vmem(3),
        scratch_shapes=[
            SMEM((bands,), jnp.int32),
            SMEM((2 * H,), jnp.int32),
            VMEM((4, len(UP_NEAR) * PER_SHIFT, lanes), f32),
            VMEM((2, bands // 2, lanes), f32),
        ],
        name="shear",
    )(shift_first, fraction_first, table, moved, *arrived)
    other = lax.ppermute(away, "dir", [(0, 1), (1, 0)])
    own = pl.pallas_call(
        scatter_kernel_own,
        out_shape=shape((2, half, lanes), f32),
        in_specs=vmem(3),
        out_specs=pl.BlockSpec(memory_space=VMEM),
        name="scatter",
    )(table, high, low)
    steps = 8
    merged = pl.pallas_call(
        merge_kernel,
        out_shape=shape((half * 4, lanes), f32),
        grid=(steps,),
        in_specs=[pl.BlockSpec((2, half // steps, lanes), lambda i: (0, i, 0))] * 2
        + [pl.BlockSpec((2, bands // 2, lanes), lambda i: (0, half // (bands // 2), 0))],
        out_specs=pl.BlockSpec((half * 4 // steps, lanes), lambda i: (i, 0)),
        scratch_shapes=[VMEM((2, bands // 2, lanes), f32)],
        name="merge",
    )(own, other, other)
    return merged.reshape(own_first, bands, 4, lanes)


def with_halo(cells, sides, width, closed):
    for axis, dim in sides:
        count = lax.axis_size(axis)
        ends = count if closed else count - 1
        head = lax.slice_in_dim(cells, 0, width, axis=dim)
        tail = lax.slice_in_dim(cells, cells.shape[dim] - width, cells.shape[dim], axis=dim)
        cells = jnp.concatenate(
            [
                lax.ppermute(tail, axis, [(i, (i + 1) % count) for i in range(ends)]),
                cells,
                lax.ppermute(head, axis, [((i + 1) % count, i) for i in range(ends)]),
            ],
            axis=dim,
        )
    return cells


def phase_tables(length):
    counter = jnp.arange(length, dtype=jnp.int32)
    product = counter[:, None] * counter[None, :] % length
    angles = product.astype(jnp.float32) * (2.0 * math.pi / length)
    factor = 1.0 / math.sqrt(length)
    return (jnp.cos(angles) * factor, jnp.sin(angles) * factor)


def contract(pattern, operand_a, operand_b):
    return jnp.einsum(
        pattern,
        operand_a,
        operand_b,
        precision=lax.Precision.HIGHEST,
        preferred_element_type=jnp.float32,
    )


def finish_bands(received):
    cos_one, sin_one = phase_tables(received.shape[1])
    real_part = contract("ts,sbax->tbax", cos_one, received[0]) + contract(
        "ts,sbax->tbax", sin_one, received[1]
    )
    return lax.all_to_all(real_part, "dir", split_axis=0, concat_axis=1, tiled=True)


def shear_block(wigner, shift_first, fraction_first):
    band_count = wigner.shape[0]
    cell_count = wigner.shape[2]
    first_band = lax.axis_index("dir") * band_count
    shifts = lax.dynamic_slice_in_dim(shift_first, first_band, band_count)
    weights = lax.dynamic_slice_in_dim(fraction_first, first_band, band_count)
    padded = with_halo(wigner, (("pos", 2),), H, False)
    rows_out = jnp.arange(cell_count, dtype=jnp.int32)
    rows_in = jnp.arange(cell_count + 2 * H, dtype=jnp.int32)
    target = rows_out[None, :, None] + H - shifts[:, None, None]
    near_tap = (rows_in[None, None, :] == target).astype(jnp.float32)
    far_tap = (rows_in[None, None, :] == target - 1).astype(jnp.float32)
    band_matrix = (1.0 - weights)[:, None, None] * near_tap + weights[:, None, None] * far_tap
    return contract("kaj,kbjx->kbax", band_matrix, padded)


def convolve(circulant, source, out_rows):
    summed = jnp.zeros((out_rows,) + source.shape[1:], jnp.float32)
    for offset in range(circulant.shape[0]):
        summed = summed + contract(
            "ij,kjax->kiax", circulant[offset], source[offset : offset + out_rows]
        )
    return summed


def body(coherence, shift_first, fraction_first, shift_second, fraction_second, scatter_kernel):
    direction_count = coherence.shape[2] * lax.axis_size("pos")
    cos_two, sin_two = phase_tables(direction_count)
    cell_block = lax.all_to_all(coherence, "pos", split_axis=3, concat_axis=2, tiled=True)
    real_in = cell_block[0].astype(jnp.float32)
    imag_in = cell_block[1].astype(jnp.float32)
    real_mid = contract("ts,bsax->btax", cos_two, real_in) + contract(
        "ts,bsax->btax", sin_two, imag_in
    )
    imag_mid = contract("ts,bsax->btax", cos_two, imag_in) - contract(
        "ts,bsax->btax", sin_two, real_in
    )
    mixed = jnp.stack([real_mid, imag_mid])
    wigner = finish_bands(lax.all_to_all(mixed, "dir", split_axis=2, concat_axis=1, tiled=True))
    moved_one = shear_block(wigner, shift_first, fraction_first)
    band_count = moved_one.shape[0]
    column_count = moved_one.shape[3]
    positions = jnp.arange(column_count, dtype=jnp.int32)
    target_two = positions[None, :, None] - shift_second[:, None, None]
    near_two = (positions[None, None, :] == target_two).astype(jnp.float32)
    far_two = (positions[None, None, :] == target_two - 1).astype(jnp.float32)
    shear_matrix = (1.0 - fraction_second)[:, None, None] * near_two + fraction_second[
        :, None, None
    ] * far_two
    moved_two = contract("bxy,kbay->kbax", shear_matrix, moved_one)
    kernel_positions = jnp.arange(direction_count, dtype=jnp.int32)
    lag_index = (kernel_positions[:, None] - kernel_positions[None, :]) % direction_count
    circulant = scatter_kernel[:, lag_index]
    extended = with_halo(moved_two, (("dir", 0),), R, True)
    summed = moved_two + convolve(circulant, extended, band_count)
    return summed


def fits(mesh, coherence):
    pairs, places = mesh.shape["dir"], mesh.shape["pos"]
    parts, first, second, cells, lanes = coherence.shape
    return (pairs, first, second, cells, lanes) == (2, 64, 64, 4 * places, 128)


def solution(mesh):
    placed = (P(None, "dir", "pos", None, None), P(), P(), P(), P(), P())

    def run(*arrays):
        chosen = fast_body if fits(mesh, arrays[0]) else body
        return jax.shard_map(
            chosen, mesh=mesh, in_specs=placed, out_specs=P("dir", None, "pos", None), check_vma=False
        )(*arrays)

    return run
```

```python
import functools
import math

import jax
import jax.numpy as jnp
import numpy as np
from jax import lax
from jax.experimental import pallas as pl
from jax.experimental.pallas import tpu as pltpu
from jax.sharding import PartitionSpec as P

R = 8
H = 4
H2 = 16

UP_NEAR = ((4, 1), (5, 0), (5, 1), (6, 0), (6, 1), (7, 0))
UP_FAR = ((6, 1), (7, 0), (7, 1))
DOWN_NEAR = ((3, 0), (2, 0), (2, 1), (1, 0), (1, 1), (0, 1))
DOWN_FAR = ((1, 0), (0, 0), (0, 1))
HALOS = (UP_NEAR, UP_FAR, DOWN_NEAR, DOWN_FAR)
PER_SHIFT = 8
TOP = 32600.0
FINE = 8.0
LEAST = 1e-30
VMEM = pltpu.VMEM
SMEM = pltpu.SMEM


def split_np(table):
    high = table.astype(jnp.bfloat16)
    low = (table - high.astype(np.float32)).astype(jnp.bfloat16)
    return high, low


def split(value):
    high = value.astype(jnp.bfloat16)
    low = (value - high.astype(jnp.float32)).astype(jnp.bfloat16)
    return high, low


def natural_tables(length):
    counter = np.arange(length)
    angles = (counter[:, None] * counter[None, :] % length) * (2.0 * math.pi / length)
    factor = 1.0 / math.sqrt(length)
    return np.cos(angles) * factor, np.sin(angles) * factor


def first_tables(length, cuts):
    cos, sin = natural_tables(length)
    width = length // cuts
    real, imag = [], []
    for cut in range(cuts):
        cols = slice(cut * width, (cut + 1) * width)
        real += [cos[:, cols], sin[:, cols]]
        imag += [-sin[:, cols], cos[:, cols]]
    table = np.concatenate(real + imag, axis=1).astype(np.float32)
    return np.concatenate(split_np(table), axis=1)


def second_tables(length):
    cos, sin = natural_tables(length)
    table = np.concatenate([cos, sin], axis=1).astype(np.float32)
    return np.concatenate(split_np(table), axis=1)


def slot_onehot(shift_row, low, stride_shift, stride_repeat):
    count = shift_row.shape[1]
    across = jnp.broadcast_to(shift_row, (count, count))
    down = across.astype(jnp.float32).T.astype(jnp.int32)
    first = lax.broadcasted_iota(jnp.int32, (count, count), 0)
    second = lax.broadcasted_iota(jnp.int32, (count, count), 1)
    same = jnp.where((across == down) & (first < second), 1, 0)
    repeat = jnp.sum(same, axis=0, keepdims=True)
    slot = (shift_row - low) * stride_shift + repeat * stride_repeat
    return first == slot


def dot(lhs, rhs):
    return jnp.dot(lhs, rhs, preferred_element_type=jnp.float32)


def place_in_line(pair, block):
    return block // 2 * 4 + (pair + block // 2) % 2 * 2 + block % 2


def device_of(line, places):
    quad, step = line // 4, line % 4
    return (step // 2 + quad) % 2 * places + quad * 2 + step % 2


def encode(columns):
    largest = jnp.maximum(jnp.max(jnp.abs(columns), axis=0, keepdims=True), LEAST)
    scale = jnp.ceil(jnp.log2(largest) * FINE)
    codes = jnp.round(columns * (jnp.exp2(scale * (-1.0 / FINE)) * TOP))
    return codes.astype(jnp.int32).astype(jnp.int16), scale


def decode(codes, scale):
    return codes.astype(jnp.int32).astype(jnp.float32) * (jnp.exp2(scale * (1.0 / FINE)) * (1.0 / TOP))


def transform_kernel(
    pairs, shift_one, shift_two, fraction_two, table_one, table_two, source,
    out, up_near, up_far, down_near, down_far, left_one, left_two, weight_near, weight_far, middle, scales,
    received, stage, load_sem, store_sem,
):
    count = 64
    lanes = out.shape[-1]
    local = received.shape[1]
    lines = received.shape[0] // (count // 8)
    loads = [
        pltpu.make_async_copy(
            source.at[pl.ds(block * lines, lines)],
            received.at[pl.ds(block * lines, lines)],
            load_sem.at[block],
        )
        for block in range(count // 8)
    ]
    for load in loads:
        load.start()
    onehot_one = jnp.where(slot_onehot(shift_one[...], -H, PER_SHIFT, 1), 1.0, 0.0)
    picked = dot(onehot_one.astype(jnp.bfloat16), table_one[...]).astype(jnp.bfloat16)
    for part in range(4):
        left_one[part * count : (part + 1) * count, :] = picked[:, part * 128 : (part + 1) * 128]
    hot_two = slot_onehot(shift_two[...], -H2, 1, 2 * H2)
    onehot_two = jnp.where(hot_two, 1.0, 0.0)
    picked = dot(onehot_two.astype(jnp.bfloat16), table_two[...]).astype(jnp.bfloat16)
    left_two[:count, :128] = picked[:, :128]
    left_two[:count, 128:] = picked[:, :128]
    left_two[count:, :128] = picked[:, 128:]
    left_two[count:, 128:] = jnp.zeros((count, 128), jnp.bfloat16)
    part_two = jnp.sum(
        jnp.where(hot_two, jnp.broadcast_to(fraction_two[...], hot_two.shape), 0.0),
        axis=1, keepdims=True,
    )
    rows = lax.broadcasted_iota(jnp.int32, (count, lanes), 0)
    origin = lax.broadcasted_iota(jnp.int32, (count, lanes), 1) - (lax.rem(rows, 2 * H2) - H2)
    weight_near[...] = jnp.where((origin >= 0) & (origin < lanes), 1.0 - part_two, 0.0)
    weight_far[...] = jnp.where((origin >= 1) & (origin <= lanes), part_two, 0.0)

    chunk = 2 * count * 8

    def first(block, carry):
        pltpu.make_async_copy(
            source.at[pl.ds(block * lines, lines)],
            received.at[pl.ds(block * lines, lines)],
            load_sem.at[block],
        ).wait()
        for index in range(8):
            group, own = block * (8 // local) + index // local, index % local
            columns = []
            for row in range(2):
                blocks = [
                    received[place_in_line(pair, group), own, part, row]
                    for pair in range(pairs)
                    for part in range(2)
                ]
                columns.append(jnp.concatenate(blocks, axis=0))
            both = dot(left_one[...], jnp.concatenate(columns, axis=1))
            both = both[: 2 * count] + both[2 * count :]
            start = pl.multiple_of(block * chunk, chunk) + index
            for row in range(2):
                middle[row, pl.ds(start, 2 * count, stride=8), :] = both[
                    :, row * lanes : (row + 1) * lanes
                ]
        return carry

    lax.fori_loop(0, count // 8, first, 0)

    targets = (up_near, up_far, down_near, down_far)
    stores = [
        pltpu.make_async_copy(
            stage.at[value % 2], out.at[pl.ds(value * PER_SHIFT, PER_SHIFT)], store_sem.at[value]
        )
        for value in range(2 * H)
    ]
    for value in range(2 * H):
        if value >= 2:
            stores[value - 2].wait()

        def second(item, carry):
            slot = value * PER_SHIFT + item
            columns = []
            for row in range(2):
                parts = [
                    middle[row, pl.ds(pl.multiple_of(block * chunk + (part * count + slot) * 8, 8), 8), :]
                    for part in range(2)
                    for block in range(count // 8)
                ]
                columns.append(jnp.concatenate(parts, axis=0))
            both = dot(
                left_two[...],
                jnp.concatenate(split(jnp.concatenate(columns, axis=1)), axis=0),
            )
            both = both[:count] + both[count:]
            for row in range(2):
                pieces = []
                for block in range(count // 8):
                    piece = both[block * 8 : block * 8 + 8, row * lanes : (row + 1) * lanes]
                    base = (lanes - H2 + 8 * (block % (2 * H2 // 8))) % lanes
                    near = pltpu.roll(piece, base, 1, stride=1, stride_axis=0)
                    far = pltpu.roll(near, 1, 1)
                    span = slice(block * 8, block * 8 + 8)
                    pieces.append(near * weight_near[span, :] + far * weight_far[span, :])
                moved = jnp.concatenate(pieces, axis=0)
                stage[value % 2, item, row] = moved
                hits = [
                    (kind, wanted.index((value, row)))
                    for kind, wanted in enumerate(HALOS)
                    if (value, row) in wanted
                ]
                if hits:
                    codes, scale = encode(moved)
                for kind, index in hits:
                    place = index * PER_SHIFT + item
                    start = pl.multiple_of(place * count, count)
                    targets[kind][pl.ds(start, count), :] = codes
                    scales[kind, pl.ds(place, 1), :] = scale
            return carry

        lax.fori_loop(0, PER_SHIFT, second, 0, unroll=4)
        stores[value].start()
    for kind, target in enumerate(targets):
        entries = target.shape[0] // (count + 1)
        target[entries * count :, :] = scales[kind, :entries, :].astype(jnp.int32).astype(jnp.int16)
    for store in stores[-2:]:
        store.wait()


def scatter_table_kernel(shift_two, kernel, table, rows):
    count = kernel.shape[1]
    reach = kernel.shape[0]
    offsets = lax.broadcasted_iota(jnp.int32, kernel.shape, 0)
    lags = lax.broadcasted_iota(jnp.int32, kernel.shape, 1)
    full = kernel[...] + jnp.where((offsets == R) & (lags == 0), 1.0, 0.0)
    high, low = split(full)
    lag = lax.broadcasted_iota(jnp.int32, (count, 2 * count), 0)
    lane = lax.broadcasted_iota(jnp.int32, (count, 2 * count), 1)
    mirror = jnp.where(lax.rem(lag + lane, count) == 0, 1.0, 0.0).astype(jnp.bfloat16)
    rows[...] = jnp.zeros(rows.shape, jnp.float32)
    rows[0, 3 : 3 + reach, :] = dot(high, mirror)
    rows[1, 3 : 3 + reach, :] = dot(low, mirror)
    onehot = jnp.where(slot_onehot(shift_two[...], -H2, 1, 2 * H2), 1.0, 0.0).T
    blank = jnp.zeros((count, count), jnp.float32)
    choose = jnp.concatenate(
        [jnp.concatenate([onehot, blank], axis=1), jnp.concatenate([blank, onehot], axis=1)], axis=0
    ).astype(jnp.bfloat16)
    left = lane < count

    def circulant(part, index):
        row = jnp.broadcast_to(rows[part, index : index + 1, :], (8, 2 * count))
        return jnp.concatenate(
            [pltpu.roll(row, 8 * block, 1, stride=1, stride_axis=0) for block in range(count // 8)],
            axis=0,
        )

    for part in range(2):
        here = circulant(part, 0)
        for index in range(reach + 5):
            there = circulant(part, index + 1)
            pair = dot(jnp.where(left, here, there).astype(jnp.bfloat16), choose)
            pair = pair.astype(jnp.bfloat16)
            here = there
            for band in range(4):
                if (index - 3 + band) % 2 == 0 and 0 <= (index - 3 + band) // 2 < 10:
                    column = (index - 3 + band) // 2 * 128
                    start = part * 256 + band * count
                    table[start : start + count, column : column + 128] = pair


def scatter_pair(index, first_group, table, high, low, out, scales):
    start = pl.multiple_of((first_group + index * 2) * 256, 256)

    def window(half):
        return jnp.concatenate(
            [half[pl.ds(start, 1280), :], half[pl.ds(start + 256, 1280), :]], axis=1
        )

    both = dot(table[...], window(high))
    rest = dot(table[:256, :], window(low))
    total = both[:256] + both[256:] + rest
    for member in range(2):
        target = pl.multiple_of((index * 2 + member) * 256, 256)
        for row in range(2):
            column = member * 256 + row * 128
            part = total[:, column : column + 128]
            blocks = [encode(part[band * 64 : band * 64 + 64]) for band in range(4)]
            out[row, pl.ds(target, 256), :] = jnp.concatenate(
                [codes for codes, _ in blocks], axis=0
            )
            for band in range(4):
                scales[row, pl.ds((index * 2 + member) * 4 + band, 1), :] = blocks[band][1]


def scatter_groups(first_group, groups, table, high, low, out, scales):
    def step(index, carry):
        scatter_pair(index, first_group, table, high, low, out, scales)
        return carry

    lax.fori_loop(0, groups // 2, step, 0)


def shear_kernel(
    shift_one, fraction_one, table_source, source, up_near, up_far, down_near, down_far,
    high_out, low_out, out, order, seen, arrived, sent, table, moved, high, low, sem, load_sem,
):
    count = moved.shape[0]
    loads = [
        pltpu.make_async_copy(
            source.at[pl.ds(value * PER_SHIFT, PER_SHIFT)],
            moved.at[pl.ds(value * PER_SHIFT, PER_SHIFT)],
            load_sem.at[value],
        )
        for value in range(2 * H)
    ]
    table_load = pltpu.make_async_copy(table_source, table, sem.at[0])
    for load in loads:
        load.start()
    table_load.start()
    for value in range(2 * H):
        seen[value] = 0

    def place(band, carry):
        value = shift_one[band] + H
        repeat = seen[value]
        order[value * PER_SHIFT + repeat] = band
        seen[value] = repeat + 1
        return carry

    lax.fori_loop(0, count, place, 0)
    sources = (up_near, up_far, down_near, down_far)
    for kind, source in enumerate(sources):
        entries = source.shape[0] // (count + 1)
        codes = source[entries * count :, :].astype(jnp.int32)
        arrived[kind, :entries, :] = codes.astype(jnp.float32)

    def fetch(value, item, row):
        if row in (0, 1):
            return moved[value * PER_SHIFT + item, row]
        if row < 0:
            kind, key = (0, (value, row + 2)) if row >= -2 else (1, (value, row + 4))
        else:
            kind, key = (2, (value, row - 2)) if row <= 3 else (3, (value, row - 4))
        place = HALOS[kind].index(key) * PER_SHIFT + item
        start = pl.multiple_of(place * count, count)
        return decode(sources[kind][pl.ds(start, count), :], arrived[kind, pl.ds(place, 1), :])

    for value in range(2 * H):
        shift = value - H
        loads[value].wait()

        def shear(item, carry):
            band = order[value * PER_SHIFT + item]
            weight = fraction_one[band]
            need = {
                row: fetch(value, item, row)
                for row in (-shift - 1, -shift, 1 - shift)
            }
            full = jnp.concatenate(
                [
                    (1.0 - weight) * need[row - shift] + weight * need[row - shift - 1]
                    for row in range(2)
                ],
                axis=1,
            )
            top, bottom = split(full)

            def put(index):
                start = pl.multiple_of(index * count, count)
                high[pl.ds(start, count), :] = top
                low[pl.ds(start, count), :] = bottom

            put(band + R)

            @pl.when(band < R)
            def _():
                put(band + R + count)

            @pl.when(band >= count - R)
            def _():
                put(band + R - count)

            return carry

        lax.fori_loop(0, PER_SHIFT, shear, 0)
    half = count // 8
    side = lax.axis_index("dir")
    first_row = pl.multiple_of(side * (half * 4 * count), half * 4 * count)
    kept = high_out.shape[0]
    keeps = [
        pltpu.make_async_copy(held.at[pl.ds(first_row, kept)], target, sem.at[index + 1])
        for index, (held, target) in enumerate(((high, high_out), (low, low_out)))
    ]
    for keep in keeps:
        keep.start()
    table_load.wait()
    scatter_groups((1 - side) * half, half, table, high, low, out, sent)
    code_scales(out, sent, 4 * half * count)
    for keep in keeps:
        keep.wait()


def code_scales(out, sent, size):
    for row in range(2):
        out[row, size:, :] = sent[row].astype(jnp.int32).astype(jnp.int16)


def scatter_kernel_own(table_source, high_source, low_source, out, sent, table, high, low, sem):
    half = high.shape[0] // 64 - 2 * R
    table_load = pltpu.make_async_copy(table_source, table, sem.at[0])
    table_load.start()
    loads = []
    for index in range(half // 8):
        begin, end = (0, 1536) if index == 0 else (1024 + index * 512, 1536 + index * 512)
        for part, (held, target) in enumerate(((high_source, high), (low_source, low))):
            load = pltpu.make_async_copy(
                held.at[pl.ds(begin, end - begin)],
                target.at[pl.ds(begin, end - begin)],
                sem.at[1 + index * 2 + part],
            )
            load.start()
            loads.append(load)
    table_load.wait()
    for index in range(half // 8):
        loads[2 * index].wait()
        loads[2 * index + 1].wait()
        scatter_pair(index, 0, table, high, low, out, sent)
    code_scales(out, sent, half // 2 * 64 * 2)


def merge_kernel(*refs):
    pieces, out, codes, scales, stage, load_sem, store_sem = refs[:4], *refs[4:]
    bands = scales.shape[1]
    size = bands * 64
    steps = store_sem.shape[0]
    width = size // steps
    block = lax.axis_index("pos")
    core = lax.rem(block, 2)
    held_here = lax.rem(lax.axis_index("dir") + lax.div(block, 2) + core, 2) == 0

    def load(piece, slot):
        for row in range(2):
            pltpu.make_async_copy(piece.at[row], codes.at[slot, row], load_sem.at[slot, row]).start()

    @pl.when(held_here)
    def _():
        load(pieces[0], 0)
        load(pieces[1], 1)

    @pl.when(jnp.logical_not(held_here))
    def _():
        load(pieces[2], 0)
        load(pieces[3], 1)

    for slot in range(2):
        for row in range(2):
            arrived = pltpu.make_async_copy(
                pieces[0].at[row], codes.at[slot, row], load_sem.at[slot, row]
            )
            arrived.wait()
            scale = codes[slot, row, size : size + bands, :].astype(jnp.int32)
            scales[slot * 2 + row] = scale.astype(jnp.float32)
    stores = [
        pltpu.make_async_copy(
            stage.at[pl.ds(step * width * 4, width * 4)],
            out.at[pl.ds(step * width * 4, width * 4)],
            store_sem.at[step],
        )
        for step in range(steps)
    ]
    for side in range(2):

        @pl.when(core == side)
        def _():
            for step in range(steps):
                for slot in range(2):
                    pair = side if slot == 0 else 1 - side
                    for row in range(2):
                        for band in range(step * width // 64, (step + 1) * width // 64):
                            rows = codes[slot, row, band * 64 : band * 64 + 64, :]
                            value = decode(rows, scales[slot * 2 + row, band : band + 1, :])
                            stage[pl.ds(2 * pair + row + band * 256, 64, stride=4), :] = value
                stores[step].start()

    for store in stores:
        store.wait()


def vmem(number):
    return [pl.BlockSpec(memory_space=VMEM)] * number


def anywhere(number):
    return [pl.BlockSpec(memory_space=pl.ANY)] * number


def smem(number):
    return [pl.BlockSpec(memory_space=SMEM)] * number


def fast_body(coherence, shift_first, fraction_first, shift_second, fraction_second, scatter_kernel):
    f32, bf16 = jnp.float32, jnp.bfloat16
    shape = jax.ShapeDtypeStruct
    pairs, places = lax.axis_size("dir"), lax.axis_size("pos")
    parts, own_first, own_second, _, lanes = coherence.shape
    bands = own_first * pairs
    total = pairs * places
    cut = coherence.reshape(parts, own_first, own_second, total, 2, lanes)
    cut = cut.transpose(3, 2, 0, 4, 1, 5)
    received = lax.all_to_all(
        cut, ("dir", "pos"), split_axis=0, concat_axis=0, tiled=True,
        axis_index_groups=[[device_of(line, places) for line in range(total)]],
    )

    row_one, row_two = shift_first.reshape(1, bands), shift_second.reshape(1, bands)
    halo_shapes = [shape((len(one) * PER_SHIFT * (bands + 1), lanes), jnp.int16) for one in HALOS]
    moved, *halos = pl.pallas_call(
        functools.partial(transform_kernel, pairs),
        out_shape=[shape((bands, 2, bands, lanes), f32)] + halo_shapes,
        in_specs=vmem(5) + [pl.BlockSpec(memory_space=pl.ANY)],
        out_specs=[pl.BlockSpec(memory_space=pl.ANY)] + vmem(4),
        scratch_shapes=[
            VMEM((4 * bands, 2 * bands), bf16),
            VMEM((2 * bands, 4 * bands), bf16),
            VMEM((bands, lanes), f32),
            VMEM((bands, lanes), f32),
            VMEM((2, 2 * bands * bands, lanes), f32),
            VMEM((4, len(UP_NEAR) * PER_SHIFT, lanes), f32),
            VMEM(received.shape, bf16),
            VMEM((2, PER_SHIFT, 2, bands, lanes), f32),
            pltpu.SemaphoreType.DMA((bands // 8,)),
            pltpu.SemaphoreType.DMA((2 * H,)),
        ],
        name="transform",
    )(
        row_one, row_two, fraction_second.reshape(1, bands),
        jnp.asarray(first_tables(bands, pairs)), jnp.asarray(second_tables(bands)), received,
    )

    def place(line):
        return device_of(line, places)

    arrived = []
    for halo, step in zip(halos, (1, 2, -1, -2)):
        hops = [(place(b), place(b + step)) for b in range(total) if 0 <= b + step < total]
        arrived.append(lax.ppermute(halo, ("dir", "pos"), hops))

    table = pl.pallas_call(
        scatter_table_kernel,
        out_shape=shape((512, 1280), bf16),
        in_specs=vmem(2),
        out_specs=pl.BlockSpec(memory_space=VMEM),
        scratch_shapes=[VMEM((2, 32, 2 * bands), f32)],
        name="scatter_table",
    )(row_two, scatter_kernel)

    wrapped = (bands + 2 * R) * bands
    half = bands * bands // 2
    high, low, away = pl.pallas_call(
        shear_kernel,
        out_shape=[shape(((bands // 2 + 2 * R) * bands, 2 * lanes), bf16)] * 2
        + [shape((2, half + bands // 2, lanes), jnp.int16)],
        in_specs=smem(2) + anywhere(2) + vmem(4),
        out_specs=anywhere(2) + vmem(1),
        scratch_shapes=[
            SMEM((bands,), jnp.int32),
            SMEM((2 * H,), jnp.int32),
            VMEM((4, len(UP_NEAR) * PER_SHIFT, lanes), f32),
            VMEM((2, bands // 2, lanes), f32),
            VMEM(table.shape, bf16),
            VMEM(moved.shape, f32),
            VMEM((wrapped, 2 * lanes), bf16),
            VMEM((wrapped, 2 * lanes), bf16),
            pltpu.SemaphoreType.DMA((3,)),
            pltpu.SemaphoreType.DMA((2 * H,)),
        ],
        name="shear",
    )(shift_first, fraction_first, table, moved, *arrived)
    home = [(d, q, c, (d + q) % 2) for d in range(pairs) for q in range(places // 2) for c in range(2)]
    same = [
        (d * places + 2 * q + c, (1 - d) * places + 2 * q + b) for d, q, c, b in home if b == c
    ]
    cross = [
        (d * places + 2 * q + c, (1 - d) * places + 2 * q + b) for d, q, c, b in home if b != c
    ]
    inside = [(d * places + 2 * q + c, d * places + 2 * q + b) for d, q, c, b in home if b != c]
    from_same = lax.ppermute(away, ("dir", "pos"), same)
    from_cross = lax.ppermute(away, ("dir", "pos"), cross)
    own = pl.pallas_call(
        scatter_kernel_own,
        out_shape=shape((2, half + bands // 2, lanes), jnp.int16),
        in_specs=anywhere(3),
        out_specs=pl.BlockSpec(memory_space=VMEM),
        scratch_shapes=[
            VMEM((2, bands // 2, lanes), f32),
            VMEM(table.shape, bf16),
            VMEM(high.shape, bf16),
            VMEM(low.shape, bf16),
            pltpu.SemaphoreType.DMA((9,)),
        ],
        name="scatter",
    )(table, high, low)
    from_inside = lax.ppermute(own, ("dir", "pos"), inside)
    merged = pl.pallas_call(
        merge_kernel,
        out_shape=shape((half * 4, lanes), f32),
        in_specs=anywhere(4),
        out_specs=pl.BlockSpec(memory_space=pl.ANY),
        scratch_shapes=[
            VMEM((2, 2, half + bands // 2, lanes), jnp.int16),
            VMEM((4, bands // 2, lanes), f32),
            VMEM((half * 4, lanes), f32),
            pltpu.SemaphoreType.DMA((2, 2)),
            pltpu.SemaphoreType.DMA((8,)),
        ],
        name="merge",
    )(own, from_inside, from_same, from_cross)
    return merged.reshape(own_first, bands, 4, lanes)


def with_halo(cells, sides, width, closed):
    for axis, dim in sides:
        count = lax.axis_size(axis)
        ends = count if closed else count - 1
        head = lax.slice_in_dim(cells, 0, width, axis=dim)
        tail = lax.slice_in_dim(cells, cells.shape[dim] - width, cells.shape[dim], axis=dim)
        cells = jnp.concatenate(
            [
                lax.ppermute(tail, axis, [(i, (i + 1) % count) for i in range(ends)]),
                cells,
                lax.ppermute(head, axis, [((i + 1) % count, i) for i in range(ends)]),
            ],
            axis=dim,
        )
    return cells


def phase_tables(length):
    counter = jnp.arange(length, dtype=jnp.int32)
    product = counter[:, None] * counter[None, :] % length
    angles = product.astype(jnp.float32) * (2.0 * math.pi / length)
    factor = 1.0 / math.sqrt(length)
    return (jnp.cos(angles) * factor, jnp.sin(angles) * factor)


def contract(pattern, operand_a, operand_b):
    return jnp.einsum(
        pattern,
        operand_a,
        operand_b,
        precision=lax.Precision.HIGHEST,
        preferred_element_type=jnp.float32,
    )


def finish_bands(received):
    cos_one, sin_one = phase_tables(received.shape[1])
    real_part = contract("ts,sbax->tbax", cos_one, received[0]) + contract(
        "ts,sbax->tbax", sin_one, received[1]
    )
    return lax.all_to_all(real_part, "dir", split_axis=0, concat_axis=1, tiled=True)


def shear_block(wigner, shift_first, fraction_first):
    band_count = wigner.shape[0]
    cell_count = wigner.shape[2]
    first_band = lax.axis_index("dir") * band_count
    shifts = lax.dynamic_slice_in_dim(shift_first, first_band, band_count)
    weights = lax.dynamic_slice_in_dim(fraction_first, first_band, band_count)
    padded = with_halo(wigner, (("pos", 2),), H, False)
    rows_out = jnp.arange(cell_count, dtype=jnp.int32)
    rows_in = jnp.arange(cell_count + 2 * H, dtype=jnp.int32)
    target = rows_out[None, :, None] + H - shifts[:, None, None]
    near_tap = (rows_in[None, None, :] == target).astype(jnp.float32)
    far_tap = (rows_in[None, None, :] == target - 1).astype(jnp.float32)
    band_matrix = (1.0 - weights)[:, None, None] * near_tap + weights[:, None, None] * far_tap
    return contract("kaj,kbjx->kbax", band_matrix, padded)


def convolve(circulant, source, out_rows):
    summed = jnp.zeros((out_rows,) + source.shape[1:], jnp.float32)
    for offset in range(circulant.shape[0]):
        summed = summed + contract(
            "ij,kjax->kiax", circulant[offset], source[offset : offset + out_rows]
        )
    return summed


def body(coherence, shift_first, fraction_first, shift_second, fraction_second, scatter_kernel):
    direction_count = coherence.shape[2] * lax.axis_size("pos")
    cos_two, sin_two = phase_tables(direction_count)
    cell_block = lax.all_to_all(coherence, "pos", split_axis=3, concat_axis=2, tiled=True)
    real_in = cell_block[0].astype(jnp.float32)
    imag_in = cell_block[1].astype(jnp.float32)
    real_mid = contract("ts,bsax->btax", cos_two, real_in) + contract(
        "ts,bsax->btax", sin_two, imag_in
    )
    imag_mid = contract("ts,bsax->btax", cos_two, imag_in) - contract(
        "ts,bsax->btax", sin_two, real_in
    )
    mixed = jnp.stack([real_mid, imag_mid])
    wigner = finish_bands(lax.all_to_all(mixed, "dir", split_axis=2, concat_axis=1, tiled=True))
    moved_one = shear_block(wigner, shift_first, fraction_first)
    band_count = moved_one.shape[0]
    column_count = moved_one.shape[3]
    positions = jnp.arange(column_count, dtype=jnp.int32)
    target_two = positions[None, :, None] - shift_second[:, None, None]
    near_two = (positions[None, None, :] == target_two).astype(jnp.float32)
    far_two = (positions[None, None, :] == target_two - 1).astype(jnp.float32)
    shear_matrix = (1.0 - fraction_second)[:, None, None] * near_two + fraction_second[
        :, None, None
    ] * far_two
    moved_two = contract("bxy,kbay->kbax", shear_matrix, moved_one)
    kernel_positions = jnp.arange(direction_count, dtype=jnp.int32)
    lag_index = (kernel_positions[:, None] - kernel_positions[None, :]) % direction_count
    circulant = scatter_kernel[:, lag_index]
    extended = with_halo(moved_two, (("dir", 0),), R, True)
    summed = moved_two + convolve(circulant, extended, band_count)
    return summed


def fits(mesh, coherence):
    pairs, places = mesh.shape["dir"], mesh.shape["pos"]
    _, first, second, cells, lanes = coherence.shape
    return 4 * places == second and (pairs, first, second, cells, lanes) == (2, 64, 64, 4 * places, 128)


def solution(mesh):
    placed = (P(None, "dir", "pos", None, None), P(), P(), P(), P(), P())

    def run(*arrays):
        fast = fits(mesh, arrays[0])
        step = jax.shard_map(
            fast_body if fast else body,
            mesh=mesh, in_specs=placed, out_specs=P("dir", None, "pos", None), check_vma=False,
        )
        return step(*arrays)

    return run
```

```python
import functools
import math

import jax
import jax.numpy as jnp
import numpy as np
from jax import lax
from jax.experimental import pallas as pl
from jax.experimental.pallas import tpu as pltpu
from jax.sharding import PartitionSpec as P

R = 8
H = 4
H2 = 16

UP_NEAR = ((4, 1), (5, 0), (5, 1), (6, 0), (6, 1), (7, 0))
UP_FAR = ((6, 1), (7, 0), (7, 1))
DOWN_NEAR = ((3, 0), (2, 0), (2, 1), (1, 0), (1, 1), (0, 1))
DOWN_FAR = ((1, 0), (0, 0), (0, 1))
HALOS = (UP_NEAR, UP_FAR, DOWN_NEAR, DOWN_FAR)
PER_SHIFT = 8
TOP = 32600.0
FINE = 8.0
LEAST = 1e-30
VMEM = pltpu.VMEM
SMEM = pltpu.SMEM


def split_np(table):
    high = table.astype(jnp.bfloat16)
    low = (table - high.astype(np.float32)).astype(jnp.bfloat16)
    return high, low


def split(value):
    high = value.astype(jnp.bfloat16)
    low = (value - high.astype(jnp.float32)).astype(jnp.bfloat16)
    return high, low


def natural_tables(length):
    counter = np.arange(length)
    angles = (counter[:, None] * counter[None, :] % length) * (2.0 * math.pi / length)
    factor = 1.0 / math.sqrt(length)
    return np.cos(angles) * factor, np.sin(angles) * factor


def first_tables(length, cuts):
    cos, sin = natural_tables(length)
    width = length // cuts
    real, imag = [], []
    for cut in range(cuts):
        cols = slice(cut * width, (cut + 1) * width)
        real += [cos[:, cols], sin[:, cols]]
        imag += [-sin[:, cols], cos[:, cols]]
    table = np.repeat(np.concatenate(real + imag, axis=1), 2, axis=1).astype(np.float32)
    return np.concatenate(split_np(table), axis=1)


def second_tables(length):
    cos, sin = natural_tables(length)
    table = np.concatenate([cos, sin], axis=1).astype(np.float32)
    return np.concatenate(split_np(table), axis=1)


def slot_onehot(shift_row, low, stride_shift, stride_repeat, copies=1):
    count = shift_row.shape[1]
    across = jnp.broadcast_to(shift_row, (count, count))
    down = across.astype(jnp.float32).T.astype(jnp.int32)
    first = lax.broadcasted_iota(jnp.int32, (count, count), 0)
    second = lax.broadcasted_iota(jnp.int32, (count, count), 1)
    same = jnp.where((across == down) & (first < second), 1, 0)
    repeat = jnp.sum(same, axis=0, keepdims=True)
    slot = (shift_row - low) * stride_shift + repeat * stride_repeat
    if copies == 2:
        first = lax.broadcasted_iota(jnp.int32, (2 * count, count), 0)
        first = lax.shift_right_logical(first, 1)
    return first == slot


def dot(lhs, rhs):
    return jnp.dot(lhs, rhs, preferred_element_type=jnp.float32)


def place_in_line(pair, block):
    return block // 2 * 4 + (pair + block // 2) % 2 * 2 + block % 2


def device_of(line, places):
    quad, step = line // 4, line % 4
    return (step // 2 + quad) % 2 * places + quad * 2 + step % 2


def deal_kernel(source, out, held, sem):
    taken = lax.broadcasted_iota(jnp.int32, (128, 128), 1)
    given = lax.broadcasted_iota(jnp.int32, (128, 128), 0)
    wanted = lax.rem(lax.div(given, 2), 8) * 16 + lax.div(given, 16) * 2 + lax.rem(given, 2)
    move = jnp.where(taken == wanted, 1.0, 0.0).astype(jnp.bfloat16)
    parts, firsts, seconds, cells, _ = source.shape

    def load(part, group):
        span = pl.ds(group * 8, 8)
        number = part * (firsts // 8) + group
        return pltpu.make_async_copy(source.at[part, span], held.at[part, span], sem.at[number])

    groups = [(part, group) for part in range(parts) for group in range(firsts // 8)]
    for part, group in groups:
        load(part, group).start()
    for part, group in groups:
        load(part, group).wait()

        def second(own, carry):
            for tile in range(0, cells // 16, 2):
                columns = [
                    jnp.concatenate(
                        [
                            held[part, group * 8 + item, own, member * 16 : member * 16 + 16, :]
                            for item in range(8)
                        ],
                        axis=0,
                    )
                    for member in (tile, tile + 1)
                ]
                moved = dot(move, jnp.concatenate(columns, axis=1)).astype(jnp.bfloat16)
                for member in range(2):
                    for item in range(8):
                        out[(tile + member) * 8 + item, own, part, group * 16 : group * 16 + 16, :] = (
                            moved[item * 16 : item * 16 + 16, member * 128 : member * 128 + 128]
                        )
            return carry

        lax.fori_loop(0, seconds, second, 0, unroll=2)


def encode(columns):
    largest = jnp.maximum(jnp.max(jnp.abs(columns), axis=0, keepdims=True), LEAST)
    scale = jnp.ceil(jnp.log2(largest) * FINE)
    codes = jnp.round(columns * (jnp.exp2(scale * (-1.0 / FINE)) * TOP))
    return codes.astype(jnp.int32).astype(jnp.int16), scale


def decode(codes, scale):
    return codes.astype(jnp.int32).astype(jnp.float32) * (jnp.exp2(scale * (1.0 / FINE)) * (1.0 / TOP))


def transform_kernel(
    pairs, shift_one, shift_two, fraction_two, table_one, table_two, source,
    out, up_near, up_far, down_near, down_far, left_one, left_two, weight_near, weight_far, middle, scales,
    received, stage, load_sem, store_sem,
):
    count = 64
    lanes = out.shape[-1]
    local = received.shape[1]
    lines = received.shape[0] // (count // 8)
    loads = [
        pltpu.make_async_copy(
            source.at[pl.ds(block * lines, lines)],
            received.at[pl.ds(block * lines, lines)],
            load_sem.at[block],
        )
        for block in range(count // 8)
    ]
    for load in loads:
        load.start()
    onehot_one = jnp.where(slot_onehot(shift_one[...], -H, PER_SHIFT, 1, copies=2), 1.0, 0.0)
    picked = dot(onehot_one.astype(jnp.bfloat16), table_one[...])
    same_row = lax.rem(
        lax.broadcasted_iota(jnp.int32, picked.shape, 0)
        + lax.broadcasted_iota(jnp.int32, picked.shape, 1),
        2,
    )
    picked = jnp.where(same_row == 0, picked, 0.0).astype(jnp.bfloat16)
    for part in range(4):
        left_one[part * 2 * count : (part + 1) * 2 * count, :] = picked[
            :, part * 4 * count : (part + 1) * 4 * count
        ]
    hot_two = slot_onehot(shift_two[...], -H2, 1, 2 * H2)
    onehot_two = jnp.where(hot_two, 1.0, 0.0)
    picked = dot(onehot_two.astype(jnp.bfloat16), table_two[...]).astype(jnp.bfloat16)
    left_two[:count, :128] = picked[:, :128]
    left_two[:count, 128:] = picked[:, :128]
    left_two[count:, :128] = picked[:, 128:]
    left_two[count:, 128:] = jnp.zeros((count, 128), jnp.bfloat16)
    part_two = jnp.sum(
        jnp.where(hot_two, jnp.broadcast_to(fraction_two[...], hot_two.shape), 0.0),
        axis=1, keepdims=True,
    )
    rows = lax.broadcasted_iota(jnp.int32, (count, lanes), 0)
    origin = lax.broadcasted_iota(jnp.int32, (count, lanes), 1) - (lax.rem(rows, 2 * H2) - H2)
    weight_near[...] = jnp.where((origin >= 0) & (origin < lanes), 1.0 - part_two, 0.0)
    weight_far[...] = jnp.where((origin >= 1) & (origin <= lanes), part_two, 0.0)

    chunk = 2 * count * 2 * 8

    def first(block, carry):
        pltpu.make_async_copy(
            source.at[pl.ds(block * lines, lines)],
            received.at[pl.ds(block * lines, lines)],
            load_sem.at[block],
        ).wait()
        for index in range(0, 8, 2):
            columns = []
            for member in (index, index + 1):
                group, own = block * (8 // local) + member // local, member % local
                blocks = [
                    received[place_in_line(pair, group), own, part]
                    for pair in range(pairs)
                    for part in range(2)
                ]
                columns.append(jnp.concatenate(blocks, axis=0))
            both = dot(left_one[...], jnp.concatenate(columns, axis=1))
            both = both[: 4 * count] + both[4 * count :]
            for member in range(2):
                start = pl.multiple_of(block * chunk, chunk) + index + member
                middle[pl.ds(start, 4 * count, stride=8), :] = both[
                    :, member * lanes : (member + 1) * lanes
                ]
        return carry

    lax.fori_loop(0, count // 8, first, 0)

    targets = (up_near, up_far, down_near, down_far)
    stores = [
        pltpu.make_async_copy(
            stage.at[value % 2], out.at[pl.ds(value * PER_SHIFT, PER_SHIFT)], store_sem.at[value]
        )
        for value in range(2 * H)
    ]
    for value in range(2 * H):
        if value >= 2:
            stores[value - 2].wait()

        def second(item, carry):
            slot = value * PER_SHIFT + item
            columns = []
            for row in range(2):
                parts = [
                    middle[
                        pl.ds(
                            pl.multiple_of(block * chunk + ((part * count + slot) * 2 + row) * 8, 8), 8
                        ),
                        :,
                    ]
                    for part in range(2)
                    for block in range(count // 8)
                ]
                columns.append(jnp.concatenate(parts, axis=0))
            both = dot(
                left_two[...],
                jnp.concatenate(split(jnp.concatenate(columns, axis=1)), axis=0),
            )
            both = both[:count] + both[count:]
            for row in range(2):
                pieces = []
                for block in range(count // 8):
                    piece = both[block * 8 : block * 8 + 8, row * lanes : (row + 1) * lanes]
                    base = (lanes - H2 + 8 * (block % (2 * H2 // 8))) % lanes
                    near = pltpu.roll(piece, base, 1, stride=1, stride_axis=0)
                    far = pltpu.roll(near, 1, 1)
                    span = slice(block * 8, block * 8 + 8)
                    pieces.append(near * weight_near[span, :] + far * weight_far[span, :])
                moved = jnp.concatenate(pieces, axis=0)
                stage[value % 2, item, row] = moved
                hits = [
                    (kind, wanted.index((value, row)))
                    for kind, wanted in enumerate(HALOS)
                    if (value, row) in wanted
                ]
                if hits:
                    codes, scale = encode(moved)
                for kind, index in hits:
                    place = index * PER_SHIFT + item
                    start = pl.multiple_of(place * count, count)
                    targets[kind][pl.ds(start, count), :] = codes
                    scales[kind, pl.ds(place, 1), :] = scale
            return carry

        lax.fori_loop(0, PER_SHIFT, second, 0, unroll=4)
        stores[value].start()
    for kind, target in enumerate(targets):
        entries = target.shape[0] // (count + 1)
        target[entries * count :, :] = scales[kind, :entries, :].astype(jnp.int32).astype(jnp.int16)
    for store in stores[-2:]:
        store.wait()


def scatter_table_kernel(shift_two, kernel, table, rows):
    count = kernel.shape[1]
    reach = kernel.shape[0]
    offsets = lax.broadcasted_iota(jnp.int32, kernel.shape, 0)
    lags = lax.broadcasted_iota(jnp.int32, kernel.shape, 1)
    full = kernel[...] + jnp.where((offsets == R) & (lags == 0), 1.0, 0.0)
    high, low = split(full)
    lag = lax.broadcasted_iota(jnp.int32, (count, 2 * count), 0)
    lane = lax.broadcasted_iota(jnp.int32, (count, 2 * count), 1)
    mirror = jnp.where(lax.rem(lag + lane, count) == 0, 1.0, 0.0).astype(jnp.bfloat16)
    rows[...] = jnp.zeros(rows.shape, jnp.float32)
    rows[0, 3 : 3 + reach, :] = dot(high, mirror)
    rows[1, 3 : 3 + reach, :] = dot(low, mirror)
    onehot = jnp.where(slot_onehot(shift_two[...], -H2, 1, 2 * H2), 1.0, 0.0).T
    blank = jnp.zeros((count, count), jnp.float32)
    choose = jnp.concatenate(
        [jnp.concatenate([onehot, blank], axis=1), jnp.concatenate([blank, onehot], axis=1)], axis=0
    ).astype(jnp.bfloat16)
    left = lane < count

    def circulant(part, index):
        row = jnp.broadcast_to(rows[part, index : index + 1, :], (8, 2 * count))
        return jnp.concatenate(
            [pltpu.roll(row, 8 * block, 1, stride=1, stride_axis=0) for block in range(count // 8)],
            axis=0,
        )

    for part in range(2):
        here = circulant(part, 0)
        for index in range(reach + 5):
            there = circulant(part, index + 1)
            pair = dot(jnp.where(left, here, there).astype(jnp.bfloat16), choose)
            pair = pair.astype(jnp.bfloat16)
            here = there
            for band in range(4):
                if (index - 3 + band) % 2 == 0 and 0 <= (index - 3 + band) // 2 < 10:
                    column = (index - 3 + band) // 2 * 128
                    start = part * 256 + band * count
                    table[start : start + count, column : column + 128] = pair


def scatter_pair(index, first_group, table, high, low, out, scales):
    start = pl.multiple_of((first_group + index * 2) * 256, 256)

    def window(half):
        return jnp.concatenate(
            [half[pl.ds(start, 1280), :], half[pl.ds(start + 256, 1280), :]], axis=1
        )

    both = dot(table[...], window(high))
    rest = dot(table[:256, :], window(low))
    total = both[:256] + both[256:] + rest
    for member in range(2):
        target = pl.multiple_of((index * 2 + member) * 256, 256)
        for row in range(2):
            column = member * 256 + row * 128
            part = total[:, column : column + 128]
            blocks = [encode(part[band * 64 : band * 64 + 64]) for band in range(4)]
            out[row, pl.ds(target, 256), :] = jnp.concatenate(
                [codes for codes, _ in blocks], axis=0
            )
            for band in range(4):
                scales[row, pl.ds((index * 2 + member) * 4 + band, 1), :] = blocks[band][1]


def scatter_groups(first_group, groups, table, high, low, out, scales):
    def step(index, carry):
        scatter_pair(index, first_group, table, high, low, out, scales)
        return carry

    lax.fori_loop(0, groups // 2, step, 0)


def shear_kernel(
    shift_one, fraction_one, table_source, source, up_near, up_far, down_near, down_far,
    high_out, low_out, out, order, seen, arrived, sent, table, moved, high, low, sem, load_sem,
):
    count = moved.shape[0]
    loads = [
        pltpu.make_async_copy(
            source.at[pl.ds(value * PER_SHIFT, PER_SHIFT)],
            moved.at[pl.ds(value * PER_SHIFT, PER_SHIFT)],
            load_sem.at[value],
        )
        for value in range(2 * H)
    ]
    table_load = pltpu.make_async_copy(table_source, table, sem.at[0])
    for load in loads:
        load.start()
    table_load.start()
    for value in range(2 * H):
        seen[value] = 0

    def place(band, carry):
        value = shift_one[band] + H
        repeat = seen[value]
        order[value * PER_SHIFT + repeat] = band
        seen[value] = repeat + 1
        return carry

    lax.fori_loop(0, count, place, 0)
    sources = (up_near, up_far, down_near, down_far)
    for kind, source in enumerate(sources):
        entries = source.shape[0] // (count + 1)
        codes = source[entries * count :, :].astype(jnp.int32)
        arrived[kind, :entries, :] = codes.astype(jnp.float32)

    def fetch(value, item, row):
        if row in (0, 1):
            return moved[value * PER_SHIFT + item, row]
        if row < 0:
            kind, key = (0, (value, row + 2)) if row >= -2 else (1, (value, row + 4))
        else:
            kind, key = (2, (value, row - 2)) if row <= 3 else (3, (value, row - 4))
        place = HALOS[kind].index(key) * PER_SHIFT + item
        start = pl.multiple_of(place * count, count)
        return decode(sources[kind][pl.ds(start, count), :], arrived[kind, pl.ds(place, 1), :])

    for value in range(2 * H):
        shift = value - H
        loads[value].wait()

        def shear(item, carry):
            band = order[value * PER_SHIFT + item]
            weight = fraction_one[band]
            need = {
                row: fetch(value, item, row)
                for row in (-shift - 1, -shift, 1 - shift)
            }
            full = jnp.concatenate(
                [
                    (1.0 - weight) * need[row - shift] + weight * need[row - shift - 1]
                    for row in range(2)
                ],
                axis=1,
            )
            top, bottom = split(full)

            def put(index):
                start = pl.multiple_of(index * count, count)
                high[pl.ds(start, count), :] = top
                low[pl.ds(start, count), :] = bottom

            put(band + R)

            @pl.when(band < R)
            def _():
                put(band + R + count)

            @pl.when(band >= count - R)
            def _():
                put(band + R - count)

            return carry

        lax.fori_loop(0, PER_SHIFT, shear, 0)
    half = count // 8
    side = lax.axis_index("dir")
    first_row = pl.multiple_of(side * (half * 4 * count), half * 4 * count)
    kept = high_out.shape[0]
    keeps = [
        pltpu.make_async_copy(held.at[pl.ds(first_row, kept)], target, sem.at[index + 1])
        for index, (held, target) in enumerate(((high, high_out), (low, low_out)))
    ]
    for keep in keeps:
        keep.start()
    table_load.wait()
    scatter_groups((1 - side) * half, half, table, high, low, out, sent)
    code_scales(out, sent, 4 * half * count)
    for keep in keeps:
        keep.wait()


def code_scales(out, sent, size):
    for row in range(2):
        out[row, size:, :] = sent[row].astype(jnp.int32).astype(jnp.int16)


def scatter_kernel_own(table_source, high_source, low_source, out, sent, table, high, low, sem):
    half = high.shape[0] // 64 - 2 * R
    table_load = pltpu.make_async_copy(table_source, table, sem.at[0])
    table_load.start()
    loads = []
    for index in range(half // 8):
        begin, end = (0, 1536) if index == 0 else (1024 + index * 512, 1536 + index * 512)
        for part, (held, target) in enumerate(((high_source, high), (low_source, low))):
            load = pltpu.make_async_copy(
                held.at[pl.ds(begin, end - begin)],
                target.at[pl.ds(begin, end - begin)],
                sem.at[1 + index * 2 + part],
            )
            load.start()
            loads.append(load)
    table_load.wait()
    for index in range(half // 8):
        loads[2 * index].wait()
        loads[2 * index + 1].wait()
        scatter_pair(index, 0, table, high, low, out, sent)
    code_scales(out, sent, half // 2 * 64 * 2)


def merge_kernel(*refs):
    pieces, out, scales, stage, store_sem = refs[:4], *refs[4:]
    bands = scales.shape[1]
    size = bands * 64
    steps = store_sem.shape[0]
    width = size // steps
    block = lax.axis_index("pos")
    core = lax.rem(block, 2)
    held_here = lax.rem(lax.axis_index("dir") + lax.div(block, 2) + core, 2) == 0
    stores = [
        pltpu.make_async_copy(
            stage.at[pl.ds(step * width * 4, width * 4)],
            out.at[pl.ds(step * width * 4, width * 4)],
            store_sem.at[step],
        )
        for step in range(steps)
    ]
    for side in range(2):
        for here in range(2):
            used = pieces[:2] if here else pieces[2:]

            @pl.when((core == side) & (held_here == (here == 1)))
            def _():
                for slot in range(2):
                    for row in range(2):
                        scale = used[slot][row, size : size + bands, :].astype(jnp.int32)
                        scales[slot * 2 + row] = scale.astype(jnp.float32)
                for step in range(steps):
                    for slot in range(2):
                        pair = side if slot == 0 else 1 - side
                        for row in range(2):
                            for band in range(step * width // 64, (step + 1) * width // 64):
                                rows = used[slot][row, band * 64 : band * 64 + 64, :]
                                value = decode(rows, scales[slot * 2 + row, band : band + 1, :])
                                stage[pl.ds(2 * pair + row + band * 256, 64, stride=4), :] = value
                    stores[step].start()

    for store in stores:
        store.wait()


def vmem(number):
    return [pl.BlockSpec(memory_space=VMEM)] * number


def grant(mebibytes):
    return pltpu.CompilerParams(vmem_limit_bytes=mebibytes << 20)


def in_vmem(value):
    return pltpu.with_memory_space_constraint(value, VMEM)


def anywhere(number):
    return [pl.BlockSpec(memory_space=pl.ANY)] * number


def smem(number):
    return [pl.BlockSpec(memory_space=SMEM)] * number


def fast_body(coherence, shift_first, fraction_first, shift_second, fraction_second, scatter_kernel):
    f32, bf16 = jnp.float32, jnp.bfloat16
    shape = jax.ShapeDtypeStruct
    pairs, places = lax.axis_size("dir"), lax.axis_size("pos")
    parts, own_first, own_second, _, lanes = coherence.shape
    bands = own_first * pairs
    total = pairs * places
    cut = pl.pallas_call(
        deal_kernel,
        out_shape=shape((total, own_second, parts, own_first * 2, lanes), bf16),
        in_specs=[pl.BlockSpec(memory_space=pltpu.HBM)],
        out_specs=pl.BlockSpec(memory_space=VMEM),
        scratch_shapes=[
            VMEM(coherence.shape, bf16),
            pltpu.SemaphoreType.DMA((parts * own_first // 8,)),
        ],
        compiler_params=grant(16),
        name="deal",
    )(pltpu.with_memory_space_constraint(coherence, pltpu.HBM))
    cut = in_vmem(cut)
    received = lax.all_to_all(
        cut, ("dir", "pos"), split_axis=0, concat_axis=0, tiled=True,
        axis_index_groups=[[device_of(line, places) for line in range(total)]],
    )

    row_one, row_two = shift_first.reshape(1, bands), shift_second.reshape(1, bands)
    halo_shapes = [shape((len(one) * PER_SHIFT * (bands + 1), lanes), jnp.int16) for one in HALOS]
    moved, *halos = pl.pallas_call(
        functools.partial(transform_kernel, pairs),
        out_shape=[shape((bands, 2, bands, lanes), f32)] + halo_shapes,
        in_specs=vmem(5) + [pl.BlockSpec(memory_space=pl.ANY)],
        out_specs=[pl.BlockSpec(memory_space=pl.ANY)] + vmem(4),
        scratch_shapes=[
            VMEM((8 * bands, 4 * bands), bf16),
            VMEM((2 * bands, 4 * bands), bf16),
            VMEM((bands, lanes), f32),
            VMEM((bands, lanes), f32),
            VMEM((4 * bands * bands, lanes), f32),
            VMEM((4, len(UP_NEAR) * PER_SHIFT, lanes), f32),
            VMEM(received.shape, bf16),
            VMEM((2, PER_SHIFT, 2, bands, lanes), f32),
            pltpu.SemaphoreType.DMA((bands // 8,)),
            pltpu.SemaphoreType.DMA((2 * H,)),
        ],
        compiler_params=grant(26),
        name="transform",
    )(
        row_one, row_two, fraction_second.reshape(1, bands),
        jnp.asarray(first_tables(bands, pairs)), jnp.asarray(second_tables(bands)), received,
    )

    def place(line):
        return device_of(line, places)

    arrived = []
    for halo, step in zip(halos, (1, 2, -1, -2)):
        hops = [(place(b), place(b + step)) for b in range(total) if 0 <= b + step < total]
        arrived.append(in_vmem(lax.ppermute(halo, ("dir", "pos"), hops)))

    table = pl.pallas_call(
        scatter_table_kernel,
        out_shape=shape((512, 1280), bf16),
        in_specs=vmem(2),
        out_specs=pl.BlockSpec(memory_space=VMEM),
        scratch_shapes=[VMEM((2, 32, 2 * bands), f32)],
        compiler_params=grant(8),
        name="scatter_table",
    )(row_two, scatter_kernel)

    wrapped = (bands + 2 * R) * bands
    half = bands * bands // 2
    high, low, away = pl.pallas_call(
        shear_kernel,
        out_shape=[shape(((bands // 2 + 2 * R) * bands, 2 * lanes), bf16)] * 2
        + [shape((2, half + bands // 2, lanes), jnp.int16)],
        in_specs=smem(2) + anywhere(2) + vmem(4),
        out_specs=anywhere(2) + vmem(1),
        scratch_shapes=[
            SMEM((bands,), jnp.int32),
            SMEM((2 * H,), jnp.int32),
            VMEM((4, len(UP_NEAR) * PER_SHIFT, lanes), f32),
            VMEM((2, bands // 2, lanes), f32),
            VMEM(table.shape, bf16),
            VMEM(moved.shape, f32),
            VMEM((wrapped, 2 * lanes), bf16),
            VMEM((wrapped, 2 * lanes), bf16),
            pltpu.SemaphoreType.DMA((3,)),
            pltpu.SemaphoreType.DMA((2 * H,)),
        ],
        compiler_params=grant(24),
        name="shear",
    )(shift_first, fraction_first, table, moved, *arrived)
    home = [(d, q, c, (d + q) % 2) for d in range(pairs) for q in range(places // 2) for c in range(2)]
    same = [
        (d * places + 2 * q + c, (1 - d) * places + 2 * q + b) for d, q, c, b in home if b == c
    ]
    cross = [
        (d * places + 2 * q + c, (1 - d) * places + 2 * q + b) for d, q, c, b in home if b != c
    ]
    inside = [(d * places + 2 * q + c, d * places + 2 * q + b) for d, q, c, b in home if b != c]
    from_same = lax.ppermute(away, ("dir", "pos"), same)
    from_cross = lax.ppermute(away, ("dir", "pos"), cross)
    own = pl.pallas_call(
        scatter_kernel_own,
        out_shape=shape((2, half + bands // 2, lanes), jnp.int16),
        in_specs=anywhere(3),
        out_specs=pl.BlockSpec(memory_space=VMEM),
        scratch_shapes=[
            VMEM((2, bands // 2, lanes), f32),
            VMEM(table.shape, bf16),
            VMEM(high.shape, bf16),
            VMEM(low.shape, bf16),
            pltpu.SemaphoreType.DMA((9,)),
        ],
        compiler_params=grant(16),
        name="scatter",
    )(table, high, low)
    from_inside = lax.ppermute(own, ("dir", "pos"), inside)
    pieces = [own] + [in_vmem(piece) for piece in (from_inside, from_same, from_cross)]
    merged = pl.pallas_call(
        merge_kernel,
        out_shape=shape((half * 4, lanes), f32),
        in_specs=vmem(4),
        out_specs=pl.BlockSpec(memory_space=pl.ANY),
        scratch_shapes=[
            VMEM((4, bands // 2, lanes), f32),
            VMEM((half * 4, lanes), f32),
            pltpu.SemaphoreType.DMA((8,)),
        ],
        compiler_params=grant(12),
        name="merge",
    )(*pieces)
    return merged.reshape(own_first, bands, 4, lanes)


def with_halo(cells, sides, width, closed):
    for axis, dim in sides:
        count = lax.axis_size(axis)
        ends = count if closed else count - 1
        head = lax.slice_in_dim(cells, 0, width, axis=dim)
        tail = lax.slice_in_dim(cells, cells.shape[dim] - width, cells.shape[dim], axis=dim)
        cells = jnp.concatenate(
            [
                lax.ppermute(tail, axis, [(i, (i + 1) % count) for i in range(ends)]),
                cells,
                lax.ppermute(head, axis, [((i + 1) % count, i) for i in range(ends)]),
            ],
            axis=dim,
        )
    return cells


def phase_tables(length):
    counter = jnp.arange(length, dtype=jnp.int32)
    product = counter[:, None] * counter[None, :] % length
    angles = product.astype(jnp.float32) * (2.0 * math.pi / length)
    factor = 1.0 / math.sqrt(length)
    return (jnp.cos(angles) * factor, jnp.sin(angles) * factor)


def contract(pattern, operand_a, operand_b):
    return jnp.einsum(
        pattern,
        operand_a,
        operand_b,
        precision=lax.Precision.HIGHEST,
        preferred_element_type=jnp.float32,
    )


def finish_bands(received):
    cos_one, sin_one = phase_tables(received.shape[1])
    real_part = contract("ts,sbax->tbax", cos_one, received[0]) + contract(
        "ts,sbax->tbax", sin_one, received[1]
    )
    return lax.all_to_all(real_part, "dir", split_axis=0, concat_axis=1, tiled=True)


def shear_block(wigner, shift_first, fraction_first):
    band_count = wigner.shape[0]
    cell_count = wigner.shape[2]
    first_band = lax.axis_index("dir") * band_count
    shifts = lax.dynamic_slice_in_dim(shift_first, first_band, band_count)
    weights = lax.dynamic_slice_in_dim(fraction_first, first_band, band_count)
    padded = with_halo(wigner, (("pos", 2),), H, False)
    rows_out = jnp.arange(cell_count, dtype=jnp.int32)
    rows_in = jnp.arange(cell_count + 2 * H, dtype=jnp.int32)
    target = rows_out[None, :, None] + H - shifts[:, None, None]
    near_tap = (rows_in[None, None, :] == target).astype(jnp.float32)
    far_tap = (rows_in[None, None, :] == target - 1).astype(jnp.float32)
    band_matrix = (1.0 - weights)[:, None, None] * near_tap + weights[:, None, None] * far_tap
    return contract("kaj,kbjx->kbax", band_matrix, padded)


def convolve(circulant, source, out_rows):
    summed = jnp.zeros((out_rows,) + source.shape[1:], jnp.float32)
    for offset in range(circulant.shape[0]):
        summed = summed + contract(
            "ij,kjax->kiax", circulant[offset], source[offset : offset + out_rows]
        )
    return summed


def body(coherence, shift_first, fraction_first, shift_second, fraction_second, scatter_kernel):
    direction_count = coherence.shape[2] * lax.axis_size("pos")
    cos_two, sin_two = phase_tables(direction_count)
    cell_block = lax.all_to_all(coherence, "pos", split_axis=3, concat_axis=2, tiled=True)
    real_in = cell_block[0].astype(jnp.float32)
    imag_in = cell_block[1].astype(jnp.float32)
    real_mid = contract("ts,bsax->btax", cos_two, real_in) + contract(
        "ts,bsax->btax", sin_two, imag_in
    )
    imag_mid = contract("ts,bsax->btax", cos_two, imag_in) - contract(
        "ts,bsax->btax", sin_two, real_in
    )
    mixed = jnp.stack([real_mid, imag_mid])
    wigner = finish_bands(lax.all_to_all(mixed, "dir", split_axis=2, concat_axis=1, tiled=True))
    moved_one = shear_block(wigner, shift_first, fraction_first)
    band_count = moved_one.shape[0]
    column_count = moved_one.shape[3]
    positions = jnp.arange(column_count, dtype=jnp.int32)
    target_two = positions[None, :, None] - shift_second[:, None, None]
    near_two = (positions[None, None, :] == target_two).astype(jnp.float32)
    far_two = (positions[None, None, :] == target_two - 1).astype(jnp.float32)
    shear_matrix = (1.0 - fraction_second)[:, None, None] * near_two + fraction_second[
        :, None, None
    ] * far_two
    moved_two = contract("bxy,kbay->kbax", shear_matrix, moved_one)
    kernel_positions = jnp.arange(direction_count, dtype=jnp.int32)
    lag_index = (kernel_positions[:, None] - kernel_positions[None, :]) % direction_count
    circulant = scatter_kernel[:, lag_index]
    extended = with_halo(moved_two, (("dir", 0),), R, True)
    summed = moved_two + convolve(circulant, extended, band_count)
    return summed


def fits(mesh, coherence):
    pairs, places = mesh.shape["dir"], mesh.shape["pos"]
    _, first, second, cells, lanes = coherence.shape
    return 4 * places == second and (pairs, first, second, cells, lanes) == (2, 64, 64, 4 * places, 128)


def solution(mesh):
    placed = (P(None, "dir", "pos", None, None), P(), P(), P(), P(), P())

    def run(*arrays):
        fast = fits(mesh, arrays[0])
        step = jax.shard_map(
            fast_body if fast else body,
            mesh=mesh, in_specs=placed, out_specs=P("dir", None, "pos", None), check_vma=False,
        )
        return step(*arrays)

    return run
```

```python
import functools
import math

import jax
import jax.numpy as jnp
import numpy as np
from jax import lax
from jax.experimental import pallas as pl
from jax.experimental.pallas import tpu as pltpu
from jax.sharding import PartitionSpec as P

R = 8
H = 4
H2 = 16

UP_NEAR = ((4, 1), (5, 0), (5, 1), (6, 0), (6, 1), (7, 0))
UP_FAR = ((6, 1), (7, 0), (7, 1))
DOWN_NEAR = ((3, 0), (2, 0), (2, 1), (1, 0), (1, 1), (0, 1))
DOWN_FAR = ((1, 0), (0, 0), (0, 1))
HALOS = (UP_NEAR, UP_FAR, DOWN_NEAR, DOWN_FAR)
PER_SHIFT = 8
TOP = 32600.0
FINE = 8.0
LEAST = 1e-30
VMEM = pltpu.VMEM
SMEM = pltpu.SMEM


def split_np(table):
    high = table.astype(jnp.bfloat16)
    low = (table - high.astype(np.float32)).astype(jnp.bfloat16)
    return high, low


def split(value):
    high = value.astype(jnp.bfloat16)
    low = (value - high.astype(jnp.float32)).astype(jnp.bfloat16)
    return high, low


def natural_tables(length):
    counter = np.arange(length)
    angles = (counter[:, None] * counter[None, :] % length) * (2.0 * math.pi / length)
    factor = 1.0 / math.sqrt(length)
    return np.cos(angles) * factor, np.sin(angles) * factor


def first_tables(length, cuts):
    cos, sin = natural_tables(length)
    width = length // cuts
    real, imag = [], []
    for cut in range(cuts):
        cols = slice(cut * width, (cut + 1) * width)
        real += [cos[:, cols], sin[:, cols]]
        imag += [-sin[:, cols], cos[:, cols]]
    table = np.repeat(np.concatenate(real + imag, axis=1), 2, axis=1).astype(np.float32)
    return np.concatenate(split_np(table), axis=1)


def second_tables(length):
    cos, sin = natural_tables(length)
    table = np.concatenate([cos, sin], axis=1).astype(np.float32)
    return np.concatenate(split_np(table), axis=1)


def slot_onehot(shift_row, low, stride_shift, stride_repeat, copies=1):
    count = shift_row.shape[1]
    across = jnp.broadcast_to(shift_row, (count, count))
    down = across.astype(jnp.float32).T.astype(jnp.int32)
    first = lax.broadcasted_iota(jnp.int32, (count, count), 0)
    second = lax.broadcasted_iota(jnp.int32, (count, count), 1)
    same = jnp.where((across == down) & (first < second), 1, 0)
    repeat = jnp.sum(same, axis=0, keepdims=True)
    slot = (shift_row - low) * stride_shift + repeat * stride_repeat
    if copies == 2:
        first = lax.broadcasted_iota(jnp.int32, (2 * count, count), 0)
        first = lax.shift_right_logical(first, 1)
    return first == slot


def dot(lhs, rhs):
    return jnp.dot(lhs, rhs, preferred_element_type=jnp.float32)


def place_in_line(pair, block):
    return block // 2 * 4 + (pair + block // 2) % 2 * 2 + block % 2


def device_of(line, places):
    quad, step = line // 4, line % 4
    return (step // 2 + quad) % 2 * places + quad * 2 + step % 2


def deal_kernel(source, out, held, sem):
    taken = lax.broadcasted_iota(jnp.int32, (128, 128), 1)
    given = lax.broadcasted_iota(jnp.int32, (128, 128), 0)
    wanted = lax.rem(lax.div(given, 2), 8) * 16 + lax.div(given, 16) * 2 + lax.rem(given, 2)
    move = jnp.where(taken == wanted, 1.0, 0.0).astype(jnp.bfloat16)
    parts, firsts, seconds, cells, _ = source.shape

    def load(part, group):
        span = pl.ds(group * 8, 8)
        number = part * (firsts // 8) + group
        return pltpu.make_async_copy(source.at[part, span], held.at[part, span], sem.at[number])

    groups = [(part, group) for part in range(parts) for group in range(firsts // 8)]
    for part, group in groups:
        load(part, group).start()
    for part, group in groups:
        load(part, group).wait()

        def second(own, carry):
            for tile in range(0, cells // 16, 2):
                columns = [
                    jnp.concatenate(
                        [
                            held[part, group * 8 + item, own, member * 16 : member * 16 + 16, :]
                            for item in range(8)
                        ],
                        axis=0,
                    )
                    for member in (tile, tile + 1)
                ]
                moved = dot(move, jnp.concatenate(columns, axis=1)).astype(jnp.bfloat16)
                for member in range(2):
                    for item in range(8):
                        out[(tile + member) * 8 + item, own, part, group * 16 : group * 16 + 16, :] = (
                            moved[item * 16 : item * 16 + 16, member * 128 : member * 128 + 128]
                        )
            return carry

        lax.fori_loop(0, seconds, second, 0, unroll=2)


def encode(columns):
    largest = jnp.maximum(jnp.max(jnp.abs(columns), axis=0, keepdims=True), LEAST)
    scale = jnp.ceil(jnp.log2(largest) * FINE)
    codes = jnp.round(columns * (jnp.exp2(scale * (-1.0 / FINE)) * TOP))
    return codes.astype(jnp.int32).astype(jnp.int16), scale


def decode(codes, scale):
    return codes.astype(jnp.int32).astype(jnp.float32) * (jnp.exp2(scale * (1.0 / FINE)) * (1.0 / TOP))


def transform_kernel(
    pairs, shift_one, shift_two, fraction_two, table_one, table_two, source,
    out, up_near, up_far, down_near, down_far, left_one, left_two, weight_near, weight_far, middle, scales,
    received, stage, load_sem, store_sem,
):
    count = 64
    lanes = out.shape[-1]
    local = received.shape[1]
    lines = received.shape[0] // (count // 8)
    loads = [
        pltpu.make_async_copy(
            source.at[pl.ds(block * lines, lines)],
            received.at[pl.ds(block * lines, lines)],
            load_sem.at[block],
        )
        for block in range(count // 8)
    ]
    for load in loads:
        load.start()
    onehot_one = jnp.where(slot_onehot(shift_one[...], -H, PER_SHIFT, 1, copies=2), 1.0, 0.0)
    picked = dot(onehot_one.astype(jnp.bfloat16), table_one[...])
    same_row = lax.rem(
        lax.broadcasted_iota(jnp.int32, picked.shape, 0)
        + lax.broadcasted_iota(jnp.int32, picked.shape, 1),
        2,
    )
    picked = jnp.where(same_row == 0, picked, 0.0).astype(jnp.bfloat16)
    for part in range(4):
        left_one[part * 2 * count : (part + 1) * 2 * count, :] = picked[
            :, part * 4 * count : (part + 1) * 4 * count
        ]
    hot_two = slot_onehot(shift_two[...], -H2, 1, 2 * H2)
    onehot_two = jnp.where(hot_two, 1.0, 0.0)
    picked = dot(onehot_two.astype(jnp.bfloat16), table_two[...]).astype(jnp.bfloat16)
    left_two[:count, :128] = picked[:, :128]
    left_two[:count, 128:] = picked[:, :128]
    left_two[count:, :128] = picked[:, 128:]
    left_two[count:, 128:] = jnp.zeros((count, 128), jnp.bfloat16)
    part_two = jnp.sum(
        jnp.where(hot_two, jnp.broadcast_to(fraction_two[...], hot_two.shape), 0.0),
        axis=1, keepdims=True,
    )
    rows = lax.broadcasted_iota(jnp.int32, (count, lanes), 0)
    origin = lax.broadcasted_iota(jnp.int32, (count, lanes), 1) - (lax.rem(rows, 2 * H2) - H2)
    weight_near[...] = jnp.where((origin >= 0) & (origin < lanes), 1.0 - part_two, 0.0)
    weight_far[...] = jnp.where((origin >= 1) & (origin <= lanes), part_two, 0.0)

    chunk = 2 * count * 2 * 8

    def first(block, carry):
        pltpu.make_async_copy(
            source.at[pl.ds(block * lines, lines)],
            received.at[pl.ds(block * lines, lines)],
            load_sem.at[block],
        ).wait()
        for index in range(0, 8, 2):
            columns = []
            for member in (index, index + 1):
                group, own = block * (8 // local) + member // local, member % local
                blocks = [
                    received[place_in_line(pair, group), own, part]
                    for pair in range(pairs)
                    for part in range(2)
                ]
                columns.append(jnp.concatenate(blocks, axis=0))
            both = dot(left_one[...], jnp.concatenate(columns, axis=1))
            both = both[: 4 * count] + both[4 * count :]
            for member in range(2):
                start = pl.multiple_of(block * chunk, chunk) + index + member
                middle[pl.ds(start, 4 * count, stride=8), :] = both[
                    :, member * lanes : (member + 1) * lanes
                ]
        return carry

    lax.fori_loop(0, count // 8, first, 0, unroll=2)

    targets = (up_near, up_far, down_near, down_far)
    stores = [
        pltpu.make_async_copy(
            stage.at[value % 2], out.at[pl.ds(value * PER_SHIFT, PER_SHIFT)], store_sem.at[value]
        )
        for value in range(2 * H)
    ]
    for value in range(2 * H):
        if value >= 2:
            stores[value - 2].wait()

        def second(item, carry):
            slot = value * PER_SHIFT + item
            columns = []
            for row in range(2):
                parts = [
                    middle[
                        pl.ds(
                            pl.multiple_of(block * chunk + ((part * count + slot) * 2 + row) * 8, 8), 8
                        ),
                        :,
                    ]
                    for part in range(2)
                    for block in range(count // 8)
                ]
                columns.append(jnp.concatenate(parts, axis=0))
            both = dot(
                left_two[...],
                jnp.concatenate(split(jnp.concatenate(columns, axis=1)), axis=0),
            )
            both = both[:count] + both[count:]
            for row in range(2):
                pieces = []
                for block in range(count // 8):
                    piece = both[block * 8 : block * 8 + 8, row * lanes : (row + 1) * lanes]
                    base = (lanes - H2 + 8 * (block % (2 * H2 // 8))) % lanes
                    near = pltpu.roll(piece, base, 1, stride=1, stride_axis=0)
                    far = pltpu.roll(near, 1, 1)
                    span = slice(block * 8, block * 8 + 8)
                    pieces.append(near * weight_near[span, :] + far * weight_far[span, :])
                moved = jnp.concatenate(pieces, axis=0)
                stage[value % 2, item, row] = moved
                hits = [
                    (kind, wanted.index((value, row)))
                    for kind, wanted in enumerate(HALOS)
                    if (value, row) in wanted
                ]
                if hits:
                    codes, scale = encode(moved)
                for kind, index in hits:
                    place = index * PER_SHIFT + item
                    start = pl.multiple_of(place * count, count)
                    targets[kind][pl.ds(start, count), :] = codes
                    scales[kind, pl.ds(place, 1), :] = scale
            return carry

        lax.fori_loop(0, PER_SHIFT, second, 0, unroll=8)
        stores[value].start()
    for kind, target in enumerate(targets):
        entries = target.shape[0] // (count + 1)
        target[entries * count :, :] = scales[kind, :entries, :].astype(jnp.int32).astype(jnp.int16)
    for store in stores[-2:]:
        store.wait()


def scatter_table_kernel(shift_two, kernel, table, rows):
    count = kernel.shape[1]
    reach = kernel.shape[0]
    offsets = lax.broadcasted_iota(jnp.int32, kernel.shape, 0)
    lags = lax.broadcasted_iota(jnp.int32, kernel.shape, 1)
    full = kernel[...] + jnp.where((offsets == R) & (lags == 0), 1.0, 0.0)
    high, low = split(full)
    lag = lax.broadcasted_iota(jnp.int32, (count, 2 * count), 0)
    lane = lax.broadcasted_iota(jnp.int32, (count, 2 * count), 1)
    mirror = jnp.where(lax.rem(lag + lane, count) == 0, 1.0, 0.0).astype(jnp.bfloat16)
    rows[...] = jnp.zeros(rows.shape, jnp.float32)
    rows[0, 3 : 3 + reach, :] = dot(high, mirror)
    rows[1, 3 : 3 + reach, :] = dot(low, mirror)
    onehot = jnp.where(slot_onehot(shift_two[...], -H2, 1, 2 * H2), 1.0, 0.0).T
    blank = jnp.zeros((count, count), jnp.float32)
    choose = jnp.concatenate(
        [jnp.concatenate([onehot, blank], axis=1), jnp.concatenate([blank, onehot], axis=1)], axis=0
    ).astype(jnp.bfloat16)
    left = lane < count

    def circulant(part, index):
        row = jnp.broadcast_to(rows[part, index : index + 1, :], (8, 2 * count))
        return jnp.concatenate(
            [pltpu.roll(row, 8 * block, 1, stride=1, stride_axis=0) for block in range(count // 8)],
            axis=0,
        )

    for part in range(2):
        here = circulant(part, 0)
        for index in range(reach + 5):
            there = circulant(part, index + 1)
            pair = dot(jnp.where(left, here, there).astype(jnp.bfloat16), choose)
            pair = pair.astype(jnp.bfloat16)
            here = there
            for band in range(4):
                if (index - 3 + band) % 2 == 0 and 0 <= (index - 3 + band) // 2 < 10:
                    column = (index - 3 + band) // 2 * 128
                    start = part * 256 + band * count
                    table[start : start + count, column : column + 128] = pair


def scatter_pair(index, first_group, table, high, low, out, scales):
    start = pl.multiple_of((first_group + index * 2) * 256, 256)

    def window(half):
        return jnp.concatenate(
            [half[pl.ds(start, 1280), :], half[pl.ds(start + 256, 1280), :]], axis=1
        )

    both = dot(table[...], window(high))
    rest = dot(table[:256, :], window(low))
    total = both[:256] + both[256:] + rest
    for member in range(2):
        target = pl.multiple_of((index * 2 + member) * 256, 256)
        for row in range(2):
            column = member * 256 + row * 128
            part = total[:, column : column + 128]
            blocks = [encode(part[band * 64 : band * 64 + 64]) for band in range(4)]
            out[row, pl.ds(target, 256), :] = jnp.concatenate(
                [codes for codes, _ in blocks], axis=0
            )
            for band in range(4):
                scales[row, pl.ds((index * 2 + member) * 4 + band, 1), :] = blocks[band][1]


def scatter_groups(first_group, groups, table, high, low, out, scales):
    def step(index, carry):
        scatter_pair(index, first_group, table, high, low, out, scales)
        return carry

    lax.fori_loop(0, groups // 2, step, 0, unroll=4)


def shear_kernel(
    shift_one, fraction_one, table, source, up_near, up_far, down_near, down_far,
    high, low, out, order, seen, arrived, sent, moved, load_sem,
):
    count = moved.shape[0]
    loads = [
        pltpu.make_async_copy(
            source.at[pl.ds(value * PER_SHIFT, PER_SHIFT)],
            moved.at[pl.ds(value * PER_SHIFT, PER_SHIFT)],
            load_sem.at[value],
        )
        for value in range(2 * H)
    ]
    for load in loads:
        load.start()
    for value in range(2 * H):
        seen[value] = 0

    def place(band, carry):
        value = shift_one[band] + H
        repeat = seen[value]
        order[value * PER_SHIFT + repeat] = band
        seen[value] = repeat + 1
        return carry

    lax.fori_loop(0, count, place, 0)
    sources = (up_near, up_far, down_near, down_far)
    for kind, source in enumerate(sources):
        entries = source.shape[0] // (count + 1)
        codes = source[entries * count :, :].astype(jnp.int32)
        arrived[kind, :entries, :] = codes.astype(jnp.float32)

    def fetch(value, item, row):
        if row in (0, 1):
            return moved[value * PER_SHIFT + item, row]
        if row < 0:
            kind, key = (0, (value, row + 2)) if row >= -2 else (1, (value, row + 4))
        else:
            kind, key = (2, (value, row - 2)) if row <= 3 else (3, (value, row - 4))
        place = HALOS[kind].index(key) * PER_SHIFT + item
        start = pl.multiple_of(place * count, count)
        return decode(sources[kind][pl.ds(start, count), :], arrived[kind, pl.ds(place, 1), :])

    for value in range(2 * H):
        shift = value - H
        loads[value].wait()

        def shear(item, carry):
            band = order[value * PER_SHIFT + item]
            weight = fraction_one[band]
            need = {
                row: fetch(value, item, row)
                for row in (-shift - 1, -shift, 1 - shift)
            }
            full = jnp.concatenate(
                [
                    (1.0 - weight) * need[row - shift] + weight * need[row - shift - 1]
                    for row in range(2)
                ],
                axis=1,
            )
            top, bottom = split(full)

            def put(index):
                start = pl.multiple_of(index * count, count)
                high[pl.ds(start, count), :] = top
                low[pl.ds(start, count), :] = bottom

            put(band + R)

            @pl.when(band < R)
            def _():
                put(band + R + count)

            @pl.when(band >= count - R)
            def _():
                put(band + R - count)

            return carry

        lax.fori_loop(0, PER_SHIFT, shear, 0, unroll=4)
    scatter_band(1 - lax.axis_index("dir"), 0, table, high, low, out, sent)


def scatter_band(side, first_group, table, high, low, out, sent):
    bands = sent.shape[1]
    first = side * (high.shape[0] // 64 - 2 * R) // 8 + first_group
    scatter_groups(first, bands // 4, table, high, low, out, sent)
    for row in range(2):
        out[row, bands * 64 :, :] = sent[row].astype(jnp.int32).astype(jnp.int16)


def scatter_away_kernel(table, high, low, out, sent):
    scatter_band(1 - lax.axis_index("dir"), sent.shape[1] // 4, table, high, low, out, sent)


def scatter_own_kernel(table, high, low, out, sent):
    scatter_band(lax.axis_index("dir"), 0, table, high, low, out, sent)


def merge_kernel(*refs):
    local, across, out, scales, stage, store_sem = refs[:2], refs[2:6], *refs[6:]
    bands = scales.shape[1]
    size = bands * 64
    steps = store_sem.shape[0]
    width = size // steps
    block = lax.axis_index("pos")
    core = lax.rem(block, 2)
    held_here = lax.rem(lax.axis_index("dir") + lax.div(block, 2) + core, 2) == 0
    stores = [
        pltpu.make_async_copy(
            stage.at[pl.ds(step * width * 4, width * 4)],
            out.at[pl.ds(step * width * 4, width * 4)],
            store_sem.at[step],
        )
        for step in range(steps)
    ]
    for side in range(2):
        for here in range(2):
            used = ((local[0],), (local[1],)) if here else (across[:2], across[2:])
            share = bands // len(used[0])

            @pl.when((core == side) & (held_here == (here == 1)))
            def _():
                for slot in range(2):
                    for row in range(2):
                        for index, piece in enumerate(used[slot]):
                            scale = piece[row, share * 64 : share * 65, :].astype(jnp.int32)
                            span = slice(index * share, (index + 1) * share)
                            scales[slot * 2 + row, span, :] = scale.astype(jnp.float32)
                for step in range(steps):
                    for slot in range(2):
                        pair = side if slot == 0 else 1 - side
                        for row in range(2):
                            for band in range(step * width // 64, (step + 1) * width // 64):
                                begin = band % share * 64
                                rows = used[slot][band // share][row, begin : begin + 64, :]
                                value = decode(rows, scales[slot * 2 + row, band : band + 1, :])
                                stage[pl.ds(2 * pair + row + band * 256, 64, stride=4), :] = value
                    stores[step].start()

    for store in stores:
        store.wait()


def vmem(number):
    return [pl.BlockSpec(memory_space=VMEM)] * number


def grant(mebibytes):
    return pltpu.CompilerParams(vmem_limit_bytes=mebibytes << 20)


def in_vmem(value):
    return pltpu.with_memory_space_constraint(value, VMEM)


def anywhere(number):
    return [pl.BlockSpec(memory_space=pl.ANY)] * number


def smem(number):
    return [pl.BlockSpec(memory_space=SMEM)] * number


def fast_body(coherence, shift_first, fraction_first, shift_second, fraction_second, scatter_kernel):
    f32, bf16 = jnp.float32, jnp.bfloat16
    shape = jax.ShapeDtypeStruct
    pairs, places = lax.axis_size("dir"), lax.axis_size("pos")
    parts, own_first, own_second, _, lanes = coherence.shape
    bands = own_first * pairs
    total = pairs * places
    cut = pl.pallas_call(
        deal_kernel,
        out_shape=shape((total, own_second, parts, own_first * 2, lanes), bf16),
        in_specs=[pl.BlockSpec(memory_space=pltpu.HBM)],
        out_specs=pl.BlockSpec(memory_space=VMEM),
        scratch_shapes=[
            VMEM(coherence.shape, bf16),
            pltpu.SemaphoreType.DMA((parts * own_first // 8,)),
        ],
        compiler_params=grant(16),
        name="deal",
    )(pltpu.with_memory_space_constraint(coherence, pltpu.HBM))
    cut = in_vmem(cut)
    received = lax.all_to_all(
        cut, ("dir", "pos"), split_axis=0, concat_axis=0, tiled=True,
        axis_index_groups=[[device_of(line, places) for line in range(total)]],
    )

    row_one, row_two = shift_first.reshape(1, bands), shift_second.reshape(1, bands)
    halo_shapes = [shape((len(one) * PER_SHIFT * (bands + 1), lanes), jnp.int16) for one in HALOS]
    moved, *halos = pl.pallas_call(
        functools.partial(transform_kernel, pairs),
        out_shape=[shape((bands, 2, bands, lanes), f32)] + halo_shapes,
        in_specs=vmem(5) + [pl.BlockSpec(memory_space=pl.ANY)],
        out_specs=[pl.BlockSpec(memory_space=pl.ANY)] + vmem(4),
        scratch_shapes=[
            VMEM((8 * bands, 4 * bands), bf16),
            VMEM((2 * bands, 4 * bands), bf16),
            VMEM((bands, lanes), f32),
            VMEM((bands, lanes), f32),
            VMEM((4 * bands * bands, lanes), f32),
            VMEM((4, len(UP_NEAR) * PER_SHIFT, lanes), f32),
            VMEM(received.shape, bf16),
            VMEM((2, PER_SHIFT, 2, bands, lanes), f32),
            pltpu.SemaphoreType.DMA((bands // 8,)),
            pltpu.SemaphoreType.DMA((2 * H,)),
        ],
        compiler_params=grant(26),
        name="transform",
    )(
        row_one, row_two, fraction_second.reshape(1, bands),
        jnp.asarray(first_tables(bands, pairs)), jnp.asarray(second_tables(bands)), received,
    )

    def place(line):
        return device_of(line, places)

    arrived = [None] * 4
    for kind, step in ((1, 2), (3, -2), (0, 1), (2, -1)):
        hops = [(place(b), place(b + step)) for b in range(total) if 0 <= b + step < total]
        arrived[kind] = in_vmem(lax.ppermute(halos[kind], ("dir", "pos"), hops))

    table = pl.pallas_call(
        scatter_table_kernel,
        out_shape=shape((512, 1280), bf16),
        in_specs=vmem(2),
        out_specs=pl.BlockSpec(memory_space=VMEM),
        scratch_shapes=[VMEM((2, 32, 2 * bands), f32)],
        compiler_params=grant(8),
        name="scatter_table",
    )(row_two, scatter_kernel)

    table = in_vmem(table)
    wrapped = (bands + 2 * R) * bands
    half = bands * bands // 2
    codes = shape((2, half + bands // 2, lanes), jnp.int16)
    half_codes = shape((2, (half + bands // 2) // 2, lanes), jnp.int16)
    high, low, away_first = pl.pallas_call(
        shear_kernel,
        out_shape=[shape((wrapped, 2 * lanes), bf16)] * 2 + [half_codes],
        in_specs=smem(2) + vmem(1) + anywhere(1) + vmem(4),
        out_specs=vmem(3),
        scratch_shapes=[
            SMEM((bands,), jnp.int32),
            SMEM((2 * H,), jnp.int32),
            VMEM((4, len(UP_NEAR) * PER_SHIFT, lanes), f32),
            VMEM((2, bands // 4, lanes), f32),
            VMEM(moved.shape, f32),
            pltpu.SemaphoreType.DMA((2 * H,)),
        ],
        compiler_params=grant(16),
        name="shear",
    )(shift_first, fraction_first, table, moved, *arrived)
    high, low = in_vmem(high), in_vmem(low)
    home = [(d, q, c, (d + q) % 2) for d in range(pairs) for q in range(places // 2) for c in range(2)]
    same = [
        (d * places + 2 * q + c, (1 - d) * places + 2 * q + b) for d, q, c, b in home if b == c
    ]
    cross = [
        (d * places + 2 * q + c, (1 - d) * places + 2 * q + b) for d, q, c, b in home if b != c
    ]
    inside = [(d * places + 2 * q + c, d * places + 2 * q + b) for d, q, c, b in home if b != c]

    def scatter(kernel, out_shape, bands_held):
        return pl.pallas_call(
            kernel,
            out_shape=out_shape,
            in_specs=vmem(3),
            out_specs=pl.BlockSpec(memory_space=VMEM),
            scratch_shapes=[VMEM((2, bands_held, lanes), f32)],
            compiler_params=grant(8),
        )(table, high, low)

    from_same, from_cross = [], []
    away = away_first
    for part in range(2):
        from_same.append(lax.ppermute(away, ("dir", "pos"), same))
        from_cross.append(lax.ppermute(away, ("dir", "pos"), cross))
        if part == 0:
            away = scatter(scatter_away_kernel, half_codes, bands // 4)
    own = scatter(scatter_own_kernel, codes, bands // 2)
    from_inside = lax.ppermute(own, ("dir", "pos"), inside)
    pieces = [own] + [in_vmem(piece) for piece in (from_inside, *from_same, *from_cross)]
    merged = pl.pallas_call(
        merge_kernel,
        out_shape=shape((half * 4, lanes), f32),
        in_specs=vmem(6),
        out_specs=pl.BlockSpec(memory_space=pl.ANY),
        scratch_shapes=[
            VMEM((4, bands // 2, lanes), f32),
            VMEM((half * 4, lanes), f32),
            pltpu.SemaphoreType.DMA((8,)),
        ],
        compiler_params=grant(12),
        name="merge",
    )(*pieces)
    return merged.reshape(own_first, bands, 4, lanes)


def with_halo(cells, sides, width, closed):
    for axis, dim in sides:
        count = lax.axis_size(axis)
        ends = count if closed else count - 1
        head = lax.slice_in_dim(cells, 0, width, axis=dim)
        tail = lax.slice_in_dim(cells, cells.shape[dim] - width, cells.shape[dim], axis=dim)
        cells = jnp.concatenate(
            [
                lax.ppermute(tail, axis, [(i, (i + 1) % count) for i in range(ends)]),
                cells,
                lax.ppermute(head, axis, [((i + 1) % count, i) for i in range(ends)]),
            ],
            axis=dim,
        )
    return cells


def phase_tables(length):
    counter = jnp.arange(length, dtype=jnp.int32)
    product = counter[:, None] * counter[None, :] % length
    angles = product.astype(jnp.float32) * (2.0 * math.pi / length)
    factor = 1.0 / math.sqrt(length)
    return (jnp.cos(angles) * factor, jnp.sin(angles) * factor)


def contract(pattern, operand_a, operand_b):
    return jnp.einsum(
        pattern,
        operand_a,
        operand_b,
        precision=lax.Precision.HIGHEST,
        preferred_element_type=jnp.float32,
    )


def finish_bands(received):
    cos_one, sin_one = phase_tables(received.shape[1])
    real_part = contract("ts,sbax->tbax", cos_one, received[0]) + contract(
        "ts,sbax->tbax", sin_one, received[1]
    )
    return lax.all_to_all(real_part, "dir", split_axis=0, concat_axis=1, tiled=True)


def shear_block(wigner, shift_first, fraction_first):
    band_count = wigner.shape[0]
    cell_count = wigner.shape[2]
    first_band = lax.axis_index("dir") * band_count
    shifts = lax.dynamic_slice_in_dim(shift_first, first_band, band_count)
    weights = lax.dynamic_slice_in_dim(fraction_first, first_band, band_count)
    padded = with_halo(wigner, (("pos", 2),), H, False)
    rows_out = jnp.arange(cell_count, dtype=jnp.int32)
    rows_in = jnp.arange(cell_count + 2 * H, dtype=jnp.int32)
    target = rows_out[None, :, None] + H - shifts[:, None, None]
    near_tap = (rows_in[None, None, :] == target).astype(jnp.float32)
    far_tap = (rows_in[None, None, :] == target - 1).astype(jnp.float32)
    band_matrix = (1.0 - weights)[:, None, None] * near_tap + weights[:, None, None] * far_tap
    return contract("kaj,kbjx->kbax", band_matrix, padded)


def convolve(circulant, source, out_rows):
    summed = jnp.zeros((out_rows,) + source.shape[1:], jnp.float32)
    for offset in range(circulant.shape[0]):
        summed = summed + contract(
            "ij,kjax->kiax", circulant[offset], source[offset : offset + out_rows]
        )
    return summed


def body(coherence, shift_first, fraction_first, shift_second, fraction_second, scatter_kernel):
    direction_count = coherence.shape[2] * lax.axis_size("pos")
    cos_two, sin_two = phase_tables(direction_count)
    cell_block = lax.all_to_all(coherence, "pos", split_axis=3, concat_axis=2, tiled=True)
    real_in = cell_block[0].astype(jnp.float32)
    imag_in = cell_block[1].astype(jnp.float32)
    real_mid = contract("ts,bsax->btax", cos_two, real_in) + contract(
        "ts,bsax->btax", sin_two, imag_in
    )
    imag_mid = contract("ts,bsax->btax", cos_two, imag_in) - contract(
        "ts,bsax->btax", sin_two, real_in
    )
    mixed = jnp.stack([real_mid, imag_mid])
    wigner = finish_bands(lax.all_to_all(mixed, "dir", split_axis=2, concat_axis=1, tiled=True))
    moved_one = shear_block(wigner, shift_first, fraction_first)
    band_count = moved_one.shape[0]
    column_count = moved_one.shape[3]
    positions = jnp.arange(column_count, dtype=jnp.int32)
    target_two = positions[None, :, None] - shift_second[:, None, None]
    near_two = (positions[None, None, :] == target_two).astype(jnp.float32)
    far_two = (positions[None, None, :] == target_two - 1).astype(jnp.float32)
    shear_matrix = (1.0 - fraction_second)[:, None, None] * near_two + fraction_second[
        :, None, None
    ] * far_two
    moved_two = contract("bxy,kbay->kbax", shear_matrix, moved_one)
    kernel_positions = jnp.arange(direction_count, dtype=jnp.int32)
    lag_index = (kernel_positions[:, None] - kernel_positions[None, :]) % direction_count
    circulant = scatter_kernel[:, lag_index]
    extended = with_halo(moved_two, (("dir", 0),), R, True)
    summed = moved_two + convolve(circulant, extended, band_count)
    return summed


def fits(mesh, coherence):
    pairs, places = mesh.shape["dir"], mesh.shape["pos"]
    _, first, second, cells, lanes = coherence.shape
    return 4 * places == second and (pairs, first, second, cells, lanes) == (2, 64, 64, 4 * places, 128)


def solution(mesh):
    placed = (P(None, "dir", "pos", None, None), P(), P(), P(), P(), P())

    def run(*arrays):
        fast = fits(mesh, arrays[0])
        step = jax.shard_map(
            fast_body if fast else body,
            mesh=mesh, in_specs=placed, out_specs=P("dir", None, "pos", None), check_vma=False,
        )
        return step(*arrays)

    return run
```

```python
import functools
import math

import jax
import jax.numpy as jnp
import numpy as np
from jax import lax
from jax.experimental import pallas as pl
from jax.experimental.pallas import tpu as pltpu
from jax.sharding import PartitionSpec as P

R = 8
H = 4
H2 = 16

UP_NEAR = ((4, 1), (5, 0), (5, 1), (6, 0), (6, 1), (7, 0))
UP_FAR = ((6, 1), (7, 0), (7, 1))
DOWN_NEAR = ((3, 0), (2, 0), (2, 1), (1, 0), (1, 1), (0, 1))
DOWN_FAR = ((1, 0), (0, 0), (0, 1))
HALOS = (UP_NEAR, UP_FAR, DOWN_NEAR, DOWN_FAR)
PER_SHIFT = 8
OUTER, INNER = (0, 1, 6, 7), (2, 3, 4, 5)
TOP = 32600.0
FINE = 8.0
LEAST = 1e-30
VMEM = pltpu.VMEM
SMEM = pltpu.SMEM


def split_np(table):
    high = table.astype(jnp.bfloat16)
    low = (table - high.astype(np.float32)).astype(jnp.bfloat16)
    return high, low


def split(value):
    high = value.astype(jnp.bfloat16)
    low = (value - high.astype(jnp.float32)).astype(jnp.bfloat16)
    return high, low


def natural_tables(length):
    counter = np.arange(length)
    angles = (counter[:, None] * counter[None, :] % length) * (2.0 * math.pi / length)
    factor = 1.0 / math.sqrt(length)
    return np.cos(angles) * factor, np.sin(angles) * factor


def first_tables(length, cuts):
    cos, sin = natural_tables(length)
    width = length // cuts
    real, imag = [], []
    for cut in range(cuts):
        cols = slice(cut * width, (cut + 1) * width)
        real += [cos[:, cols], sin[:, cols]]
        imag += [-sin[:, cols], cos[:, cols]]
    table = np.repeat(np.concatenate(real + imag, axis=1), 2, axis=1).astype(np.float32)
    return np.concatenate(split_np(table), axis=1)


def second_tables(length):
    cos, sin = natural_tables(length)
    table = np.concatenate([cos, sin], axis=1).astype(np.float32)
    return np.concatenate(split_np(table), axis=1)


def slot_onehot(shift_row, low, stride_shift, stride_repeat, copies=1):
    count = shift_row.shape[1]
    across = jnp.broadcast_to(shift_row, (count, count))
    down = across.astype(jnp.float32).T.astype(jnp.int32)
    first = lax.broadcasted_iota(jnp.int32, (count, count), 0)
    second = lax.broadcasted_iota(jnp.int32, (count, count), 1)
    same = jnp.where((across == down) & (first < second), 1, 0)
    repeat = jnp.sum(same, axis=0, keepdims=True)
    slot = (shift_row - low) * stride_shift + repeat * stride_repeat
    if copies == 2:
        first = lax.broadcasted_iota(jnp.int32, (2 * count, count), 0)
        first = lax.shift_right_logical(first, 1)
    return first == slot


def dot(lhs, rhs):
    return jnp.dot(lhs, rhs, preferred_element_type=jnp.float32)


def place_in_line(pair, block):
    return block // 2 * 4 + (pair + block // 2) % 2 * 2 + block % 2


def device_of(line, places):
    quad, step = line // 4, line % 4
    return (step // 2 + quad) % 2 * places + quad * 2 + step % 2


def deal_kernel(source, out, held, sem):
    taken = lax.broadcasted_iota(jnp.int32, (128, 128), 1)
    given = lax.broadcasted_iota(jnp.int32, (128, 128), 0)
    wanted = lax.rem(lax.div(given, 2), 8) * 16 + lax.div(given, 16) * 2 + lax.rem(given, 2)
    move = jnp.where(taken == wanted, 1.0, 0.0).astype(jnp.bfloat16)
    parts, firsts, seconds, cells, _ = source.shape

    def load(part, group):
        span = pl.ds(group * 8, 8)
        number = part * (firsts // 8) + group
        return pltpu.make_async_copy(source.at[part, span], held.at[part, span], sem.at[number])

    groups = [(part, group) for part in range(parts) for group in range(firsts // 8)]
    for part, group in groups:
        load(part, group).start()
    for part, group in groups:
        load(part, group).wait()

        def second(own, carry):
            for tile in range(0, cells // 16, 2):
                columns = [
                    jnp.concatenate(
                        [
                            held[part, group * 8 + item, own, member * 16 : member * 16 + 16, :]
                            for item in range(8)
                        ],
                        axis=0,
                    )
                    for member in (tile, tile + 1)
                ]
                moved = dot(move, jnp.concatenate(columns, axis=1)).astype(jnp.bfloat16)
                for member in range(2):
                    for item in range(8):
                        out[(tile + member) * 8 + item, own, part, group * 16 : group * 16 + 16, :] = (
                            moved[item * 16 : item * 16 + 16, member * 128 : member * 128 + 128]
                        )
            return carry

        lax.fori_loop(0, seconds, second, 0, unroll=2)


def encode(columns):
    largest = jnp.maximum(jnp.max(jnp.abs(columns), axis=0, keepdims=True), LEAST)
    scale = jnp.ceil(jnp.log2(largest) * FINE)
    codes = jnp.round(columns * (jnp.exp2(scale * (-1.0 / FINE)) * TOP))
    return codes.astype(jnp.int32).astype(jnp.int16), scale


def decode(codes, scale):
    return codes.astype(jnp.int32).astype(jnp.float32) * (jnp.exp2(scale * (1.0 / FINE)) * (1.0 / TOP))


def transform_kernel(
    pairs, shift_one, shift_two, fraction_two, table_one, table_two, source,
    out, up_near, up_far, down_near, down_far, middle, left_two, weight_near, weight_far, scales,
    left_one, received, load_sem,
):
    count = 64
    lanes = out.shape[-1]
    local = received.shape[1]
    lines = received.shape[0] // (count // 8)
    loads = [
        pltpu.make_async_copy(
            source.at[pl.ds(block * lines, lines)],
            received.at[pl.ds(block * lines, lines)],
            load_sem.at[block],
        )
        for block in range(count // 8)
    ]
    for load in loads:
        load.start()
    onehot_one = jnp.where(slot_onehot(shift_one[...], -H, PER_SHIFT, 1, copies=2), 1.0, 0.0)
    picked = dot(onehot_one.astype(jnp.bfloat16), table_one[...])
    same_row = lax.rem(
        lax.broadcasted_iota(jnp.int32, picked.shape, 0)
        + lax.broadcasted_iota(jnp.int32, picked.shape, 1),
        2,
    )
    picked = jnp.where(same_row == 0, picked, 0.0).astype(jnp.bfloat16)
    for part in range(4):
        left_one[part * 2 * count : (part + 1) * 2 * count, :] = picked[
            :, part * 4 * count : (part + 1) * 4 * count
        ]
    hot_two = slot_onehot(shift_two[...], -H2, 1, 2 * H2)
    onehot_two = jnp.where(hot_two, 1.0, 0.0)
    picked = dot(onehot_two.astype(jnp.bfloat16), table_two[...]).astype(jnp.bfloat16)
    left_two[:count, :128] = picked[:, :128]
    left_two[:count, 128:] = picked[:, :128]
    left_two[count:, :128] = picked[:, 128:]
    left_two[count:, 128:] = jnp.zeros((count, 128), jnp.bfloat16)
    part_two = jnp.sum(
        jnp.where(hot_two, jnp.broadcast_to(fraction_two[...], hot_two.shape), 0.0),
        axis=1, keepdims=True,
    )
    rows = lax.broadcasted_iota(jnp.int32, (count, lanes), 0)
    origin = lax.broadcasted_iota(jnp.int32, (count, lanes), 1) - (lax.rem(rows, 2 * H2) - H2)
    weight_near[...] = jnp.where((origin >= 0) & (origin < lanes), 1.0 - part_two, 0.0)
    weight_far[...] = jnp.where((origin >= 1) & (origin <= lanes), part_two, 0.0)

    chunk = 2 * count * 2 * 8

    def first(block, carry):
        pltpu.make_async_copy(
            source.at[pl.ds(block * lines, lines)],
            received.at[pl.ds(block * lines, lines)],
            load_sem.at[block],
        ).wait()
        for index in range(0, 8, 2):
            columns = []
            for member in (index, index + 1):
                group, own = block * (8 // local) + member // local, member % local
                blocks = [
                    received[place_in_line(pair, group), own, part]
                    for pair in range(pairs)
                    for part in range(2)
                ]
                columns.append(jnp.concatenate(blocks, axis=0))
            both = dot(left_one[...], jnp.concatenate(columns, axis=1))
            both = both[: 4 * count] + both[4 * count :]
            for member in range(2):
                start = pl.multiple_of(block * chunk, chunk) + index + member
                middle[pl.ds(start, 4 * count, stride=8), :] = both[
                    :, member * lanes : (member + 1) * lanes
                ]
        return carry

    lax.fori_loop(0, count // 8, first, 0, unroll=2)

    targets = (up_near, up_far, down_near, down_far)
    finish_directions(OUTER, middle, left_two, weight_near, weight_far, out, targets, scales)
    code_halo_scales(1, up_far, scales)
    code_halo_scales(3, down_far, scales)


def rest_kernel(
    up_near_in, down_near_in, middle, left_two, weight_near, weight_far, scales_in,
    out, up_near, down_near, scales,
):
    scales[...] = scales_in[...]
    up_near[...] = up_near_in[...]
    down_near[...] = down_near_in[...]
    targets = (up_near, None, down_near, None)
    finish_directions(INNER, middle, left_two, weight_near, weight_far, out, targets, scales)
    code_halo_scales(0, up_near, scales)
    code_halo_scales(2, down_near, scales)


def code_halo_scales(kind, target, scales):
    entries = target.shape[0] // 65
    target[entries * 64 :, :] = scales[kind, :entries, :].astype(jnp.int32).astype(jnp.int16)


def finish_directions(values, middle, left_two, weight_near, weight_far, out, targets, scales):
    count = 64
    lanes = out.shape[-1]
    chunk = 2 * count * 2 * 8
    for position, value in enumerate(values):

        def second(item, carry):
            slot = value * PER_SHIFT + item
            columns = []
            for row in range(2):
                parts = [
                    middle[
                        pl.ds(
                            pl.multiple_of(block * chunk + ((part * count + slot) * 2 + row) * 8, 8), 8
                        ),
                        :,
                    ]
                    for part in range(2)
                    for block in range(count // 8)
                ]
                columns.append(jnp.concatenate(parts, axis=0))
            both = dot(
                left_two[...],
                jnp.concatenate(split(jnp.concatenate(columns, axis=1)), axis=0),
            )
            both = both[:count] + both[count:]
            for row in range(2):
                pieces = []
                for block in range(count // 8):
                    piece = both[block * 8 : block * 8 + 8, row * lanes : (row + 1) * lanes]
                    base = (lanes - H2 + 8 * (block % (2 * H2 // 8))) % lanes
                    near = pltpu.roll(piece, base, 1, stride=1, stride_axis=0)
                    far = pltpu.roll(near, 1, 1)
                    span = slice(block * 8, block * 8 + 8)
                    pieces.append(near * weight_near[span, :] + far * weight_far[span, :])
                moved = jnp.concatenate(pieces, axis=0)
                out[position * PER_SHIFT + item, row] = moved
                hits = [
                    (kind, wanted.index((value, row)))
                    for kind, wanted in enumerate(HALOS)
                    if (value, row) in wanted
                ]
                if hits:
                    codes, scale = encode(moved)
                for kind, index in hits:
                    place = index * PER_SHIFT + item
                    start = pl.multiple_of(place * count, count)
                    targets[kind][pl.ds(start, count), :] = codes
                    scales[kind, pl.ds(place, 1), :] = scale
            return carry

        lax.fori_loop(0, PER_SHIFT, second, 0, unroll=8)


def scatter_table_kernel(shift_two, kernel, table, rows):
    count = kernel.shape[1]
    reach = kernel.shape[0]
    offsets = lax.broadcasted_iota(jnp.int32, kernel.shape, 0)
    lags = lax.broadcasted_iota(jnp.int32, kernel.shape, 1)
    full = kernel[...] + jnp.where((offsets == R) & (lags == 0), 1.0, 0.0)
    high, low = split(full)
    lag = lax.broadcasted_iota(jnp.int32, (count, 2 * count), 0)
    lane = lax.broadcasted_iota(jnp.int32, (count, 2 * count), 1)
    mirror = jnp.where(lax.rem(lag + lane, count) == 0, 1.0, 0.0).astype(jnp.bfloat16)
    rows[...] = jnp.zeros(rows.shape, jnp.float32)
    rows[0, 3 : 3 + reach, :] = dot(high, mirror)
    rows[1, 3 : 3 + reach, :] = dot(low, mirror)
    onehot = jnp.where(slot_onehot(shift_two[...], -H2, 1, 2 * H2), 1.0, 0.0).T
    blank = jnp.zeros((count, count), jnp.float32)
    choose = jnp.concatenate(
        [jnp.concatenate([onehot, blank], axis=1), jnp.concatenate([blank, onehot], axis=1)], axis=0
    ).astype(jnp.bfloat16)
    left = lane < count

    def circulant(part, index):
        row = jnp.broadcast_to(rows[part, index : index + 1, :], (8, 2 * count))
        return jnp.concatenate(
            [pltpu.roll(row, 8 * block, 1, stride=1, stride_axis=0) for block in range(count // 8)],
            axis=0,
        )

    for part in range(2):
        here = circulant(part, 0)
        for index in range(reach + 5):
            there = circulant(part, index + 1)
            pair = dot(jnp.where(left, here, there).astype(jnp.bfloat16), choose)
            pair = pair.astype(jnp.bfloat16)
            here = there
            for band in range(4):
                if (index - 3 + band) % 2 == 0 and 0 <= (index - 3 + band) // 2 < 10:
                    column = (index - 3 + band) // 2 * 128
                    start = part * 256 + band * count
                    table[start : start + count, column : column + 128] = pair


def scatter_pair(index, first_group, table, high, low, out, scales):
    start = pl.multiple_of((first_group + index * 2) * 256, 256)

    def window(half):
        return jnp.concatenate(
            [half[pl.ds(start, 1280), :], half[pl.ds(start + 256, 1280), :]], axis=1
        )

    both = dot(table[...], window(high))
    rest = dot(table[:256, :], window(low))
    total = both[:256] + both[256:] + rest
    for member in range(2):
        target = pl.multiple_of((index * 2 + member) * 256, 256)
        for row in range(2):
            column = member * 256 + row * 128
            part = total[:, column : column + 128]
            blocks = [encode(part[band * 64 : band * 64 + 64]) for band in range(4)]
            out[row, pl.ds(target, 256), :] = jnp.concatenate(
                [codes for codes, _ in blocks], axis=0
            )
            for band in range(4):
                scales[row, pl.ds((index * 2 + member) * 4 + band, 1), :] = blocks[band][1]


def scatter_groups(first_group, groups, table, high, low, out, scales):
    def step(index, carry):
        scatter_pair(index, first_group, table, high, low, out, scales)
        return carry

    lax.fori_loop(0, groups // 2, step, 0, unroll=4)


def shear_kernel(
    shift_one, fraction_one, table, outer, inner, up_near, up_far, down_near, down_far,
    high, low, out, order, seen, arrived, sent,
):
    count = outer.shape[2]
    for value in range(2 * H):
        seen[value] = 0

    def place(band, carry):
        value = shift_one[band] + H
        repeat = seen[value]
        order[value * PER_SHIFT + repeat] = band
        seen[value] = repeat + 1
        return carry

    lax.fori_loop(0, count, place, 0)
    sources = (up_near, up_far, down_near, down_far)
    for kind, source in enumerate(sources):
        entries = source.shape[0] // (count + 1)
        codes = source[entries * count :, :].astype(jnp.int32)
        arrived[kind, :entries, :] = codes.astype(jnp.float32)

    def fetch(value, item, row):
        if row in (0, 1):
            held, values = (outer, OUTER) if value in OUTER else (inner, INNER)
            return held[values.index(value) * PER_SHIFT + item, row]
        if row < 0:
            kind, key = (0, (value, row + 2)) if row >= -2 else (1, (value, row + 4))
        else:
            kind, key = (2, (value, row - 2)) if row <= 3 else (3, (value, row - 4))
        place = HALOS[kind].index(key) * PER_SHIFT + item
        start = pl.multiple_of(place * count, count)
        return decode(sources[kind][pl.ds(start, count), :], arrived[kind, pl.ds(place, 1), :])

    for value in range(2 * H):
        shift = value - H

        def shear(item, carry):
            band = order[value * PER_SHIFT + item]
            weight = fraction_one[band]
            need = {
                row: fetch(value, item, row)
                for row in (-shift - 1, -shift, 1 - shift)
            }
            full = jnp.concatenate(
                [
                    (1.0 - weight) * need[row - shift] + weight * need[row - shift - 1]
                    for row in range(2)
                ],
                axis=1,
            )
            top, bottom = split(full)

            def put(index):
                start = pl.multiple_of(index * count, count)
                high[pl.ds(start, count), :] = top
                low[pl.ds(start, count), :] = bottom

            put(band + R)

            @pl.when(band < R)
            def _():
                put(band + R + count)

            @pl.when(band >= count - R)
            def _():
                put(band + R - count)

            return carry

        lax.fori_loop(0, PER_SHIFT, shear, 0, unroll=4)
    scatter_band(1 - lax.axis_index("dir"), 0, table, high, low, out, sent)


def scatter_band(side, first_group, table, high, low, out, sent):
    bands = sent.shape[1]
    first = side * (high.shape[0] // 64 - 2 * R) // 8 + first_group
    scatter_groups(first, bands // 4, table, high, low, out, sent)
    for row in range(2):
        out[row, bands * 64 :, :] = sent[row].astype(jnp.int32).astype(jnp.int16)


def scatter_away_kernel(table, high, low, out, sent):
    scatter_band(1 - lax.axis_index("dir"), sent.shape[1] // 4, table, high, low, out, sent)


def scatter_own_kernel(table, high, low, out, sent):
    scatter_band(lax.axis_index("dir"), 0, table, high, low, out, sent)


def merge_kernel(*refs):
    local, across, out, scales, stage, store_sem = refs[:2], refs[2:6], *refs[6:]
    bands = scales.shape[1]
    size = bands * 64
    steps = store_sem.shape[0]
    width = size // steps
    block = lax.axis_index("pos")
    core = lax.rem(block, 2)
    held_here = lax.rem(lax.axis_index("dir") + lax.div(block, 2) + core, 2) == 0
    stores = [
        pltpu.make_async_copy(
            stage.at[pl.ds(step * width * 4, width * 4)],
            out.at[pl.ds(step * width * 4, width * 4)],
            store_sem.at[step],
        )
        for step in range(steps)
    ]
    for side in range(2):
        for here in range(2):
            used = ((local[0],), (local[1],)) if here else (across[:2], across[2:])
            share = bands // len(used[0])

            @pl.when((core == side) & (held_here == (here == 1)))
            def _():
                for slot in range(2):
                    for row in range(2):
                        for index, piece in enumerate(used[slot]):
                            scale = piece[row, share * 64 : share * 65, :].astype(jnp.int32)
                            span = slice(index * share, (index + 1) * share)
                            scales[slot * 2 + row, span, :] = scale.astype(jnp.float32)
                for step in range(steps):
                    for slot in range(2):
                        pair = side if slot == 0 else 1 - side
                        for row in range(2):
                            for band in range(step * width // 64, (step + 1) * width // 64):
                                begin = band % share * 64
                                rows = used[slot][band // share][row, begin : begin + 64, :]
                                value = decode(rows, scales[slot * 2 + row, band : band + 1, :])
                                stage[pl.ds(2 * pair + row + band * 256, 64, stride=4), :] = value
                    stores[step].start()

    for store in stores:
        store.wait()


def vmem(number):
    return [pl.BlockSpec(memory_space=VMEM)] * number


def grant(mebibytes):
    return pltpu.CompilerParams(vmem_limit_bytes=mebibytes << 20)


def in_vmem(value):
    return pltpu.with_memory_space_constraint(value, VMEM)


def smem(number):
    return [pl.BlockSpec(memory_space=SMEM)] * number


def fast_body(coherence, shift_first, fraction_first, shift_second, fraction_second, scatter_kernel):
    f32, bf16 = jnp.float32, jnp.bfloat16
    shape = jax.ShapeDtypeStruct
    pairs, places = lax.axis_size("dir"), lax.axis_size("pos")
    parts, own_first, own_second, _, lanes = coherence.shape
    bands = own_first * pairs
    total = pairs * places
    cut = pl.pallas_call(
        deal_kernel,
        out_shape=shape((total, own_second, parts, own_first * 2, lanes), bf16),
        in_specs=[pl.BlockSpec(memory_space=pltpu.HBM)],
        out_specs=pl.BlockSpec(memory_space=VMEM),
        scratch_shapes=[
            VMEM(coherence.shape, bf16),
            pltpu.SemaphoreType.DMA((parts * own_first // 8,)),
        ],
        compiler_params=grant(16),
        name="deal",
    )(pltpu.with_memory_space_constraint(coherence, pltpu.HBM))
    cut = in_vmem(cut)
    received = lax.all_to_all(
        cut, ("dir", "pos"), split_axis=0, concat_axis=0, tiled=True,
        axis_index_groups=[[device_of(line, places) for line in range(total)]],
    )

    row_one, row_two = shift_first.reshape(1, bands), shift_second.reshape(1, bands)
    halo_shapes = [shape((len(one) * PER_SHIFT * (bands + 1), lanes), jnp.int16) for one in HALOS]
    rest_shapes = [
        shape((4 * bands * bands, lanes), f32),
        shape((2 * bands, 4 * bands), bf16),
        shape((bands, lanes), f32),
        shape((bands, lanes), f32),
        shape((4, len(UP_NEAR) * PER_SHIFT, lanes), f32),
    ]
    part_shape = shape((bands // 2, 2, bands, lanes), f32)
    outer, *halos = pl.pallas_call(
        functools.partial(transform_kernel, pairs),
        out_shape=[part_shape] + halo_shapes + rest_shapes,
        in_specs=vmem(5) + [pl.BlockSpec(memory_space=pl.ANY)],
        out_specs=vmem(10),
        scratch_shapes=[
            VMEM((8 * bands, 4 * bands), bf16),
            VMEM(received.shape, bf16),
            pltpu.SemaphoreType.DMA((bands // 8,)),
        ],
        compiler_params=grant(12),
        name="transform",
    )(
        row_one, row_two, fraction_second.reshape(1, bands),
        jnp.asarray(first_tables(bands, pairs)), jnp.asarray(second_tables(bands)), received,
    )

    outer = in_vmem(outer)
    rest = [in_vmem(value) for value in halos[4:]]

    def send(halo, step):
        hops = [
            (device_of(b, places), device_of(b + step, places))
            for b in range(total)
            if 0 <= b + step < total
        ]
        return in_vmem(lax.ppermute(halo, ("dir", "pos"), hops))

    far_up = send(halos[1], 2)
    far_down = send(halos[3], -2)
    inner, near_up, near_down = pl.pallas_call(
        rest_kernel,
        out_shape=[part_shape, halo_shapes[0], halo_shapes[2]],
        in_specs=vmem(7),
        out_specs=vmem(3),
        scratch_shapes=[VMEM(rest_shapes[-1].shape, f32)],
        compiler_params=grant(8),
        name="rest",
    )(in_vmem(halos[0]), in_vmem(halos[2]), *rest)
    inner = in_vmem(inner)
    arrived = [send(near_up, 1), far_up, send(near_down, -1), far_down]

    table = pl.pallas_call(
        scatter_table_kernel,
        out_shape=shape((512, 1280), bf16),
        in_specs=vmem(2),
        out_specs=pl.BlockSpec(memory_space=VMEM),
        scratch_shapes=[VMEM((2, 32, 2 * bands), f32)],
        compiler_params=grant(8),
        name="scatter_table",
    )(row_two, scatter_kernel)

    table = in_vmem(table)
    wrapped = (bands + 2 * R) * bands
    half = bands * bands // 2
    codes = shape((2, half + bands // 2, lanes), jnp.int16)
    half_codes = shape((2, (half + bands // 2) // 2, lanes), jnp.int16)
    high, low, away_first = pl.pallas_call(
        shear_kernel,
        out_shape=[shape((wrapped, 2 * lanes), bf16)] * 2 + [half_codes],
        in_specs=smem(2) + vmem(7),
        out_specs=vmem(3),
        scratch_shapes=[
            SMEM((bands,), jnp.int32),
            SMEM((2 * H,), jnp.int32),
            VMEM((4, len(UP_NEAR) * PER_SHIFT, lanes), f32),
            VMEM((2, bands // 4, lanes), f32),
        ],
        compiler_params=grant(12),
        name="shear",
    )(shift_first, fraction_first, table, outer, inner, *arrived)
    high, low = in_vmem(high), in_vmem(low)
    home = [(d, q, c, (d + q) % 2) for d in range(pairs) for q in range(places // 2) for c in range(2)]
    same = [
        (d * places + 2 * q + c, (1 - d) * places + 2 * q + b) for d, q, c, b in home if b == c
    ]
    cross = [
        (d * places + 2 * q + c, (1 - d) * places + 2 * q + b) for d, q, c, b in home if b != c
    ]
    inside = [(d * places + 2 * q + c, d * places + 2 * q + b) for d, q, c, b in home if b != c]

    def scatter(kernel, out_shape, bands_held):
        return pl.pallas_call(
            kernel,
            out_shape=out_shape,
            in_specs=vmem(3),
            out_specs=pl.BlockSpec(memory_space=VMEM),
            scratch_shapes=[VMEM((2, bands_held, lanes), f32)],
            compiler_params=grant(8),
        )(table, high, low)

    from_same, from_cross = [], []
    away = away_first
    for part in range(2):
        from_same.append(lax.ppermute(away, ("dir", "pos"), same))
        from_cross.append(lax.ppermute(away, ("dir", "pos"), cross))
        if part == 0:
            away = scatter(scatter_away_kernel, half_codes, bands // 4)
    own = scatter(scatter_own_kernel, codes, bands // 2)
    from_inside = lax.ppermute(own, ("dir", "pos"), inside)
    pieces = [own] + [in_vmem(piece) for piece in (from_inside, *from_same, *from_cross)]
    merged = pl.pallas_call(
        merge_kernel,
        out_shape=shape((half * 4, lanes), f32),
        in_specs=vmem(6),
        out_specs=pl.BlockSpec(memory_space=pl.ANY),
        scratch_shapes=[
            VMEM((4, bands // 2, lanes), f32),
            VMEM((half * 4, lanes), f32),
            pltpu.SemaphoreType.DMA((8,)),
        ],
        compiler_params=grant(12),
        name="merge",
    )(*pieces)
    return merged.reshape(own_first, bands, 4, lanes)


def with_halo(cells, sides, width, closed):
    for axis, dim in sides:
        count = lax.axis_size(axis)
        ends = count if closed else count - 1
        head = lax.slice_in_dim(cells, 0, width, axis=dim)
        tail = lax.slice_in_dim(cells, cells.shape[dim] - width, cells.shape[dim], axis=dim)
        cells = jnp.concatenate(
            [
                lax.ppermute(tail, axis, [(i, (i + 1) % count) for i in range(ends)]),
                cells,
                lax.ppermute(head, axis, [((i + 1) % count, i) for i in range(ends)]),
            ],
            axis=dim,
        )
    return cells


def phase_tables(length):
    counter = jnp.arange(length, dtype=jnp.int32)
    product = counter[:, None] * counter[None, :] % length
    angles = product.astype(jnp.float32) * (2.0 * math.pi / length)
    factor = 1.0 / math.sqrt(length)
    return (jnp.cos(angles) * factor, jnp.sin(angles) * factor)


def contract(pattern, operand_a, operand_b):
    return jnp.einsum(
        pattern,
        operand_a,
        operand_b,
        precision=lax.Precision.HIGHEST,
        preferred_element_type=jnp.float32,
    )


def finish_bands(received):
    cos_one, sin_one = phase_tables(received.shape[1])
    real_part = contract("ts,sbax->tbax", cos_one, received[0]) + contract(
        "ts,sbax->tbax", sin_one, received[1]
    )
    return lax.all_to_all(real_part, "dir", split_axis=0, concat_axis=1, tiled=True)


def shear_block(wigner, shift_first, fraction_first):
    band_count = wigner.shape[0]
    cell_count = wigner.shape[2]
    first_band = lax.axis_index("dir") * band_count
    shifts = lax.dynamic_slice_in_dim(shift_first, first_band, band_count)
    weights = lax.dynamic_slice_in_dim(fraction_first, first_band, band_count)
    padded = with_halo(wigner, (("pos", 2),), H, False)
    rows_out = jnp.arange(cell_count, dtype=jnp.int32)
    rows_in = jnp.arange(cell_count + 2 * H, dtype=jnp.int32)
    target = rows_out[None, :, None] + H - shifts[:, None, None]
    near_tap = (rows_in[None, None, :] == target).astype(jnp.float32)
    far_tap = (rows_in[None, None, :] == target - 1).astype(jnp.float32)
    band_matrix = (1.0 - weights)[:, None, None] * near_tap + weights[:, None, None] * far_tap
    return contract("kaj,kbjx->kbax", band_matrix, padded)


def convolve(circulant, source, out_rows):
    summed = jnp.zeros((out_rows,) + source.shape[1:], jnp.float32)
    for offset in range(circulant.shape[0]):
        summed = summed + contract(
            "ij,kjax->kiax", circulant[offset], source[offset : offset + out_rows]
        )
    return summed


def body(coherence, shift_first, fraction_first, shift_second, fraction_second, scatter_kernel):
    direction_count = coherence.shape[2] * lax.axis_size("pos")
    cos_two, sin_two = phase_tables(direction_count)
    cell_block = lax.all_to_all(coherence, "pos", split_axis=3, concat_axis=2, tiled=True)
    real_in = cell_block[0].astype(jnp.float32)
    imag_in = cell_block[1].astype(jnp.float32)
    real_mid = contract("ts,bsax->btax", cos_two, real_in) + contract(
        "ts,bsax->btax", sin_two, imag_in
    )
    imag_mid = contract("ts,bsax->btax", cos_two, imag_in) - contract(
        "ts,bsax->btax", sin_two, real_in
    )
    mixed = jnp.stack([real_mid, imag_mid])
    wigner = finish_bands(lax.all_to_all(mixed, "dir", split_axis=2, concat_axis=1, tiled=True))
    moved_one = shear_block(wigner, shift_first, fraction_first)
    band_count = moved_one.shape[0]
    column_count = moved_one.shape[3]
    positions = jnp.arange(column_count, dtype=jnp.int32)
    target_two = positions[None, :, None] - shift_second[:, None, None]
    near_two = (positions[None, None, :] == target_two).astype(jnp.float32)
    far_two = (positions[None, None, :] == target_two - 1).astype(jnp.float32)
    shear_matrix = (1.0 - fraction_second)[:, None, None] * near_two + fraction_second[
        :, None, None
    ] * far_two
    moved_two = contract("bxy,kbay->kbax", shear_matrix, moved_one)
    kernel_positions = jnp.arange(direction_count, dtype=jnp.int32)
    lag_index = (kernel_positions[:, None] - kernel_positions[None, :]) % direction_count
    circulant = scatter_kernel[:, lag_index]
    extended = with_halo(moved_two, (("dir", 0),), R, True)
    summed = moved_two + convolve(circulant, extended, band_count)
    return summed


def fits(mesh, coherence):
    pairs, places = mesh.shape["dir"], mesh.shape["pos"]
    _, first, second, cells, lanes = coherence.shape
    return 4 * places == second and (pairs, first, second, cells, lanes) == (2, 64, 64, 4 * places, 128)


def solution(mesh):
    placed = (P(None, "dir", "pos", None, None), P(), P(), P(), P(), P())

    def run(*arrays):
        fast = fits(mesh, arrays[0])
        step = jax.shard_map(
            fast_body if fast else body,
            mesh=mesh, in_specs=placed, out_specs=P("dir", None, "pos", None), check_vma=False,
        )
        return step(*arrays)

    return run
```

```python
import functools
import math

import jax
import jax.numpy as jnp
import numpy as np
from jax import lax
from jax.experimental import pallas as pl
from jax.experimental.pallas import tpu as pltpu
from jax.sharding import PartitionSpec as P

R = 8
H = 4
H2 = 16

UP_NEAR = ((4, 1), (5, 0), (5, 1), (6, 0), (6, 1), (7, 0))
UP_FAR = ((6, 1), (7, 0), (7, 1))
DOWN_NEAR = ((3, 0), (2, 0), (2, 1), (1, 0), (1, 1), (0, 1))
DOWN_FAR = ((1, 0), (0, 0), (0, 1))
HALOS = (UP_NEAR, UP_FAR, DOWN_NEAR, DOWN_FAR)
PER_SHIFT = 8
OUTER, INNER = (0, 1, 6, 7), (2, 3, 4, 5)
TOP = 32600.0
FINE = 8.0
LEAST = 1e-30
VMEM = pltpu.VMEM
SMEM = pltpu.SMEM


def split_np(table):
    high = table.astype(jnp.bfloat16)
    low = (table - high.astype(np.float32)).astype(jnp.bfloat16)
    return high, low


def split(value):
    high = value.astype(jnp.bfloat16)
    low = (value - high.astype(jnp.float32)).astype(jnp.bfloat16)
    return high, low


def natural_tables(length):
    counter = np.arange(length)
    angles = (counter[:, None] * counter[None, :] % length) * (2.0 * math.pi / length)
    factor = 1.0 / math.sqrt(length)
    return np.cos(angles) * factor, np.sin(angles) * factor


def first_tables(length, cuts):
    cos, sin = natural_tables(length)
    width = length // cuts
    real, imag = [], []
    for cut in range(cuts):
        cols = slice(cut * width, (cut + 1) * width)
        real += [cos[:, cols], sin[:, cols]]
        imag += [-sin[:, cols], cos[:, cols]]
    table = np.repeat(np.concatenate(real + imag, axis=1), 2, axis=1).astype(np.float32)
    return np.concatenate(split_np(table), axis=1)


def second_tables(length):
    cos, sin = natural_tables(length)
    table = np.concatenate([cos, sin], axis=1).astype(np.float32)
    return np.concatenate(split_np(table), axis=1)


def slot_onehot(shift_row, low, stride_shift, stride_repeat, copies=1):
    count = shift_row.shape[1]
    across = jnp.broadcast_to(shift_row, (count, count))
    down = across.astype(jnp.float32).T.astype(jnp.int32)
    first = lax.broadcasted_iota(jnp.int32, (count, count), 0)
    second = lax.broadcasted_iota(jnp.int32, (count, count), 1)
    same = jnp.where((across == down) & (first < second), 1, 0)
    repeat = jnp.sum(same, axis=0, keepdims=True)
    slot = (shift_row - low) * stride_shift + repeat * stride_repeat
    if copies == 2:
        first = lax.broadcasted_iota(jnp.int32, (2 * count, count), 0)
        first = lax.shift_right_logical(first, 1)
    return first == slot


def dot(lhs, rhs):
    return jnp.dot(lhs, rhs, preferred_element_type=jnp.float32)


def place_in_line(pair, block):
    return block // 2 * 4 + (pair + block // 2) % 2 * 2 + block % 2


def device_of(line, places):
    quad, step = line // 4, line % 4
    return (step // 2 + quad) % 2 * places + quad * 2 + step % 2


def deal_kernel(source, out, held, sem):
    taken = lax.broadcasted_iota(jnp.int32, (128, 128), 1)
    given = lax.broadcasted_iota(jnp.int32, (128, 128), 0)
    wanted = lax.rem(lax.div(given, 2), 8) * 16 + lax.div(given, 16) * 2 + lax.rem(given, 2)
    move = jnp.where(taken == wanted, 1.0, 0.0).astype(jnp.bfloat16)
    parts, firsts, seconds, cells, _ = source.shape

    def load(part, group):
        span = pl.ds(group * 8, 8)
        number = part * (firsts // 8) + group
        return pltpu.make_async_copy(source.at[part, span], held.at[part, span], sem.at[number])

    groups = [(part, group) for part in range(parts) for group in range(firsts // 8)]
    for part, group in groups:
        load(part, group).start()
    for part, group in groups:
        load(part, group).wait()

        def second(own, carry):
            for tile in range(0, cells // 16, 2):
                columns = [
                    jnp.concatenate(
                        [
                            held[part, group * 8 + item, own, member * 16 : member * 16 + 16, :]
                            for item in range(8)
                        ],
                        axis=0,
                    )
                    for member in (tile, tile + 1)
                ]
                moved = dot(move, jnp.concatenate(columns, axis=1)).astype(jnp.bfloat16)
                for member in range(2):
                    for item in range(8):
                        out[(tile + member) * 8 + item, own, part, group * 16 : group * 16 + 16, :] = (
                            moved[item * 16 : item * 16 + 16, member * 128 : member * 128 + 128]
                        )
            return carry

        lax.fori_loop(0, seconds, second, 0, unroll=4)


def encode(columns):
    largest = jnp.maximum(jnp.max(jnp.abs(columns), axis=0, keepdims=True), LEAST)
    scale = jnp.ceil(jnp.log2(largest) * FINE)
    codes = jnp.round(columns * (jnp.exp2(scale * (-1.0 / FINE)) * TOP))
    return codes.astype(jnp.int32).astype(jnp.int16), scale


def decode(codes, scale):
    return codes.astype(jnp.int32).astype(jnp.float32) * (jnp.exp2(scale * (1.0 / FINE)) * (1.0 / TOP))


def transform_kernel(
    pairs, shift_one, shift_two, fraction_two, table_one, table_two, source,
    out, up_near, up_far, down_near, down_far, middle, left_two, weight_near, weight_far, scales,
    left_one, received, load_sem,
):
    count = 64
    lanes = out.shape[-1]
    local = received.shape[1]
    lines = received.shape[0] // (count // 8)
    loads = [
        pltpu.make_async_copy(
            source.at[pl.ds(block * lines, lines)],
            received.at[pl.ds(block * lines, lines)],
            load_sem.at[block],
        )
        for block in range(count // 8)
    ]
    for load in loads:
        load.start()
    onehot_one = jnp.where(slot_onehot(shift_one[...], -H, PER_SHIFT, 1, copies=2), 1.0, 0.0)
    picked = dot(onehot_one.astype(jnp.bfloat16), table_one[...])
    same_row = lax.rem(
        lax.broadcasted_iota(jnp.int32, picked.shape, 0)
        + lax.broadcasted_iota(jnp.int32, picked.shape, 1),
        2,
    )
    picked = jnp.where(same_row == 0, picked, 0.0).astype(jnp.bfloat16)
    for part in range(4):
        left_one[part * 2 * count : (part + 1) * 2 * count, :] = picked[
            :, part * 4 * count : (part + 1) * 4 * count
        ]
    hot_two = slot_onehot(shift_two[...], -H2, 1, 2 * H2)
    onehot_two = jnp.where(hot_two, 1.0, 0.0)
    picked = dot(onehot_two.astype(jnp.bfloat16), table_two[...]).astype(jnp.bfloat16)
    left_two[:count, :128] = picked[:, :128]
    left_two[:count, 128:] = picked[:, :128]
    left_two[count:, :128] = picked[:, 128:]
    left_two[count:, 128:] = jnp.zeros((count, 128), jnp.bfloat16)
    part_two = jnp.sum(
        jnp.where(hot_two, jnp.broadcast_to(fraction_two[...], hot_two.shape), 0.0),
        axis=1, keepdims=True,
    )
    rows = lax.broadcasted_iota(jnp.int32, (count, lanes), 0)
    origin = lax.broadcasted_iota(jnp.int32, (count, lanes), 1) - (lax.rem(rows, 2 * H2) - H2)
    weight_near[...] = jnp.where((origin >= 0) & (origin < lanes), 1.0 - part_two, 0.0)
    weight_far[...] = jnp.where((origin >= 1) & (origin <= lanes), part_two, 0.0)

    chunk = 2 * count * 2 * 8

    def first(block, carry):
        pltpu.make_async_copy(
            source.at[pl.ds(block * lines, lines)],
            received.at[pl.ds(block * lines, lines)],
            load_sem.at[block],
        ).wait()
        for index in range(0, 8, 2):
            columns = []
            for member in (index, index + 1):
                group, own = block * (8 // local) + member // local, member % local
                blocks = [
                    received[place_in_line(pair, group), own, part]
                    for pair in range(pairs)
                    for part in range(2)
                ]
                columns.append(jnp.concatenate(blocks, axis=0))
            both = dot(left_one[...], jnp.concatenate(columns, axis=1))
            both = both[: 4 * count] + both[4 * count :]
            for member in range(2):
                start = pl.multiple_of(block * chunk, chunk) + index + member
                middle[pl.ds(start, 4 * count, stride=8), :] = both[
                    :, member * lanes : (member + 1) * lanes
                ]
        return carry

    lax.fori_loop(0, count // 8, first, 0, unroll=2)

    targets = (up_near, up_far, down_near, down_far)
    finish_directions(OUTER, middle, left_two, weight_near, weight_far, out, targets, scales)
    code_halo_scales(1, up_far, scales)
    code_halo_scales(3, down_far, scales)


def rest_kernel(
    up_near_in, down_near_in, middle, left_two, weight_near, weight_far, scales_in,
    out, up_near, down_near, scales,
):
    scales[...] = scales_in[...]
    up_near[...] = up_near_in[...]
    down_near[...] = down_near_in[...]
    targets = (up_near, None, down_near, None)
    finish_directions(INNER, middle, left_two, weight_near, weight_far, out, targets, scales)
    code_halo_scales(0, up_near, scales)
    code_halo_scales(2, down_near, scales)


def code_halo_scales(kind, target, scales):
    entries = target.shape[0] // 65
    target[entries * 64 :, :] = scales[kind, :entries, :].astype(jnp.int32).astype(jnp.int16)


def finish_directions(values, middle, left_two, weight_near, weight_far, out, targets, scales):
    count = 64
    lanes = out.shape[-1]
    chunk = 2 * count * 2 * 8
    for position, value in enumerate(values):

        def second(item, carry):
            slot = value * PER_SHIFT + item
            columns = []
            for row in range(2):
                parts = [
                    middle[
                        pl.ds(
                            pl.multiple_of(block * chunk + ((part * count + slot) * 2 + row) * 8, 8), 8
                        ),
                        :,
                    ]
                    for part in range(2)
                    for block in range(count // 8)
                ]
                columns.append(jnp.concatenate(parts, axis=0))
            both = dot(
                left_two[...],
                jnp.concatenate(split(jnp.concatenate(columns, axis=1)), axis=0),
            )
            both = both[:count] + both[count:]
            for row in range(2):
                pieces = []
                for block in range(count // 8):
                    piece = both[block * 8 : block * 8 + 8, row * lanes : (row + 1) * lanes]
                    base = (lanes - H2 + 8 * (block % (2 * H2 // 8))) % lanes
                    near = pltpu.roll(piece, base, 1, stride=1, stride_axis=0)
                    far = pltpu.roll(near, 1, 1)
                    span = slice(block * 8, block * 8 + 8)
                    pieces.append(near * weight_near[span, :] + far * weight_far[span, :])
                moved = jnp.concatenate(pieces, axis=0)
                out[position * PER_SHIFT + item, row] = moved
                hits = [
                    (kind, wanted.index((value, row)))
                    for kind, wanted in enumerate(HALOS)
                    if (value, row) in wanted
                ]
                if hits:
                    codes, scale = encode(moved)
                for kind, index in hits:
                    place = index * PER_SHIFT + item
                    start = pl.multiple_of(place * count, count)
                    targets[kind][pl.ds(start, count), :] = codes
                    scales[kind, pl.ds(place, 1), :] = scale
            return carry

        lax.fori_loop(0, PER_SHIFT, second, 0, unroll=8)


def scatter_table_kernel(shift_two, kernel, table, rows):
    count = kernel.shape[1]
    reach = kernel.shape[0]
    offsets = lax.broadcasted_iota(jnp.int32, kernel.shape, 0)
    lags = lax.broadcasted_iota(jnp.int32, kernel.shape, 1)
    full = kernel[...] + jnp.where((offsets == R) & (lags == 0), 1.0, 0.0)
    high, low = split(full)
    lag = lax.broadcasted_iota(jnp.int32, (count, 2 * count), 0)
    lane = lax.broadcasted_iota(jnp.int32, (count, 2 * count), 1)
    mirror = jnp.where(lax.rem(lag + lane, count) == 0, 1.0, 0.0).astype(jnp.bfloat16)
    rows[...] = jnp.zeros(rows.shape, jnp.float32)
    rows[0, 3 : 3 + reach, :] = dot(high, mirror)
    rows[1, 3 : 3 + reach, :] = dot(low, mirror)
    onehot = jnp.where(slot_onehot(shift_two[...], -H2, 1, 2 * H2), 1.0, 0.0).T
    blank = jnp.zeros((count, count), jnp.float32)
    choose = jnp.concatenate(
        [jnp.concatenate([onehot, blank], axis=1), jnp.concatenate([blank, onehot], axis=1)], axis=0
    ).astype(jnp.bfloat16)
    left = lane < count

    def circulant(part, index):
        row = jnp.broadcast_to(rows[part, index : index + 1, :], (8, 2 * count))
        return jnp.concatenate(
            [pltpu.roll(row, 8 * block, 1, stride=1, stride_axis=0) for block in range(count // 8)],
            axis=0,
        )

    for part in range(2):
        here = circulant(part, 0)
        for index in range(reach + 5):
            there = circulant(part, index + 1)
            pair = dot(jnp.where(left, here, there).astype(jnp.bfloat16), choose)
            pair = pair.astype(jnp.bfloat16)
            here = there
            for band in range(4):
                if (index - 3 + band) % 2 == 0 and 0 <= (index - 3 + band) // 2 < 10:
                    column = (index - 3 + band) // 2 * 128
                    start = part * 256 + band * count
                    table[start : start + count, column : column + 128] = pair


def scatter_pair(index, first_group, table, high, low, out, scales):
    start = pl.multiple_of((first_group + index * 2) * 256, 256)

    def window(half):
        return jnp.concatenate(
            [half[pl.ds(start, 1280), :], half[pl.ds(start + 256, 1280), :]], axis=1
        )

    both = dot(table[...], window(high))
    rest = dot(table[:256, :], window(low))
    total = both[:256] + both[256:] + rest
    for member in range(2):
        target = pl.multiple_of((index * 2 + member) * 256, 256)
        for row in range(2):
            column = member * 256 + row * 128
            part = total[:, column : column + 128]
            blocks = [encode(part[band * 64 : band * 64 + 64]) for band in range(4)]
            out[row, pl.ds(target, 256), :] = jnp.concatenate(
                [codes for codes, _ in blocks], axis=0
            )
            for band in range(4):
                scales[row, pl.ds((index * 2 + member) * 4 + band, 1), :] = blocks[band][1]


def scatter_groups(first_group, groups, table, high, low, out, scales):
    def step(index, carry):
        scatter_pair(index, first_group, table, high, low, out, scales)
        return carry

    lax.fori_loop(0, groups // 2, step, 0, unroll=groups // 2)


def shear_kernel(
    shift_one, fraction_one, table, outer, inner, up_near, up_far, down_near, down_far,
    high, low, out, order, seen, arrived, sent,
):
    count = outer.shape[2]
    for value in range(2 * H):
        seen[value] = 0

    def place(band, carry):
        value = shift_one[band] + H
        repeat = seen[value]
        order[value * PER_SHIFT + repeat] = band
        seen[value] = repeat + 1
        return carry

    lax.fori_loop(0, count, place, 0)
    sources = (up_near, up_far, down_near, down_far)
    for kind, source in enumerate(sources):
        entries = source.shape[0] // (count + 1)
        codes = source[entries * count :, :].astype(jnp.int32)
        arrived[kind, :entries, :] = codes.astype(jnp.float32)

    def fetch(value, item, row):
        if row in (0, 1):
            held, values = (outer, OUTER) if value in OUTER else (inner, INNER)
            return held[values.index(value) * PER_SHIFT + item, row]
        if row < 0:
            kind, key = (0, (value, row + 2)) if row >= -2 else (1, (value, row + 4))
        else:
            kind, key = (2, (value, row - 2)) if row <= 3 else (3, (value, row - 4))
        place = HALOS[kind].index(key) * PER_SHIFT + item
        start = pl.multiple_of(place * count, count)
        return decode(sources[kind][pl.ds(start, count), :], arrived[kind, pl.ds(place, 1), :])

    for value in range(2 * H):
        shift = value - H

        def shear(item, carry):
            band = order[value * PER_SHIFT + item]
            weight = fraction_one[band]
            need = {
                row: fetch(value, item, row)
                for row in (-shift - 1, -shift, 1 - shift)
            }
            full = jnp.concatenate(
                [
                    (1.0 - weight) * need[row - shift] + weight * need[row - shift - 1]
                    for row in range(2)
                ],
                axis=1,
            )
            top, bottom = split(full)

            def put(index):
                start = pl.multiple_of(index * count, count)
                high[pl.ds(start, count), :] = top
                low[pl.ds(start, count), :] = bottom

            put(band + R)

            @pl.when(band < R)
            def _():
                put(band + R + count)

            @pl.when(band >= count - R)
            def _():
                put(band + R - count)

            return carry

        lax.fori_loop(0, PER_SHIFT, shear, 0, unroll=4)
    scatter_band(1 - lax.axis_index("dir"), 0, table, high, low, out, sent)


def scatter_band(side, first_group, table, high, low, out, sent):
    bands = sent.shape[1]
    first = side * (high.shape[0] // 64 - 2 * R) // 8 + first_group
    scatter_groups(first, bands // 4, table, high, low, out, sent)
    for row in range(2):
        out[row, bands * 64 :, :] = sent[row].astype(jnp.int32).astype(jnp.int16)


def scatter_away_kernel(table, high, low, out, sent):
    whole = (high.shape[0] // 64 - 2 * R) // 2
    scatter_band(1 - lax.axis_index("dir"), (whole - sent.shape[1]) // 4, table, high, low, out, sent)


def scatter_own_kernel(table, high, low, out, sent):
    scatter_band(lax.axis_index("dir"), 0, table, high, low, out, sent)


def merge_kernel(*refs):
    local, across, out, scales, stage, store_sem = refs[:2], refs[2:6], *refs[6:]
    bands = scales.shape[1]
    size = bands * 64
    steps = store_sem.shape[0]
    width = size // steps
    block = lax.axis_index("pos")
    core = lax.rem(block, 2)
    held_here = lax.rem(lax.axis_index("dir") + lax.div(block, 2) + core, 2) == 0
    stores = [
        pltpu.make_async_copy(
            stage.at[pl.ds(step * width * 4, width * 4)],
            out.at[pl.ds(step * width * 4, width * 4)],
            store_sem.at[step],
        )
        for step in range(steps)
    ]
    for side in range(2):
        for here in range(2):
            used = ((local[0],), (local[1],)) if here else (across[:2], across[2:])
            shares = [piece.shape[1] // 65 for piece in used[0]]
            place = [(index, band) for index, held in enumerate(shares) for band in range(held)]

            @pl.when((core == side) & (held_here == (here == 1)))
            def _():
                for slot in range(2):
                    for row in range(2):
                        for index, piece in enumerate(used[slot]):
                            held, begin = shares[index], sum(shares[:index])
                            scale = piece[row, held * 64 : held * 65, :].astype(jnp.int32)
                            span = slice(begin, begin + held)
                            scales[slot * 2 + row, span, :] = scale.astype(jnp.float32)
                for step in range(steps):
                    for slot in range(2):
                        pair = side if slot == 0 else 1 - side
                        for row in range(2):
                            for band in range(step * width // 64, (step + 1) * width // 64):
                                index, begin = place[band][0], place[band][1] * 64
                                rows = used[slot][index][row, begin : begin + 64, :]
                                value = decode(rows, scales[slot * 2 + row, band : band + 1, :])
                                stage[pl.ds(2 * pair + row + band * 256, 64, stride=4), :] = value
                    stores[step].start()

    for store in stores:
        store.wait()


def vmem(number):
    return [pl.BlockSpec(memory_space=VMEM)] * number


def grant(mebibytes):
    return pltpu.CompilerParams(vmem_limit_bytes=mebibytes << 20)


def in_vmem(value):
    return pltpu.with_memory_space_constraint(value, VMEM)


def smem(number):
    return [pl.BlockSpec(memory_space=SMEM)] * number


def fast_body(coherence, shift_first, fraction_first, shift_second, fraction_second, scatter_kernel):
    f32, bf16 = jnp.float32, jnp.bfloat16
    shape = jax.ShapeDtypeStruct
    pairs, places = lax.axis_size("dir"), lax.axis_size("pos")
    parts, own_first, own_second, _, lanes = coherence.shape
    bands = own_first * pairs
    total = pairs * places
    cut = pl.pallas_call(
        deal_kernel,
        out_shape=shape((total, own_second, parts, own_first * 2, lanes), bf16),
        in_specs=[pl.BlockSpec(memory_space=pltpu.HBM)],
        out_specs=pl.BlockSpec(memory_space=VMEM),
        scratch_shapes=[
            VMEM(coherence.shape, bf16),
            pltpu.SemaphoreType.DMA((parts * own_first // 8,)),
        ],
        compiler_params=grant(16),
        name="deal",
    )(pltpu.with_memory_space_constraint(coherence, pltpu.HBM))
    cut = in_vmem(cut)
    received = lax.all_to_all(
        cut, ("dir", "pos"), split_axis=0, concat_axis=0, tiled=True,
        axis_index_groups=[[device_of(line, places) for line in range(total)]],
    )

    row_one, row_two = shift_first.reshape(1, bands), shift_second.reshape(1, bands)
    halo_shapes = [shape((len(one) * PER_SHIFT * (bands + 1), lanes), jnp.int16) for one in HALOS]
    rest_shapes = [
        shape((4 * bands * bands, lanes), f32),
        shape((2 * bands, 4 * bands), bf16),
        shape((bands, lanes), f32),
        shape((bands, lanes), f32),
        shape((4, len(UP_NEAR) * PER_SHIFT, lanes), f32),
    ]
    part_shape = shape((bands // 2, 2, bands, lanes), f32)
    outer, *halos = pl.pallas_call(
        functools.partial(transform_kernel, pairs),
        out_shape=[part_shape] + halo_shapes + rest_shapes,
        in_specs=vmem(5) + [pl.BlockSpec(memory_space=pl.ANY)],
        out_specs=vmem(10),
        scratch_shapes=[
            VMEM((8 * bands, 4 * bands), bf16),
            VMEM(received.shape, bf16),
            pltpu.SemaphoreType.DMA((bands // 8,)),
        ],
        compiler_params=grant(12),
        name="transform",
    )(
        row_one, row_two, fraction_second.reshape(1, bands),
        jnp.asarray(first_tables(bands, pairs)), jnp.asarray(second_tables(bands)), received,
    )

    outer = in_vmem(outer)
    rest = [in_vmem(value) for value in halos[4:]]

    def send(halo, step):
        hops = [
            (device_of(b, places), device_of(b + step, places))
            for b in range(total)
            if 0 <= b + step < total
        ]
        return in_vmem(lax.ppermute(halo, ("dir", "pos"), hops))

    far_up = send(halos[1], 2)
    far_down = send(halos[3], -2)
    inner, near_up, near_down = pl.pallas_call(
        rest_kernel,
        out_shape=[part_shape, halo_shapes[0], halo_shapes[2]],
        in_specs=vmem(7),
        out_specs=vmem(3),
        scratch_shapes=[VMEM(rest_shapes[-1].shape, f32)],
        compiler_params=grant(8),
        name="rest",
    )(in_vmem(halos[0]), in_vmem(halos[2]), *rest)
    inner = in_vmem(inner)
    arrived = [send(near_up, 1), far_up, send(near_down, -1), far_down]

    table = pl.pallas_call(
        scatter_table_kernel,
        out_shape=shape((512, 1280), bf16),
        in_specs=vmem(2),
        out_specs=pl.BlockSpec(memory_space=VMEM),
        scratch_shapes=[VMEM((2, 32, 2 * bands), f32)],
        compiler_params=grant(8),
        name="scatter_table",
    )(row_two, scatter_kernel)

    table = in_vmem(table)
    wrapped = (bands + 2 * R) * bands
    half = bands * bands // 2
    codes = shape((2, half + bands // 2, lanes), jnp.int16)
    early = bands // 8
    early_codes = shape((2, early * (bands + 1), lanes), jnp.int16)
    late_codes = shape((2, (bands // 2 - early) * (bands + 1), lanes), jnp.int16)
    high, low, away_first = pl.pallas_call(
        shear_kernel,
        out_shape=[shape((wrapped, 2 * lanes), bf16)] * 2 + [early_codes],
        in_specs=smem(2) + vmem(7),
        out_specs=vmem(3),
        scratch_shapes=[
            SMEM((bands,), jnp.int32),
            SMEM((2 * H,), jnp.int32),
            VMEM((4, len(UP_NEAR) * PER_SHIFT, lanes), f32),
            VMEM((2, early, lanes), f32),
        ],
        compiler_params=grant(12),
        name="shear",
    )(shift_first, fraction_first, table, outer, inner, *arrived)
    high, low = in_vmem(high), in_vmem(low)
    home = [(d, q, c, (d + q) % 2) for d in range(pairs) for q in range(places // 2) for c in range(2)]
    same = [
        (d * places + 2 * q + c, (1 - d) * places + 2 * q + b) for d, q, c, b in home if b == c
    ]
    cross = [
        (d * places + 2 * q + c, (1 - d) * places + 2 * q + b) for d, q, c, b in home if b != c
    ]
    inside = [(d * places + 2 * q + c, d * places + 2 * q + b) for d, q, c, b in home if b != c]

    def scatter(kernel, out_shape, bands_held):
        return pl.pallas_call(
            kernel,
            out_shape=out_shape,
            in_specs=vmem(3),
            out_specs=pl.BlockSpec(memory_space=VMEM),
            scratch_shapes=[VMEM((2, bands_held, lanes), f32)],
            compiler_params=grant(8),
        )(table, high, low)

    from_same, from_cross = [], []
    away = away_first
    for part in range(2):
        from_same.append(lax.ppermute(away, ("dir", "pos"), same))
        from_cross.append(lax.ppermute(away, ("dir", "pos"), cross))
        if part == 0:
            away = scatter(scatter_away_kernel, late_codes, bands // 2 - early)
    own = scatter(scatter_own_kernel, codes, bands // 2)
    from_inside = lax.ppermute(own, ("dir", "pos"), inside)
    pieces = [own] + [in_vmem(piece) for piece in (from_inside, *from_same, *from_cross)]
    merged = pl.pallas_call(
        merge_kernel,
        out_shape=shape((half * 4, lanes), f32),
        in_specs=vmem(6),
        out_specs=pl.BlockSpec(memory_space=pl.ANY),
        scratch_shapes=[
            VMEM((4, bands // 2, lanes), f32),
            VMEM((half * 4, lanes), f32),
            pltpu.SemaphoreType.DMA((8,)),
        ],
        compiler_params=grant(12),
        name="merge",
    )(*pieces)
    return merged.reshape(own_first, bands, 4, lanes)


def with_halo(cells, sides, width, closed):
    for axis, dim in sides:
        count = lax.axis_size(axis)
        ends = count if closed else count - 1
        head = lax.slice_in_dim(cells, 0, width, axis=dim)
        tail = lax.slice_in_dim(cells, cells.shape[dim] - width, cells.shape[dim], axis=dim)
        cells = jnp.concatenate(
            [
                lax.ppermute(tail, axis, [(i, (i + 1) % count) for i in range(ends)]),
                cells,
                lax.ppermute(head, axis, [((i + 1) % count, i) for i in range(ends)]),
            ],
            axis=dim,
        )
    return cells


def phase_tables(length):
    counter = jnp.arange(length, dtype=jnp.int32)
    product = counter[:, None] * counter[None, :] % length
    angles = product.astype(jnp.float32) * (2.0 * math.pi / length)
    factor = 1.0 / math.sqrt(length)
    return (jnp.cos(angles) * factor, jnp.sin(angles) * factor)


def contract(pattern, operand_a, operand_b):
    return jnp.einsum(
        pattern,
        operand_a,
        operand_b,
        precision=lax.Precision.HIGHEST,
        preferred_element_type=jnp.float32,
    )


def finish_bands(received):
    cos_one, sin_one = phase_tables(received.shape[1])
    real_part = contract("ts,sbax->tbax", cos_one, received[0]) + contract(
        "ts,sbax->tbax", sin_one, received[1]
    )
    return lax.all_to_all(real_part, "dir", split_axis=0, concat_axis=1, tiled=True)


def shear_block(wigner, shift_first, fraction_first):
    band_count = wigner.shape[0]
    cell_count = wigner.shape[2]
    first_band = lax.axis_index("dir") * band_count
    shifts = lax.dynamic_slice_in_dim(shift_first, first_band, band_count)
    weights = lax.dynamic_slice_in_dim(fraction_first, first_band, band_count)
    padded = with_halo(wigner, (("pos", 2),), H, False)
    rows_out = jnp.arange(cell_count, dtype=jnp.int32)
    rows_in = jnp.arange(cell_count + 2 * H, dtype=jnp.int32)
    target = rows_out[None, :, None] + H - shifts[:, None, None]
    near_tap = (rows_in[None, None, :] == target).astype(jnp.float32)
    far_tap = (rows_in[None, None, :] == target - 1).astype(jnp.float32)
    band_matrix = (1.0 - weights)[:, None, None] * near_tap + weights[:, None, None] * far_tap
    return contract("kaj,kbjx->kbax", band_matrix, padded)


def convolve(circulant, source, out_rows):
    summed = jnp.zeros((out_rows,) + source.shape[1:], jnp.float32)
    for offset in range(circulant.shape[0]):
        summed = summed + contract(
            "ij,kjax->kiax", circulant[offset], source[offset : offset + out_rows]
        )
    return summed


def body(coherence, shift_first, fraction_first, shift_second, fraction_second, scatter_kernel):
    direction_count = coherence.shape[2] * lax.axis_size("pos")
    cos_two, sin_two = phase_tables(direction_count)
    cell_block = lax.all_to_all(coherence, "pos", split_axis=3, concat_axis=2, tiled=True)
    real_in = cell_block[0].astype(jnp.float32)
    imag_in = cell_block[1].astype(jnp.float32)
    real_mid = contract("ts,bsax->btax", cos_two, real_in) + contract(
        "ts,bsax->btax", sin_two, imag_in
    )
    imag_mid = contract("ts,bsax->btax", cos_two, imag_in) - contract(
        "ts,bsax->btax", sin_two, real_in
    )
    mixed = jnp.stack([real_mid, imag_mid])
    wigner = finish_bands(lax.all_to_all(mixed, "dir", split_axis=2, concat_axis=1, tiled=True))
    moved_one = shear_block(wigner, shift_first, fraction_first)
    band_count = moved_one.shape[0]
    column_count = moved_one.shape[3]
    positions = jnp.arange(column_count, dtype=jnp.int32)
    target_two = positions[None, :, None] - shift_second[:, None, None]
    near_two = (positions[None, None, :] == target_two).astype(jnp.float32)
    far_two = (positions[None, None, :] == target_two - 1).astype(jnp.float32)
    shear_matrix = (1.0 - fraction_second)[:, None, None] * near_two + fraction_second[
        :, None, None
    ] * far_two
    moved_two = contract("bxy,kbay->kbax", shear_matrix, moved_one)
    kernel_positions = jnp.arange(direction_count, dtype=jnp.int32)
    lag_index = (kernel_positions[:, None] - kernel_positions[None, :]) % direction_count
    circulant = scatter_kernel[:, lag_index]
    extended = with_halo(moved_two, (("dir", 0),), R, True)
    summed = moved_two + convolve(circulant, extended, band_count)
    return summed


def fits(mesh, coherence):
    pairs, places = mesh.shape["dir"], mesh.shape["pos"]
    _, first, second, cells, lanes = coherence.shape
    return 4 * places == second and (pairs, first, second, cells, lanes) == (2, 64, 64, 4 * places, 128)


def solution(mesh):
    placed = (P(None, "dir", "pos", None, None), P(), P(), P(), P(), P())

    def run(*arrays):
        fast = fits(mesh, arrays[0])
        step = jax.shard_map(
            fast_body if fast else body,
            mesh=mesh, in_specs=placed, out_specs=P("dir", None, "pos", None), check_vma=False,
        )
        return step(*arrays)

    return run
```
